256 devices in a mesh: contacts: 32 (over y, z), tm: 8 (over x, core).
Axes of the slice: x: 4, y: 4, z: 8, core: 2. Of those that a mesh axis runs over, the one named last changes fastest.
Arguments:
- signal: bfloat16 [8192, 1024], P('contacts', 'tm'), may hold values from -6 to 6
- pos_idx: int32 [8192], P('contacts'), may hold values from 0 to 4095
- live_count: int32 [32], P('contacts'), may hold values from 128 to 256, as said below
- latents: bfloat16 [256, 512], replicated, may hold values from -400 to 400
- pos_table: bfloat16 [4096, 512], replicated, may hold values from -6 to 6
- w_in: bfloat16 [32, 512], replicated, may hold values from -1 to 1
- w_kv: bfloat16 [512, 1024], replicated, may hold values from -0.25 to 0.25
- w_query: bfloat16 [512, 512], replicated, may hold values from -0.25 to 0.25
- w_out: bfloat16 [512, 512], replicated, may hold values from -0.25 to 0.25
- conv_weight: bfloat16 [2, 3, 512, 512], replicated, may hold values from -0.15625 to 0.15625
- conv_bias: float32 [2, 512], replicated, may hold values from -3 to 3
- cotangent: bfloat16 [32, 256, 512], P('tm', 'contacts'), may hold values from -6 to 6
Outputs:
- features: bfloat16 [32, 256, 512], P('tm', 'contacts')
- d_latents: float32 [256, 512], replicated
The draws below stay inside these ranges and needn't reach their ends.
Inputs may be any that keep to these rules, and one draw needn't show every extreme that they name: The first live_count[b] contacts of block b are valid; some block is full and some block has exactly 128 valid contacts.
All inputs are finite; a program needn't handle non-finite values.
Results may differ from the reference program's by a relative error of at most 0.018.
The reference program's roundings to bfloat16 on the way count: a program that leaves them out, or rounds other values in their place, can miss the bound.
Values may be sent and summed in bfloat16 or wider, within the bound.
No kernel may reach another device: no remote copies, remote signals or barrier semaphores. Data moves between devices by JAX's collectives and lax.ppermute only.
A program may use at most 192 MiB of HBM per device.

```python
import jax
import jax.numpy as jnp
from jax import lax

D = 512
HD = 64
LAT = 256
POS = 4096
PATCH = 32
KSIZE = 3
LAYERS = 2
CON_DEV = 256
CONTACTS = 8192
NPATCH = 32
SAMPLES = 1024
N_CONTACTS = 32


def draw_latents(key, part):
    key_base = jax.random.fold_in(key, 0)
    base_vals = jax.random.normal(key_base, (LAT, D), jnp.float32)
    base_vals = jnp.clip(base_vals, -4.0, 4.0)
    return base_vals.astype(jnp.bfloat16)


def draw_live_count(key, part):
    key_vals = jax.random.fold_in(key, 701)
    key_order = jax.random.fold_in(key, 702)
    counts = jax.random.randint(key_vals, (N_CONTACTS,), CON_DEV // 2, CON_DEV + 1, dtype=jnp.int32)
    order = jax.random.permutation(key_order, N_CONTACTS)
    slots = jnp.arange(N_CONTACTS, dtype=jnp.int32)
    counts = jnp.where(slots == order[0], CON_DEV, counts)
    counts = jnp.where(slots == order[1], CON_DEV // 2, counts)
    return counts.astype(jnp.int32)


def touch_ends(entries, stream_key, least, top_value):
    spot = [jax.random.randint(jax.random.fold_in(stream_key, axis), (), 0, length) for axis, length in enumerate(entries.shape)]
    main_axis = entries.shape.index(max(entries.shape))
    next_to = spot[:main_axis] + [(spot[main_axis] + 1) % entries.shape[main_axis]] + spot[main_axis + 1:]
    return entries.at[tuple(spot)].set(least).at[tuple(next_to)].set(top_value)


def block_scale(rng, extent, cuts, low, top_value):
    gain, own = 1.0, jax.random.fold_in(rng, 6)
    for dim, shards_of in cuts:
        draws = jnp.exp(jax.random.uniform(jax.random.fold_in(own, dim), (shards_of,), jnp.float32, low / len(cuts), top_value / len(cuts)))
        gain = gain * jnp.repeat(draws, extent[dim] // shards_of).reshape([-1 if axis == dim else 1 for axis in range(len(extent))])
    return gain


def gaussian(rng, extent, scale, most, shards=(), kind=jnp.bfloat16):
    array = jax.random.normal(rng, extent, jnp.float32) * scale
    if len(shards) > 0:
        array = block_scale(rng, extent, shards, -0.22, 0.18) * array
    return jnp.clip(array, min=-most, max=most).astype(kind)


def setup_inputs(seed: int = 0) -> dict:
    streams_of = jax.random.split(jax.random.key(seed), 13)
    return {
        "signal": gaussian(streams_of[0], (CONTACTS, SAMPLES), 1.0, 6.0, ((0, 32), (1, 8))),
        "pos_idx": touch_ends(jax.random.randint(streams_of[1], (CONTACTS,), 0, POS), jax.random.fold_in(streams_of[1], 1), 0, POS - 1).astype(jnp.int32),
        "live_count": draw_live_count(jax.random.fold_in(streams_of[12], 71), 0),
        "latents": draw_latents(jax.random.fold_in(streams_of[12], 71), 0),
        "pos_table": gaussian(streams_of[4], (POS, D), 1.0, 6.0),
        "w_in": gaussian(streams_of[5], (PATCH, D), PATCH ** -0.5, 1.0),
        "w_kv": gaussian(streams_of[6], (D, 2 * D), D ** -0.5, 0.25),
        "w_query": gaussian(streams_of[7], (D, D), D ** -0.5, 0.25),
        "w_out": gaussian(streams_of[8], (D, D), D ** -0.5, 0.25),
        "conv_weight": gaussian(streams_of[9], (LAYERS, KSIZE, D, D), (3 * D) ** -0.5, 0.15625),
        "conv_bias": gaussian(streams_of[10], (LAYERS, D), 0.5, 3.0, (), jnp.float32),
        "cotangent": gaussian(streams_of[11], (NPATCH, LAT, D), 1.0, 6.0, ((0, 8), (1, 32))),
    }


neg_big = -1.0e30
scale_dot = 0.125


def rounded(value):
    return lax.optimization_barrier(value.astype(jnp.bfloat16))


def silu_slope(pre_act):
    sigmoid_v = jax.nn.sigmoid(pre_act)
    return sigmoid_v * (1.0 + pre_act * (1.0 - sigmoid_v))


def reference(signal, pos_idx, live_count, latents, pos_table, w_in, w_kv, w_query, w_out, conv_weight, conv_bias, cotangent):
    head_count = D // HD
    contact_ids = jnp.arange(CONTACTS, dtype=jnp.int32)
    is_valid = (contact_ids % CON_DEV) < jnp.repeat(live_count, CON_DEV)
    pos_rows = jnp.take(pos_table, pos_idx, axis=0).astype(jnp.float32)
    queries = rounded(jnp.dot(latents, w_query, preferred_element_type=jnp.float32))
    query_f = queries.astype(jnp.float32).reshape(LAT, head_count, HD)

    def patch_keys(patch_idx):
        sig_piece = lax.dynamic_slice_in_dim(signal, patch_idx * PATCH, PATCH, 1)
        embedded = jnp.dot(sig_piece, w_in, preferred_element_type=jnp.float32)
        tokens = rounded(embedded + pos_rows)
        keyval = rounded(jnp.dot(tokens, w_kv, preferred_element_type=jnp.float32)).astype(jnp.float32)
        key_part = keyval[:, :D].reshape(CONTACTS, head_count, HD)
        value_part = keyval[:, D:].reshape(CONTACTS, head_count, HD)
        return key_part, value_part

    def masked_scores(key_part):
        scores = jnp.einsum("ihe,che->hic", query_f, key_part) * scale_dot
        return jnp.where(is_valid, scores, neg_big)

    def forward_patch(patch_idx):
        key_part, value_part = patch_keys(patch_idx)
        scores = masked_scores(key_part)
        top_score = jnp.max(scores, axis=2)
        weights = jnp.where(is_valid, jnp.exp(scores - top_score[..., None]), 0.0)
        totals = jnp.sum(weights, axis=2)
        weights_b = rounded(weights).astype(jnp.float32)
        mixed = jnp.einsum("hic,che->ihe", weights_b, value_part)
        attended = (mixed / jnp.transpose(totals)[:, :, None]).reshape(LAT, D).astype(jnp.bfloat16)
        return attended, top_score, totals

    patch_ids = jnp.arange(NPATCH, dtype=jnp.int32)
    attended, top_all, total_all = lax.map(forward_patch, patch_ids)
    attended = lax.optimization_barrier(attended)

    start_x = rounded(jnp.dot(attended.reshape(NPATCH * LAT, D), w_out, preferred_element_type=jnp.float32)).reshape(NPATCH, LAT, D)
    hidden_list = []
    current = start_x
    for layer_no in range(LAYERS):
        dilation = 2 ** layer_no
        padded = jnp.pad(current, ((dilation, dilation), (0, 0), (0, 0)))
        stacked = jnp.stack([padded[j * dilation: j * dilation + NPATCH] for j in range(KSIZE)], axis=2).astype(jnp.float32)
        pre_act = jnp.einsum("tlji,jio->tlo", stacked, conv_weight[layer_no].astype(jnp.float32)) + conv_bias[layer_no]
        current = rounded(current.astype(jnp.float32) + jax.nn.silu(pre_act))
        hidden_list.append(pre_act)
    features = current

    grad_now = cotangent.astype(jnp.float32)
    for layer_no in reversed(range(LAYERS)):
        dilation = 2 ** layer_no
        grad_pre = rounded(grad_now * silu_slope(hidden_list[layer_no]))
        padded = jnp.pad(grad_pre, ((dilation, dilation), (0, 0), (0, 0)))
        stacked = jnp.stack([padded[(KSIZE - 1 - j) * dilation: (KSIZE - 1 - j) * dilation + NPATCH] for j in range(KSIZE)], axis=2).astype(jnp.float32)
        grad_now = grad_now + jnp.einsum("tljo,jio->tli", stacked, conv_weight[layer_no].astype(jnp.float32))

    grad_att = rounded(lax.dot_general(rounded(grad_now).reshape(NPATCH * LAT, D), w_out, (((1,), (1,)), ((), ())), preferred_element_type=jnp.float32)).reshape(NPATCH, LAT, D)
    delta_row = jnp.sum(grad_att.astype(jnp.float32).reshape(NPATCH, LAT, head_count, HD) * attended.astype(jnp.float32).reshape(NPATCH, LAT, head_count, HD), axis=3)

    def back_patch(dq_sum, patch_idx):
        key_part, value_part = patch_keys(patch_idx)
        scores = masked_scores(key_part)
        top_now = top_all[patch_idx]
        total_now = total_all[patch_idx]
        prob_vals = jnp.where(is_valid, jnp.exp(scores - top_now[..., None]) / total_now[..., None], 0.0)
        grad_rows = grad_att[patch_idx].astype(jnp.float32).reshape(LAT, head_count, HD)
        grad_prob = jnp.einsum("ihe,che->hic", grad_rows, value_part)
        delta_now = jnp.transpose(delta_row[patch_idx])
        dscore = rounded(prob_vals * (grad_prob - delta_now[..., None])).astype(jnp.float32)
        return dq_sum + jnp.einsum("hic,che->ihe", dscore, key_part), None

    dq_sum, unused = lax.scan(back_patch, jnp.zeros((LAT, head_count, HD), jnp.float32), patch_ids)
    query_grad = (dq_sum * scale_dot).reshape(LAT, D)
    d_latents = lax.dot_general(rounded(query_grad), w_query, (((1,), (1,)), ((), ())), preferred_element_type=jnp.float32)
    return features, d_latents
```

```python
import jax
import jax.numpy as jnp
from jax import lax
from jax.experimental import pallas as pl
from jax.experimental.pallas import tpu as pltpu
from jax.sharding import Mesh
from jax.sharding import PartitionSpec as P

HD = 64
PATCH = 32
KSIZE = 3
LAYERS = 2

neg_big = -1e30
scale_dot = 0.125

bf16 = jnp.bfloat16
f32 = jnp.float32

NY, NZH, NZL, NTM = 4, 4, 2, 8


def nt_dot(a, b):
    return lax.dot_general(a, b, (((1,), (1,)), ((), ())), preferred_element_type=f32)


def nn_dot(a, b):
    return jnp.dot(a, b, preferred_element_type=f32)


def head_of_lane(shape):
    return lax.broadcasted_iota(jnp.int32, shape, len(shape) - 1) // HD


def spread_heads(rows, heads):
    head = head_of_lane(rows.shape)
    zero = jnp.zeros_like(rows)
    return jnp.concatenate([jnp.where(head == h, rows, zero) for h in range(heads)], axis=0)


def collect_heads(blocks, heads):
    r = blocks.shape[0] // heads
    head = head_of_lane((r, blocks.shape[1]))
    out = blocks[:r]
    for h in range(1, heads):
        out = jnp.where(head == h, blocks[h * r : (h + 1) * r], out)
    return out


def columns_to_lanes(column, heads, first, base):
    r = base.shape[0]
    lane = lax.broadcasted_iota(jnp.int32, base.shape, 1)
    for h in range(heads):
        base = jnp.where(lane == first + h, column[h * r : (h + 1) * r], base)
    return base


def lanes_to_column(stats, heads, first):
    return jnp.concatenate([stats[:, first + h : first + h + 1] for h in range(heads)], axis=0)


def lanes_to_columns_wide(stats, heads, first):
    r = stats.shape[0]
    head = head_of_lane((r, heads * HD))
    out = jnp.broadcast_to(stats[:, first : first + 1], (r, heads * HD))
    for h in range(1, heads):
        out = jnp.where(head == h, stats[:, first + h : first + h + 1], out)
    return out


def silu_slope(pre_act):
    sigmoid_v = jax.nn.sigmoid(pre_act)
    return sigmoid_v * (1.0 + pre_act * (1.0 - sigmoid_v))


def rounded(value):
    return value.astype(bf16).astype(f32)


def pos_kernel(idx_ref, table_ref, out_ref):
    idx = idx_ref[...]
    n, pos = idx.shape[0], table_ref.shape[0]
    step = 512
    acc = jnp.zeros(out_ref.shape, f32)
    for k in range(pos // step):
        ids = lax.broadcasted_iota(jnp.int32, (n, step), 1) + k * step
        hot = jnp.where(ids == idx, 1.0, 0.0).astype(bf16)
        acc = acc + nn_dot(hot, table_ref[k * step : (k + 1) * step, :])
    out_ref[...] = acc.astype(bf16)


def pos_rows(idx, table):
    rows, width = idx.shape[0], table.shape[1]
    tile = 256
    return pl.pallas_call(
        pos_kernel,
        grid=(rows // tile,),
        in_specs=[
            pl.BlockSpec((tile, 1), lambda i: (i, 0)),
            pl.BlockSpec(table.shape, lambda i: (0, 0), pipeline_mode=pl.Buffered(1)),
        ],
        out_specs=pl.BlockSpec((tile, width), lambda i: (i, 0)),
        out_shape=jax.ShapeDtypeStruct((rows, width), bf16),
        name="pos_rows",
    )(idx, table)


def forward_kernel(sig_ref, pos_ref, valid_ref, q_ref, w_in_ref, w_kv_ref, kv_ref, part_ref, score_ref):
    heads = q_ref.shape[1] // HD
    width = q_ref.shape[1]
    contacts = sig_ref.shape[0]
    step = 256
    window = pl.program_id(0)
    w_in = w_in_ref[...]
    tall = jnp.concatenate([w_in] * (sig_ref.shape[1] // PATCH), axis=0)
    own = lax.broadcasted_iota(jnp.int32, tall.shape, 0) // PATCH == window
    w_here = jnp.where(own, tall, jnp.zeros_like(tall))
    q_wide = spread_heads(q_ref[...], heads)
    for k in range(contacts // step):
        rows = slice(k * step, (k + 1) * step)
        embedded = nn_dot(sig_ref[rows, :], w_here)
        tokens = (embedded + pos_ref[rows, :].astype(f32)).astype(bf16)
        keyval = nn_dot(tokens, w_kv_ref[...]).astype(bf16)
        kv_ref[0, rows, :] = keyval
        scores = nt_dot(q_wide, keyval[:, :width]) * scale_dot
        score_ref[:, rows] = jnp.where(valid_ref[:, rows] > 0.0, scores, neg_big)
    top = jnp.max(score_ref[...], axis=1, keepdims=True)
    totals = jnp.zeros_like(top)
    accum = jnp.zeros((q_wide.shape[0], width), f32)
    for k in range(contacts // step):
        rows = slice(k * step, (k + 1) * step)
        weights = jnp.exp(score_ref[:, rows] - top)
        totals = totals + jnp.sum(weights, axis=1, keepdims=True)
        accum = accum + nn_dot(weights.astype(bf16), kv_ref[0, rows, width:])
    mixed = collect_heads(accum, heads)
    lat = mixed.shape[0]
    stats = jnp.zeros((lat, 128), f32)
    stats = columns_to_lanes(top, heads, 0, stats)
    stats = columns_to_lanes(totals, heads, heads, stats)
    each = part_ref.shape[2]
    for s in range(part_ref.shape[0]):
        part_ref[s, 0, :, :width] = mixed[s * each : (s + 1) * each]
        part_ref[s, 0, :, width:] = stats[s * each : (s + 1) * each]


def forward_attention(sig, pos, valid, q, w_in, w_kv, slots):
    contacts, width = pos.shape
    windows = sig.shape[1] // PATCH
    lat = q.shape[0]
    whole = lambda a: pl.BlockSpec(a.shape, lambda p: (0,) * a.ndim, pipeline_mode=pl.Buffered(1))
    return pl.pallas_call(
        forward_kernel,
        grid=(windows,),
        in_specs=[whole(sig), whole(pos), whole(valid), whole(q), whole(w_in), whole(w_kv)],
        out_specs=[
            pl.BlockSpec((1, contacts, 2 * width), lambda p: (p, 0, 0)),
            pl.BlockSpec((slots, 1, lat // slots, width + 128), lambda p: (0, p, 0, 0)),
        ],
        out_shape=[
            jax.ShapeDtypeStruct((windows, contacts, 2 * width), bf16),
            jax.ShapeDtypeStruct((slots, windows, lat // slots, width + 128), f32),
        ],
        scratch_shapes=[pltpu.VMEM((lat * (width // HD), contacts), f32)],
        name="forward_attention",
    )(sig, pos, valid, q, w_in, w_kv)


def combine_kernel(*refs):
    *part_refs, att_ref, stats_ref = refs
    rows, width = att_ref.shape
    heads = width // HD
    lane = lax.broadcasted_iota(jnp.int32, (rows, 128), 1)
    parts = [ref[...].reshape(rows, width + 128) for ref in part_refs]
    top = parts[0][:, width:]
    for part in parts[1:]:
        top = jnp.maximum(top, part[:, width:])
    totals = jnp.zeros((rows, 128), f32)
    accum = jnp.zeros((rows, width), f32)
    for part in parts:
        factor = jnp.exp(jnp.where(lane < heads, part[:, width:] - top, 0.0))
        totals = totals + factor * pltpu.roll(part[:, width:], 128 - heads, 1)
        accum = accum + part[:, :width] * lanes_to_columns_wide(factor, heads, 0)
    totals = jnp.where(lane < heads, totals, 1.0)
    att_ref[...] = (accum / lanes_to_columns_wide(totals, heads, 0)).astype(bf16)
    stats_ref[...] = jnp.where(lane < heads, top, pltpu.roll(1.0 / totals, heads, 1))


def combine(parts):
    windows, each, wide = parts[0].shape
    rows = windows * each
    return pl.pallas_call(
        combine_kernel,
        out_shape=[
            jax.ShapeDtypeStruct((rows, wide - 128), bf16),
            jax.ShapeDtypeStruct((rows, 128), f32),
        ],
        name="combine_parts",
    )(*parts)


def conv_kernel(
    tm_ref, l2_ref, l4_ref, own_ref, r4_ref, r2_ref, stats_ref, cl_ref, cot_ref, cr_ref,
    w_out_ref, conv_ref, bias_ref, feat_ref, msg_ref,
):
    rows, width = own_ref.shape
    heads = width // HD
    windows = 4
    each = rows // windows
    reach = 6
    first = tm_ref[0] * windows - reach
    total_windows = NTM * windows

    def inside(lo, count):
        w = lax.broadcasted_iota(jnp.int32, (count * each, width), 0) // each + (first + lo)
        return jnp.logical_and(w >= 0, w < total_windows)

    att = jnp.concatenate([r[...].astype(f32) for r in (l2_ref, l4_ref, own_ref, r4_ref, r2_ref)], axis=0)
    w_out = w_out_ref[...]
    x0 = rounded(nn_dot(att.astype(bf16), w_out))
    n0 = 14 * each
    pre0 = bias_ref[0:1, :] + sum(nn_dot(x0[j * each : j * each + n0].astype(bf16), conv_ref[0, j]) for j in range(KSIZE))
    x1 = rounded(x0[each : each + n0] + jax.nn.silu(pre0))
    x1 = jnp.where(inside(1, 14), x1, 0.0)
    n1 = 10 * each
    pre1 = bias_ref[1:2, :] + sum(nn_dot(x1[2 * j * each : 2 * j * each + n1].astype(bf16), conv_ref[1, j]) for j in range(KSIZE))
    feat_ref[...] = (x1[5 * each : 9 * each] + jax.nn.silu(pre1[3 * each : 7 * each])).astype(bf16)
    g2 = jnp.concatenate([r[...].astype(f32) for r in (cl_ref, cot_ref, cr_ref)], axis=0)
    gpre1 = rounded(g2 * silu_slope(pre1))
    n2 = 6 * each
    g1 = g2[2 * each : 8 * each] + sum(
        nt_dot(gpre1[(4 - 2 * j) * each : (4 - 2 * j) * each + n2].astype(bf16), conv_ref[1, j]) for j in range(KSIZE)
    )
    gpre0 = rounded(g1 * silu_slope(pre0[4 * each : 10 * each]))
    gpre0 = jnp.where(inside(5, 6), gpre0, 0.0)
    g0 = g1[each : 5 * each] + sum(
        nt_dot(gpre0[(2 - j) * each : (2 - j) * each + rows].astype(bf16), conv_ref[0, j]) for j in range(KSIZE)
    )
    grad_att = rounded(nt_dot(g0.astype(bf16), w_out))
    msg_ref[:, :width] = grad_att.astype(bf16)
    product = grad_att * own_ref[...].astype(f32)
    head = head_of_lane((rows, width))
    lane = lax.broadcasted_iota(jnp.int32, (rows, 128), 1)
    stats = stats_ref[...]
    for h in range(heads):
        delta = jnp.sum(jnp.where(head == h, product, 0.0), axis=1, keepdims=True)
        stats = jnp.where(lane == 2 * heads + h, delta, stats)
    stats = jnp.where(lane < 3 * heads, stats, 0.0)
    high = rounded(stats)
    middle = rounded(stats - high)
    low = (stats - high) - middle
    msg_ref[:, width:] = (high + pltpu.roll(middle, 32, 1) + pltpu.roll(low, 64, 1)).astype(bf16)


def conv_stack(tm, halo, own, stats, cots, w_out, conv_weight, conv_bias):
    rows, width = own.shape
    l2, l4, r4, r2 = halo
    cl, cot, cr = cots
    vmem = pl.BlockSpec(memory_space=pltpu.VMEM)
    return pl.pallas_call(
        conv_kernel,
        in_specs=[pl.BlockSpec(memory_space=pltpu.SMEM)] + [vmem] * 12,
        out_specs=[vmem, vmem],
        out_shape=[
            jax.ShapeDtypeStruct((rows, width), bf16),
            jax.ShapeDtypeStruct((rows, width + 128), bf16),
        ],
        name="conv_stack",
    )(tm, l2, l4, own, r4, r2, stats, cl, cot, cr, w_out, conv_weight, conv_bias)


def backward_kernel(zh_ref, kv_ref, valid_ref, q_ref, *refs):
    *msg_refs, dq_ref, acc_ref = refs
    width = q_ref.shape[1]
    heads = width // HD
    contacts = kv_ref.shape[1]
    step = 256
    window = pl.program_id(0)
    msg = jnp.concatenate([r[0].astype(f32) for r in msg_refs], axis=0)
    terms = msg[:, width:]
    stats = terms + pltpu.roll(terms, 96, 1) + pltpu.roll(terms, 64, 1)
    top = lanes_to_column(stats, heads, 0)
    inverse = lanes_to_column(stats, heads, heads)
    delta = lanes_to_column(stats, heads, 2 * heads)
    grad_wide = spread_heads(msg[:, :width].astype(bf16), heads)
    q_wide = spread_heads(q_ref[...], heads)
    accum = jnp.zeros((q_wide.shape[0], width), f32)
    for k in range(contacts // step):
        rows = slice(k * step, (k + 1) * step)
        key_rows = kv_ref[0, rows, :width]
        scores = nt_dot(q_wide, key_rows) * scale_dot
        scores = jnp.where(valid_ref[:, rows] > 0.0, scores, neg_big)
        prob = jnp.exp(scores - top) * inverse
        grad_prob = nt_dot(grad_wide, kv_ref[0, rows, width:])
        dscore = (prob * (grad_prob - delta)).astype(bf16)
        accum = accum + nn_dot(dscore, key_rows)

    @pl.when(window == 0)
    def _():
        acc_ref[...] = accum

    @pl.when(window > 0)
    def _():
        acc_ref[...] = acc_ref[...] + accum

    @pl.when(window == pl.num_programs(0) - 1)
    def _():
        dq = collect_heads(acc_ref[...], heads) * scale_dot
        slots = len(msg_refs)
        each = dq.shape[0] // slots
        for s in range(slots):
            place = pl.multiple_of(((zh_ref[0] + (slots - s)) % slots) * each, each)
            dq_ref[pl.ds(place, each), :] = dq[s * each : (s + 1) * each]


def backward_attention(zh, kv, valid, q, msgs):
    windows, contacts, wide = kv.shape
    lat, width = q.shape
    heads = width // HD
    whole = lambda a: pl.BlockSpec(a.shape, lambda p: (0,) * a.ndim, pipeline_mode=pl.Buffered(1))
    return pl.pallas_call(
        backward_kernel,
        grid=(windows,),
        in_specs=[
            pl.BlockSpec(memory_space=pltpu.SMEM),
            pl.BlockSpec((1, contacts, wide), lambda p: (p, 0, 0)),
            whole(valid),
            whole(q),
        ]
        + [pl.BlockSpec((1,) + m.shape[1:], lambda p: (p, 0, 0)) for m in msgs],
        out_specs=pl.BlockSpec((lat, width), lambda p: (0, 0)),
        out_shape=jax.ShapeDtypeStruct((lat, width), f32),
        scratch_shapes=[pltpu.VMEM((lat * heads, width), f32)],
        name="backward_attention",
    )(zh, kv, valid, q, *msgs)


def shift(axis, count, by):
    return [(i, (i + by) % count) for i in range(count)]


def local(
    signal, pos_idx, live_count, latents, pos_table, w_in, w_kv, w_query, w_out,
    conv_weight, conv_bias, cotangent,
):
    con_dev = signal.shape[0]
    pat_dev = signal.shape[1] // PATCH
    width = w_query.shape[0]
    lat_rows = latents.shape[0]
    y, zh, zl, tm = (lax.axis_index(a) for a in ("y", "zh", "zl", "tm"))
    lat_dev = lat_rows // (NY * NZH * NZL)

    up1 = [(i, i + 1) for i in range(NTM - 1)]
    down1 = [(i + 1, i) for i in range(NTM - 1)]
    up2 = [(i, i + 2) for i in range(NTM - 2)]
    down2 = [(i + 2, i) for i in range(NTM - 2)]
    cot = cotangent.reshape(pat_dev * lat_dev, width)

    high = (pos_idx // 64).astype(bf16).reshape(-1, signal.shape[1])
    low = (pos_idx % 64).astype(bf16).reshape(-1, signal.shape[1])
    live = jnp.broadcast_to(live_count.astype(bf16)[:, None], (4, signal.shape[1]))
    message = jnp.concatenate([signal, high, low, live], axis=0)
    other = lax.ppermute(message, "zl", shift("zl", NZL, 1))
    pair = jnp.stack([message, other])
    group = jnp.concatenate([pair] + [lax.ppermute(pair, "y", shift("y", NY, s)) for s in range(1, NY)], axis=0)
    blocks = group.shape[0]
    sig = group[:, :con_dev].reshape(blocks * con_dev, -1)
    tail = group[:, con_dev:].astype(f32)
    half = high.shape[0]
    idx = (tail[:, :half] * 64.0 + tail[:, half : 2 * half]).astype(jnp.int32).reshape(blocks * con_dev, 1)
    lives = tail[:, 2 * half, :1]
    valid = (jnp.arange(con_dev, dtype=jnp.int32)[None, :].astype(f32) < lives).astype(f32)
    valid = valid.reshape(1, blocks * con_dev)

    cot_left = lax.ppermute(cot[lat_dev:], "tm", up1)
    cot_right = lax.ppermute(cot[: 3 * lat_dev], "tm", down1)

    by_owner = latents.reshape(NY, NZH, NZL, lat_dev, width)
    mine = lax.dynamic_slice(by_owner, (y, 0, zl, 0, 0), (1, NZH, 1, lat_dev, width)).reshape(NZH, lat_dev, width)
    slots = jnp.stack([lax.dynamic_index_in_dim(mine, (zh + NZH - s) % NZH, 0, False) for s in range(NZH)])
    queries = nn_dot(slots.reshape(NZH * lat_dev, width), w_query).astype(bf16)

    pos = pos_rows(idx, pos_table)
    kv, parts = forward_attention(sig, pos, valid, queries, w_in, w_kv, NZH)
    received = [lax.ppermute(parts[s], "zh", shift("zh", NZH, -s)) for s in range(1, NZH)]
    att, stats = combine([parts[0]] + received)

    left4 = lax.ppermute(att, "tm", up1)
    right4 = lax.ppermute(att, "tm", down1)
    left2 = lax.ppermute(att[2 * lat_dev :], "tm", up2)
    right2 = lax.ppermute(att[: 2 * lat_dev], "tm", down2)
    features, msg = conv_stack(
        tm.reshape(1), (left2, left4, right4, right2), att, stats,
        (cot_left, cot, cot_right), w_out, conv_weight, conv_bias,
    )

    msg = msg.reshape(pat_dev, lat_dev, width + 128)
    msgs = [msg] + [lax.ppermute(msg, "zh", shift("zh", NZH, s)) for s in range(1, NZH)]
    dq = backward_attention(zh.reshape(1), kv, valid, queries, msgs)

    pieces = lax.all_to_all(dq, ("zh", "tm"), 0, 0, tiled=True)
    dq_row = jnp.sum(pieces, axis=0, keepdims=True).astype(bf16)
    dq_all = lax.all_to_all(
        jnp.broadcast_to(dq_row, (lat_rows, width)), ("y", "zh", "zl", "tm"), 0, 0, tiled=True
    )
    d_latents = nt_dot(dq_all, w_query)
    return features.reshape(pat_dev, lat_dev, width), d_latents


def solution(mesh):
    split = Mesh(mesh.devices.reshape(NY, NZH, NZL, NTM), ("y", "zh", "zl", "tm"))
    contacts = ("y", "zh", "zl")
    in_specs = (
        P(contacts, "tm"),
        P(contacts),
        P(contacts),
        P(),
        P(),
        P(),
        P(),
        P(),
        P(),
        P(),
        P(),
        P("tm", contacts, None),
    )
    out_specs = (P("tm", contacts, None), P())
    return jax.shard_map(local, mesh=split, in_specs=in_specs, out_specs=out_specs, check_vma=False)
```

```python
import functools

import jax
import jax.numpy as jnp
from jax import lax
from jax.experimental import pallas as pl
from jax.experimental.pallas import tpu as pltpu
from jax.sharding import Mesh
from jax.sharding import PartitionSpec as P

HD = 64
PATCH = 32
KSIZE = 3
LAYERS = 2

neg_big = -1e30
scale_dot = 0.125

bf16 = jnp.bfloat16
f32 = jnp.float32

NY, NZ, NTM = 4, 8, 8
MIB = 1 << 20


def nt_dot(a, b):
    return lax.dot_general(a, b, (((1,), (1,)), ((), ())), preferred_element_type=f32)


def nn_dot(a, b):
    return jnp.dot(a, b, preferred_element_type=f32)


def head_of_lane(shape):
    return lax.broadcasted_iota(jnp.int32, shape, len(shape) - 1) // HD


def spread_heads(rows, heads):
    head = head_of_lane(rows.shape)
    zero = jnp.zeros_like(rows)
    return jnp.concatenate([jnp.where(head == h, rows, zero) for h in range(heads)], axis=0)


def collect_heads(blocks, heads):
    r = blocks.shape[0] // heads
    head = head_of_lane((r, blocks.shape[1]))
    out = blocks[:r]
    for h in range(1, heads):
        out = jnp.where(head == h, blocks[h * r : (h + 1) * r], out)
    return out


def columns_to_lanes(column, heads, first, base):
    r = base.shape[0]
    lane = lax.broadcasted_iota(jnp.int32, base.shape, 1)
    for h in range(heads):
        base = jnp.where(lane == first + h, column[h * r : (h + 1) * r], base)
    return base


def lanes_to_column(stats, heads, first):
    return jnp.concatenate([stats[:, first + h : first + h + 1] for h in range(heads)], axis=0)


def lanes_to_columns_wide(stats, heads, first):
    r = stats.shape[0]
    head = head_of_lane((r, heads * HD))
    out = jnp.broadcast_to(stats[:, first : first + 1], (r, heads * HD))
    for h in range(1, heads):
        out = jnp.where(head == h, stats[:, first + h : first + h + 1], out)
    return out


def silu_slope(pre_act):
    sigmoid_v = jax.nn.sigmoid(pre_act)
    return sigmoid_v * (1.0 + pre_act * (1.0 - sigmoid_v))


def rounded(value):
    return value.astype(bf16).astype(f32)


def absorb_kernel(*refs, fresh, last, count):
    refs = list(refs)
    messages = [refs.pop(0) for _ in range(count)]
    q_ref, w_in_ref, w_kv_ref, table_ref = (refs.pop(0) for _ in range(4))
    if not fresh:
        refs.pop(0), refs.pop(0)
        acc_in, stat_in = refs.pop(0), refs.pop(0)
    kv_ref, valid_ref = refs.pop(0), refs.pop(0)
    if last:
        part_refs = [refs.pop(0) for _ in range(NY)]
    else:
        acc_out, stat_out = refs.pop(0), refs.pop(0)
    pos_ref = refs.pop(0)
    width = q_ref.shape[1]
    heads = width // HD
    con_dev, span = messages[0].shape[0], messages[0].shape[1] - 128
    step_no = pl.program_id(0)
    message = messages[0][...]
    if count == 2:
        message = jnp.where(step_no == 0, message, messages[1][...])
    sig = message[:, :span]
    meta = message[:, span:].astype(f32)
    idx = meta[:, 0:1] * 64.0 + meta[:, 1:2]
    live = meta[0:1, 2:3]
    lane = lax.broadcasted_iota(jnp.int32, (1, con_dev), 1).astype(f32)
    valid = jnp.where(lane < live, 1.0, 0.0)
    valid_ref[...] = jnp.broadcast_to(valid, valid_ref.shape)
    piece = 512
    ids = lax.broadcasted_iota(jnp.int32, (con_dev, piece), 1).astype(f32)

    def add_rows(k, pos):
        for part in range(2):
            start = pl.multiple_of((2 * k + part) * piece, piece)
            hot = jnp.where(ids == idx - start.astype(f32), 1.0, 0.0).astype(bf16)
            pos = pos + nn_dot(hot, table_ref[pl.ds(start, piece), :])
        return pos

    pos = lax.fori_loop(0, table_ref.shape[0] // (2 * piece), add_rows, jnp.zeros((con_dev, width), f32))
    pos_ref[...] = pos
    windows = span // PATCH

    def one_window(w):
        pos = pos_ref[...]
        q_wide = spread_heads(q_ref[...], heads)
        tall = jnp.concatenate([w_in_ref[...]] * windows, axis=0)
        band = lax.broadcasted_iota(jnp.int32, tall.shape, 0) // PATCH
        embedded = nn_dot(sig, jnp.where(band == w, tall, jnp.zeros_like(tall)))
        tokens = (embedded + pos).astype(bf16)
        keyval = nn_dot(tokens, w_kv_ref[...]).astype(bf16)
        kv_ref[w] = keyval
        scores = nt_dot(q_wide, keyval[:, :width]) * scale_dot
        scores = jnp.where(valid > 0.0, scores, neg_big)
        top = jnp.max(scores, axis=1, keepdims=True)
        if not fresh:
            acc_now, stat_now = (acc_out, stat_out) if count > 1 else (acc_in, stat_in)
            before, total_before, acc_before = stat_now[w, :, 0:1], stat_now[w, :, 1:2], acc_now[w]
            top = jnp.maximum(top, before)
        weights = jnp.exp(scores - top)
        totals = jnp.sum(weights, axis=1, keepdims=True)
        accum = nn_dot(weights.astype(bf16), keyval[:, width:])
        if not fresh:
            fade = jnp.exp(before - top)
            totals = totals + total_before * fade
            accum = accum + acc_before * fade
        if not last:
            acc_out[w] = accum
            stat_out[w, :, 0:1] = top
            stat_out[w, :, 1:2] = totals
        else:
            mixed = collect_heads(accum, heads)
            stats = jnp.zeros((mixed.shape[0], 128), f32)
            stats = columns_to_lanes(top, heads, 0, stats)
            stats = columns_to_lanes(totals, heads, heads, stats)
            each = mixed.shape[0] // NY
            for s, part_ref in enumerate(part_refs):
                part_ref[w, :, :width] = mixed[s * each : (s + 1) * each]
                part_ref[w, :, width:] = stats[s * each : (s + 1) * each]

    if count > 1:

        @pl.when(step_no == 0)
        def _():
            acc_out[...] = acc_in[...]
            stat_out[...] = stat_in[...]

    @pl.loop(0, windows // 2)
    def _(k):
        one_window(2 * k)
        one_window(2 * k + 1)


def absorb(messages, base, q, w_in, w_kv, table, state, last):
    count = len(messages)
    lat, width = q.shape
    con_dev = messages[0].shape[0]
    windows = (messages[0].shape[1] - 128) // PATCH
    rows = lat * (width // HD)
    fresh = state is None
    whole = lambda a: pl.BlockSpec(a.shape, lambda i: (0,) * a.ndim, pipeline_mode=pl.Buffered(1))
    fixed = lambda shape: pl.BlockSpec(shape, lambda i: (0,) * len(shape), pipeline_mode=pl.Buffered(1))
    anywhere = pl.BlockSpec(memory_space=pl.ANY)
    operands = list(messages) + [q, w_in, w_kv, table]
    in_specs = [whole(a) for a in operands]
    aliases = {}
    if not fresh:
        n = len(operands)
        operands += list(state)
        in_specs += [anywhere, anywhere] + [whole(a) for a in state[2:]]
        aliases = {n: 0, n + 1: 1}
    acc = jax.ShapeDtypeStruct((windows, rows, width), f32)
    stat = jax.ShapeDtypeStruct((windows, rows, 128), f32)
    part = jax.ShapeDtypeStruct((windows, lat // NY, width + 128), f32)
    tail = [part] * NY if last else [acc, stat]
    return pl.pallas_call(
        functools.partial(absorb_kernel, fresh=fresh, last=last, count=count),
        grid=(count,),
        in_specs=in_specs,
        out_specs=[
            pl.BlockSpec((windows, con_dev, 2 * width), lambda i: (0, base + i, 0)),
            pl.BlockSpec((8, con_dev), lambda i: (0, base + i)),
        ]
        + [fixed(a.shape) for a in tail],
        out_shape=[
            jax.ShapeDtypeStruct((windows, NZ * con_dev, 2 * width), bf16),
            jax.ShapeDtypeStruct((8, NZ * con_dev), f32),
        ]
        + tail,
        scratch_shapes=[pltpu.VMEM((con_dev, width), f32)],
        input_output_aliases=aliases,
        compiler_params=pltpu.CompilerParams(vmem_limit_bytes=28 * MIB),
        name="absorb",
    )(*operands)


def combine_kernel(*refs):
    *part_refs, att_ref, stats_ref = refs
    rows, width = att_ref.shape
    heads = width // HD
    lane = lax.broadcasted_iota(jnp.int32, (rows, 128), 1)
    parts = [ref[...].reshape(rows, width + 128) for ref in part_refs]
    top = parts[0][:, width:]
    for part in parts[1:]:
        top = jnp.maximum(top, part[:, width:])
    totals = jnp.zeros((rows, 128), f32)
    accum = jnp.zeros((rows, width), f32)
    for part in parts:
        factor = jnp.exp(jnp.where(lane < heads, part[:, width:] - top, 0.0))
        totals = totals + factor * pltpu.roll(part[:, width:], 128 - heads, 1)
        accum = accum + part[:, :width] * lanes_to_columns_wide(factor, heads, 0)
    totals = jnp.where(lane < heads, totals, 1.0)
    att_ref[...] = (accum / lanes_to_columns_wide(totals, heads, 0)).astype(bf16)
    stats_ref[...] = jnp.where(lane < heads, top, pltpu.roll(1.0 / totals, heads, 1))


def combine(parts):
    windows, each, wide = parts[0].shape
    rows = windows * each
    return pl.pallas_call(
        combine_kernel,
        out_shape=[
            jax.ShapeDtypeStruct((rows, wide - 128), bf16),
            jax.ShapeDtypeStruct((rows, 128), f32),
        ],
        compiler_params=pltpu.CompilerParams(vmem_limit_bytes=8 * MIB),
        name="combine_parts",
    )(*parts)


def conv_kernel(
    tm_ref, left_ref, own_ref, partner_ref, right_ref, stats_ref, cl_ref, cot_ref, cr_ref,
    w_out_ref, conv_ref, bias_ref, feat_ref, msg_ref, ext_ref,
):
    rows, width = own_ref.shape
    heads = width // HD
    windows = 4
    each = rows // windows
    reach = 6
    first = tm_ref[0] * windows - reach
    total_windows = NTM * windows

    def inside(lo, count):
        w = lax.broadcasted_iota(jnp.int32, (count * each, width), 0) // each + (first + lo)
        return jnp.logical_and(w >= 0, w < total_windows)

    core = tm_ref[0] % 2
    side = reach * each
    ext_ref[:side, :] = left_ref[...].astype(f32)
    ext_ref[pl.ds(pl.multiple_of(side + core * rows, each), rows), :] = own_ref[...].astype(f32)
    ext_ref[pl.ds(pl.multiple_of(side + (1 - core) * rows, each), rows), :] = partner_ref[...].astype(f32)
    ext_ref[side + 2 * rows :, :] = right_ref[...].astype(f32)
    att = ext_ref[pl.ds(pl.multiple_of(core * rows, each), 2 * side + rows), :]
    w_out = w_out_ref[...]
    x0 = rounded(nn_dot(att.astype(bf16), w_out))
    n0 = 14 * each
    pre0 = bias_ref[0:1, :] + sum(nn_dot(x0[j * each : j * each + n0].astype(bf16), conv_ref[0, j]) for j in range(KSIZE))
    x1 = rounded(x0[each : each + n0] + jax.nn.silu(pre0))
    x1 = jnp.where(inside(1, 14), x1, 0.0)
    n1 = 10 * each
    pre1 = bias_ref[1:2, :] + sum(nn_dot(x1[2 * j * each : 2 * j * each + n1].astype(bf16), conv_ref[1, j]) for j in range(KSIZE))
    feat_ref[...] = (x1[5 * each : 9 * each] + jax.nn.silu(pre1[3 * each : 7 * each])).astype(bf16)
    g2 = jnp.concatenate([r[...].astype(f32) for r in (cl_ref, cot_ref, cr_ref)], axis=0)
    gpre1 = rounded(g2 * silu_slope(pre1))
    n2 = 6 * each
    g1 = g2[2 * each : 8 * each] + sum(
        nt_dot(gpre1[(4 - 2 * j) * each : (4 - 2 * j) * each + n2].astype(bf16), conv_ref[1, j]) for j in range(KSIZE)
    )
    gpre0 = rounded(g1 * silu_slope(pre0[4 * each : 10 * each]))
    gpre0 = jnp.where(inside(5, 6), gpre0, 0.0)
    g0 = g1[each : 5 * each] + sum(
        nt_dot(gpre0[(2 - j) * each : (2 - j) * each + rows].astype(bf16), conv_ref[0, j]) for j in range(KSIZE)
    )
    grad_att = rounded(nt_dot(g0.astype(bf16), w_out))
    msg_ref[:, :width] = grad_att.astype(bf16)
    product = grad_att * own_ref[...].astype(f32)
    head = head_of_lane((rows, width))
    lane = lax.broadcasted_iota(jnp.int32, (rows, 128), 1)
    stats = stats_ref[...]
    for h in range(heads):
        delta = jnp.sum(jnp.where(head == h, product, 0.0), axis=1, keepdims=True)
        stats = jnp.where(lane == 2 * heads + h, delta, stats)
    stats = jnp.where(lane < 3 * heads, stats, 0.0)
    high = rounded(stats)
    middle = rounded(stats - high)
    low = (stats - high) - middle
    msg_ref[:, width:] = (high + pltpu.roll(middle, 32, 1) + pltpu.roll(low, 64, 1)).astype(bf16)


def conv_stack(tm, halo, own, stats, cots, w_out, conv_weight, conv_bias):
    rows, width = own.shape
    left, partner, right = halo
    cl, cot, cr = cots
    vmem = pl.BlockSpec(memory_space=pltpu.VMEM)
    return pl.pallas_call(
        conv_kernel,
        in_specs=[pl.BlockSpec(memory_space=pltpu.SMEM)] + [vmem] * 11,
        out_specs=[vmem, vmem],
        out_shape=[
            jax.ShapeDtypeStruct((rows, width), bf16),
            jax.ShapeDtypeStruct((rows, width + 128), bf16),
        ],
        scratch_shapes=[pltpu.VMEM((left.shape[0] + 2 * rows + right.shape[0], width), f32)],
        compiler_params=pltpu.CompilerParams(vmem_limit_bytes=24 * MIB),
        name="conv_stack",
    )(tm, left, own, partner, right, stats, cl, cot, cr, w_out, conv_weight, conv_bias)


def backward_kernel(y_ref, kv_ref, valid_ref, q_ref, *refs):
    *msg_refs, dq_ref, acc_ref = refs
    width = q_ref.shape[1]
    heads = width // HD
    contacts = kv_ref.shape[1]
    step = 256
    window = pl.program_id(0)
    msg = jnp.concatenate([r[0].astype(f32) for r in msg_refs], axis=0)
    terms = msg[:, width:]
    stats = terms + pltpu.roll(terms, 96, 1) + pltpu.roll(terms, 64, 1)
    top = lanes_to_column(stats, heads, 0)
    inverse = lanes_to_column(stats, heads, heads)
    delta = lanes_to_column(stats, heads, 2 * heads)
    grad_wide = spread_heads(msg[:, :width].astype(bf16), heads)
    q_wide = spread_heads(q_ref[...], heads)

    @pl.when(window == 0)
    def _():
        acc_ref[...] = jnp.zeros_like(acc_ref)

    def one_chunk(start):
        rows = pl.ds(pl.multiple_of(start, step), step)
        key_rows = kv_ref[0, rows, :width]
        scores = nt_dot(q_wide, key_rows) * scale_dot
        scores = jnp.where(valid_ref[0:1, rows] > 0.0, scores, neg_big)
        prob = jnp.exp(scores - top) * inverse
        grad_prob = nt_dot(grad_wide, kv_ref[0, rows, width:])
        dscore = (prob * (grad_prob - delta)).astype(bf16)
        acc_ref[...] = acc_ref[...] + nn_dot(dscore, key_rows)

    @pl.loop(0, contacts // step // 2)
    def _(k):
        one_chunk(2 * k * step)
        one_chunk((2 * k + 1) * step)

    @pl.when(window == pl.num_programs(0) - 1)
    def _():
        dq = collect_heads(acc_ref[...], heads) * scale_dot
        slots = len(msg_refs)
        each = dq.shape[0] // slots
        for s in range(slots):
            place = pl.multiple_of(((y_ref[0] + (slots - s)) % slots) * each, each)
            dq_ref[pl.ds(place, each), :] = dq[s * each : (s + 1) * each]


def backward_attention(y, kv, valid, q, msgs):
    windows, contacts, wide = kv.shape
    lat, width = q.shape
    heads = width // HD
    whole = lambda a: pl.BlockSpec(a.shape, lambda p: (0,) * a.ndim, pipeline_mode=pl.Buffered(1))
    return pl.pallas_call(
        backward_kernel,
        grid=(windows,),
        in_specs=[
            pl.BlockSpec(memory_space=pltpu.SMEM),
            pl.BlockSpec((1, contacts, wide), lambda p: (p, 0, 0)),
            whole(valid),
            whole(q),
        ]
        + [pl.BlockSpec((1,) + m.shape[1:], lambda p: (p, 0, 0)) for m in msgs],
        out_specs=pl.BlockSpec((lat, width), lambda p: (0, 0)),
        out_shape=jax.ShapeDtypeStruct((lat, width), f32),
        scratch_shapes=[pltpu.VMEM((lat * heads, width), f32)],
        compiler_params=pltpu.CompilerParams(vmem_limit_bytes=52 * MIB),
        name="backward_attention",
    )(y, kv, valid, q, *msgs)


def shift(count, by):
    return [(i, (i + by) % count) for i in range(count)]


def local(
    signal, pos_idx, live_count, latents, pos_table, w_in, w_kv, w_query, w_out,
    conv_weight, conv_bias, cotangent,
):
    con_dev = signal.shape[0]
    pat_dev = signal.shape[1] // PATCH
    width = w_query.shape[0]
    lat_rows = latents.shape[0]
    y, z, tm = (lax.axis_index(a) for a in ("y", "z", "tm"))
    lat_dev = lat_rows // (NY * NZ)
    up1 = [(i, i + 1) for i in range(NTM - 1)]
    down1 = [(i + 1, i) for i in range(NTM - 1)]
    up2 = [(i, i + 2) for i in range(NTM - 2)]
    down2 = [(i + 2, i) for i in range(NTM - 2)]
    swap = [(i, i ^ 1) for i in range(NTM)]

    by_owner = latents.reshape(NY, NZ, lat_dev, width)
    mine = lax.dynamic_index_in_dim(by_owner, z, 1, False)
    slots = jnp.stack([lax.dynamic_index_in_dim(mine, (y + NY - s) % NY, 0, False) for s in range(NY)])
    queries = nn_dot(slots.reshape(NY * lat_dev, width), w_query).astype(bf16)

    lane = lax.broadcasted_iota(jnp.int32, (con_dev, 128), 1)
    index = pos_idx[:, None]
    meta = jnp.where(lane == 0, index // 64, jnp.where(lane == 1, index % 64, live_count[0]))
    own = jnp.concatenate([signal, meta.astype(bf16)], axis=1)

    def absorbed(messages, base, state, last=False):
        return absorb(messages, base, queries, w_in, w_kv, pos_table, state, last)

    cot = cotangent.reshape(pat_dev * lat_dev, width)
    cot_left = lax.ppermute(cot[lat_dev:], "tm", up1)
    cot_right = lax.ppermute(cot[: 3 * lat_dev], "tm", down1)

    below, above = own, own
    at_hand, base, state = [own], 0, None
    for step in range(1, NZ // 2 + 1):
        below = lax.ppermute(below, "z", shift(NZ, 1))
        if step < NZ // 2:
            above = lax.ppermute(above, "z", shift(NZ, -1))
        state = list(absorbed(at_hand, base, state))
        base += len(at_hand)
        if step == 2:
            below, above, state[1], cot_left, cot_right = lax.optimization_barrier(
                (below, above, state[1], cot_left, cot_right)
            )
        elif step < NZ // 2:
            below, above, state[1] = lax.optimization_barrier((below, above, state[1]))
        at_hand = [below, above] if step < NZ // 2 else [below]
    kv, valid, *parts = absorbed(at_hand, base, state, last=True)

    received = [lax.ppermute(parts[s], "y", shift(NY, -s)) for s in range(1, NY)]
    att, stats = combine([parts[0]] + received)

    partner = lax.ppermute(att, "tm", swap)
    chip = jnp.where(tm % 2 == 0, jnp.concatenate([att, partner]), jnp.concatenate([partner, att]))
    left = lax.ppermute(chip[2 * lat_dev :], "tm", up2)
    right = lax.ppermute(chip[: 6 * lat_dev], "tm", down2)
    features, msg = conv_stack(
        tm.reshape(1), (left, partner, right), att, stats,
        (cot_left, cot, cot_right), w_out, conv_weight, conv_bias,
    )

    msg = msg.reshape(pat_dev, lat_dev, width + 128)
    msgs = [msg] + [lax.ppermute(msg, "y", shift(NY, s)) for s in range(1, NY)]
    dq = backward_attention(y.reshape(1), kv, valid, queries, msgs)

    pieces = lax.all_to_all(dq, ("y", "tm"), 0, 0, tiled=True)
    dq_row = jnp.sum(pieces, axis=0, keepdims=True).astype(bf16)
    copies = jnp.broadcast_to(dq_row.reshape(1, width // 128, 128), (lat_rows, width // 128, 128))
    dq_all = lax.all_to_all(copies, ("y", "z", "tm"), 0, 0, tiled=True)
    d_latents = nt_dot(dq_all.reshape(lat_rows, width), w_query)
    return features.reshape(pat_dev, lat_dev, width), d_latents


def solution(mesh):
    split = Mesh(mesh.devices.reshape(NY, NZ, NTM), ("y", "z", "tm"))
    contacts = ("y", "z")
    in_specs = (P(contacts, "tm"), P(contacts), P(contacts)) + (P(),) * 8 + (P("tm", contacts, None),)
    out_specs = (P("tm", contacts, None), P())
    return jax.shard_map(local, mesh=split, in_specs=in_specs, out_specs=out_specs, check_vma=False)
```

```python
import functools

import jax
import jax.numpy as jnp
from jax import lax
from jax.experimental import pallas as pl
from jax.experimental.pallas import tpu as pltpu
from jax.sharding import Mesh
from jax.sharding import PartitionSpec as P

HD = 64
PATCH = 32
KSIZE = 3
LAYERS = 2

neg_big = -1e30
scale_dot = 0.125

bf16 = jnp.bfloat16
f32 = jnp.float32

NY, NZ, NTM = 4, 8, 8
MIB = 1 << 20
PIECE, PARTS, HALVES, VMEM_ABSORB = 2048, 2, 2, 28
WUNROLL, VMEM_BACK = 4, 40


def nt_dot(a, b):
    return lax.dot_general(a, b, (((1,), (1,)), ((), ())), preferred_element_type=f32)


def nn_dot(a, b):
    return jnp.dot(a, b, preferred_element_type=f32)


def head_of_lane(shape):
    return lax.broadcasted_iota(jnp.int32, shape, len(shape) - 1) // HD


def spread_heads(rows, heads):
    head = head_of_lane(rows.shape)
    zero = jnp.zeros_like(rows)
    return jnp.concatenate([jnp.where(head == h, rows, zero) for h in range(heads)], axis=0)


def collect_heads(blocks, heads):
    r = blocks.shape[0] // heads
    head = head_of_lane((r, blocks.shape[1]))
    out = blocks[:r]
    for h in range(1, heads):
        out = jnp.where(head == h, blocks[h * r : (h + 1) * r], out)
    return out


def columns_to_lanes(column, heads, first, base):
    r = base.shape[0]
    lane = lax.broadcasted_iota(jnp.int32, base.shape, 1)
    for h in range(heads):
        base = jnp.where(lane == first + h, column[h * r : (h + 1) * r], base)
    return base


def lanes_to_column(stats, heads, first):
    return jnp.concatenate([stats[:, first + h : first + h + 1] for h in range(heads)], axis=0)


def lanes_to_columns_wide(stats, heads, first):
    r = stats.shape[0]
    head = head_of_lane((r, heads * HD))
    out = jnp.broadcast_to(stats[:, first : first + 1], (r, heads * HD))
    for h in range(1, heads):
        out = jnp.where(head == h, stats[:, first + h : first + h + 1], out)
    return out


def silu_slope(pre_act):
    sigmoid_v = jax.nn.sigmoid(pre_act)
    return sigmoid_v * (1.0 + pre_act * (1.0 - sigmoid_v))


def rounded(value):
    return value.astype(bf16).astype(f32)


def absorb_kernel(*refs, fresh, last, count):
    refs = list(refs)
    messages = [refs.pop(0) for _ in range(count)]
    q_ref, w_in_ref, w_kv_ref, table_ref = (refs.pop(0) for _ in range(4))
    if not fresh:
        acc_in, stat_in = refs.pop(0), refs.pop(0)
    kv_hbm, valid_ref = refs.pop(0), refs.pop(0)
    if last:
        part_refs = [refs.pop(0) for _ in range(NY)]
    else:
        acc_out, stat_out = refs.pop(0), refs.pop(0)
    pos_ref, tok_ref, kv_ref, sem = refs
    width = q_ref.shape[1]
    heads = width // HD
    con_dev, span = messages[0].shape[0], messages[0].shape[1] - 128
    windows = span // PATCH
    rows = count * con_dev
    message = jnp.concatenate([m[...] for m in messages], axis=0)
    sig = message[:, :span]
    meta = message[:, span:].astype(f32)
    idx = meta[:, 0:1] * 64.0 + meta[:, 1:2]
    lane = lax.broadcasted_iota(jnp.int32, (1, con_dev), 1).astype(f32)
    valid = jnp.concatenate(
        [jnp.where(lane < meta[c * con_dev : c * con_dev + 1, 2:3], 1.0, 0.0) for c in range(count)], axis=1
    )
    valid_ref[...] = jnp.broadcast_to(valid, valid_ref.shape)
    piece = PIECE
    ids = lax.broadcasted_iota(jnp.int32, (rows, piece), 1).astype(f32)
    pos_ref[...] = jnp.zeros_like(pos_ref)

    @pl.loop(0, table_ref.shape[0] // piece)
    def _(k):
        start = pl.multiple_of(k * piece, piece)
        hot = jnp.where(ids == idx - start.astype(f32), 1.0, 0.0).astype(bf16)
        pos_ref[...] = pos_ref[...] + nn_dot(hot, table_ref[pl.ds(start, piece), :])

    tall = jnp.concatenate([w_in_ref[...]] * windows, axis=0)
    band = lax.broadcasted_iota(jnp.int32, sig.shape, 1) // PATCH
    for w in range(windows):
        embedded = nn_dot(jnp.where(band == w, sig, jnp.zeros_like(sig)), tall)
        tok_ref[w * rows : (w + 1) * rows, :] = (embedded + pos_ref[...]).astype(bf16)
    copies = []
    for part in range(PARTS):
        ws = windows // PARTS
        tokens = tok_ref[part * ws * rows : (part + 1) * ws * rows, :]
        for half in range(HALVES):
            cols = slice(half * 2 * width // HALVES, (half + 1) * 2 * width // HALVES)
            keyval = nn_dot(tokens, w_kv_ref[:, cols]).astype(bf16)
            kv_ref[part * ws : (part + 1) * ws, :, cols] = keyval.reshape(ws, rows, 2 * width // HALVES)
        copies.append(
            pltpu.make_async_copy(
                kv_ref.at[pl.ds(part * ws, ws)],
                kv_hbm.at[pl.ds(part * ws, ws)],
                sem.at[part],
            )
        )
        copies[-1].start()
    q_wide = spread_heads(q_ref[...], heads)

    def one_window(w):
        scores = nt_dot(q_wide, kv_ref[w, :, :width]) * scale_dot
        scores = jnp.where(valid > 0.0, scores, neg_big)
        top = jnp.max(scores, axis=1, keepdims=True)
        if not fresh:
            before, total_before = stat_in[w, :, 0:1], stat_in[w, :, 1:2]
            top = jnp.maximum(top, before)
        weights = jnp.exp(scores - top)
        totals = jnp.sum(weights, axis=1, keepdims=True)
        accum = nn_dot(weights.astype(bf16), kv_ref[w, :, width:])
        if not fresh:
            fade = jnp.exp(before - top)
            totals = totals + total_before * fade
            accum = accum + acc_in[w] * fade
        if not last:
            acc_out[w] = accum
            stat_out[w, :, 0:1] = top
            stat_out[w, :, 1:2] = totals
        else:
            mixed = collect_heads(accum, heads)
            stats = jnp.zeros((mixed.shape[0], 128), f32)
            stats = columns_to_lanes(top, heads, 0, stats)
            stats = columns_to_lanes(totals, heads, heads, stats)
            each = mixed.shape[0] // NY
            for s, part_ref in enumerate(part_refs):
                part_ref[w, :, :width] = mixed[s * each : (s + 1) * each]
                part_ref[w, :, width:] = stats[s * each : (s + 1) * each]

    together = WUNROLL // count

    @pl.loop(0, windows // together)
    def _(k):
        for part in range(together):
            one_window(k * together + part)

    for copy in copies:
        copy.wait()


def absorb(messages, q, w_in, w_kv, table, state, last):
    count = len(messages)
    lat, width = q.shape
    con_dev = messages[0].shape[0]
    windows = (messages[0].shape[1] - 128) // PATCH
    rows = lat * (width // HD)
    fresh = state is None
    vmem = pl.BlockSpec(memory_space=pltpu.VMEM)
    hbm = pl.BlockSpec(memory_space=pltpu.HBM)
    operands = list(messages) + [q, w_in, w_kv, table]
    in_specs = [vmem] * len(operands)
    aliases = {}
    if not fresh:
        n = len(operands)
        operands += list(state)
        in_specs += [vmem, vmem]
        aliases = {} if last else {n: 2, n + 1: 3}
    acc = jax.ShapeDtypeStruct((windows, rows, width), f32)
    stat = jax.ShapeDtypeStruct((windows, rows, 128), f32)
    part = jax.ShapeDtypeStruct((windows, lat // NY, width + 128), f32)
    tail = [part] * NY if last else [acc, stat]
    return pl.pallas_call(
        functools.partial(absorb_kernel, fresh=fresh, last=last, count=count),
        in_specs=in_specs,
        out_specs=[hbm, vmem] + [vmem] * len(tail),
        out_shape=[
            pltpu.HBM((windows, count * con_dev, 2 * width), bf16),
            jax.ShapeDtypeStruct((8, count * con_dev), f32),
        ]
        + tail,
        scratch_shapes=[
            pltpu.VMEM((count * con_dev, width), f32),
            pltpu.VMEM((windows * count * con_dev, width), bf16),
            pltpu.VMEM((windows, count * con_dev, 2 * width), bf16),
            pltpu.SemaphoreType.DMA((PARTS,)),
        ],
        input_output_aliases=aliases,
        compiler_params=pltpu.CompilerParams(vmem_limit_bytes=VMEM_ABSORB * MIB),
        name="absorb",
    )(*operands)


def combine_kernel(*refs):
    *part_refs, att_ref, stats_ref = refs
    rows, width = att_ref.shape
    heads = width // HD
    lane = lax.broadcasted_iota(jnp.int32, (rows, 128), 1)
    parts = [ref[...].reshape(rows, width + 128) for ref in part_refs]
    top = parts[0][:, width:]
    for part in parts[1:]:
        top = jnp.maximum(top, part[:, width:])
    totals = jnp.zeros((rows, 128), f32)
    accum = jnp.zeros((rows, width), f32)
    for part in parts:
        factor = jnp.exp(jnp.where(lane < heads, part[:, width:] - top, 0.0))
        totals = totals + factor * pltpu.roll(part[:, width:], 128 - heads, 1)
        accum = accum + part[:, :width] * lanes_to_columns_wide(factor, heads, 0)
    totals = jnp.where(lane < heads, totals, 1.0)
    att_ref[...] = (accum / lanes_to_columns_wide(totals, heads, 0)).astype(bf16)
    stats_ref[...] = jnp.where(lane < heads, top, pltpu.roll(1.0 / totals, heads, 1))


def combine(parts):
    windows, each, wide = parts[0].shape
    rows = windows * each
    return pl.pallas_call(
        combine_kernel,
        out_shape=[
            jax.ShapeDtypeStruct((rows, wide - 128), bf16),
            jax.ShapeDtypeStruct((rows, 128), f32),
        ],
        compiler_params=pltpu.CompilerParams(vmem_limit_bytes=8 * MIB),
        name="combine_parts",
    )(*parts)


def conv_kernel(
    tm_ref, left_ref, own_ref, partner_ref, right_ref, stats_ref, cl_ref, cot_ref, cr_ref,
    w_out_ref, conv_hbm, bias_ref, feat_ref, msg_ref, ext_ref, conv_ref, sem,
):
    weights = [pltpu.make_async_copy(conv_hbm.at[l], conv_ref.at[l], sem.at[l]) for l in range(LAYERS)]
    for copy in weights:
        copy.start()
    rows, width = own_ref.shape
    heads = width // HD
    windows = 4
    each = rows // windows
    reach = 6
    first = tm_ref[0] * windows - reach
    total_windows = NTM * windows

    def inside(lo, count):
        w = lax.broadcasted_iota(jnp.int32, (count * each, width), 0) // each + (first + lo)
        return jnp.logical_and(w >= 0, w < total_windows)

    core = tm_ref[0] % 2
    side = reach * each
    ext_ref[:side, :] = left_ref[...].astype(f32)
    ext_ref[pl.ds(pl.multiple_of(side + core * rows, each), rows), :] = own_ref[...].astype(f32)
    ext_ref[pl.ds(pl.multiple_of(side + (1 - core) * rows, each), rows), :] = partner_ref[...].astype(f32)
    ext_ref[side + 2 * rows :, :] = right_ref[...].astype(f32)
    att = ext_ref[pl.ds(pl.multiple_of(core * rows, each), 2 * side + rows), :]
    w_out = w_out_ref[...]
    x0 = rounded(nn_dot(att.astype(bf16), w_out))
    n0 = 14 * each
    weights[0].wait()
    pre0 = bias_ref[0:1, :] + sum(nn_dot(x0[j * each : j * each + n0].astype(bf16), conv_ref[0, j]) for j in range(KSIZE))
    x1 = rounded(x0[each : each + n0] + jax.nn.silu(pre0))
    x1 = jnp.where(inside(1, 14), x1, 0.0)
    n1 = 10 * each
    weights[1].wait()
    pre1 = bias_ref[1:2, :] + sum(nn_dot(x1[2 * j * each : 2 * j * each + n1].astype(bf16), conv_ref[1, j]) for j in range(KSIZE))
    feat_ref[...] = (x1[5 * each : 9 * each] + jax.nn.silu(pre1[3 * each : 7 * each])).astype(bf16)
    g2 = jnp.concatenate([r[...].astype(f32) for r in (cl_ref, cot_ref, cr_ref)], axis=0)
    gpre1 = rounded(g2 * silu_slope(pre1))
    n2 = 6 * each
    g1 = g2[2 * each : 8 * each] + sum(
        nt_dot(gpre1[(4 - 2 * j) * each : (4 - 2 * j) * each + n2].astype(bf16), conv_ref[1, j]) for j in range(KSIZE)
    )
    gpre0 = rounded(g1 * silu_slope(pre0[4 * each : 10 * each]))
    gpre0 = jnp.where(inside(5, 6), gpre0, 0.0)
    g0 = g1[each : 5 * each] + sum(
        nt_dot(gpre0[(2 - j) * each : (2 - j) * each + rows].astype(bf16), conv_ref[0, j]) for j in range(KSIZE)
    )
    grad_att = rounded(nt_dot(g0.astype(bf16), w_out))
    msg_ref[:, :width] = grad_att.astype(bf16)
    product = grad_att * own_ref[...].astype(f32)
    head = head_of_lane((rows, width))
    lane = lax.broadcasted_iota(jnp.int32, (rows, 128), 1)
    stats = stats_ref[...]
    for h in range(heads):
        delta = jnp.sum(jnp.where(head == h, product, 0.0), axis=1, keepdims=True)
        stats = jnp.where(lane == 2 * heads + h, delta, stats)
    stats = jnp.where(lane < 3 * heads, stats, 0.0)
    high = rounded(stats)
    middle = rounded(stats - high)
    low = (stats - high) - middle
    msg_ref[:, width:] = (high + pltpu.roll(middle, 32, 1) + pltpu.roll(low, 64, 1)).astype(bf16)


def conv_stack(tm, halo, own, stats, cots, w_out, conv_weight, conv_bias):
    rows, width = own.shape
    left, partner, right = halo
    cl, cot, cr = cots
    vmem = pl.BlockSpec(memory_space=pltpu.VMEM)
    return pl.pallas_call(
        conv_kernel,
        in_specs=[pl.BlockSpec(memory_space=pltpu.SMEM)] + [vmem] * 9 + [pl.BlockSpec(memory_space=pltpu.HBM), vmem],
        out_specs=[vmem, vmem],
        out_shape=[
            jax.ShapeDtypeStruct((rows, width), bf16),
            jax.ShapeDtypeStruct((rows, width + 128), bf16),
        ],
        scratch_shapes=[
            pltpu.VMEM((left.shape[0] + 2 * rows + right.shape[0], width), f32),
            pltpu.VMEM(conv_weight.shape, conv_weight.dtype),
            pltpu.SemaphoreType.DMA((LAYERS,)),
        ],
        compiler_params=pltpu.CompilerParams(vmem_limit_bytes=24 * MIB),
        name="conv_stack",
    )(tm, left, own, partner, right, stats, cl, cot, cr, w_out, pltpu.with_memory_space_constraint(conv_weight, pltpu.HBM), conv_bias)


def backward_kernel(y_ref, q_ref, *refs, slots):
    *refs, dq_ref, acc_ref = refs
    msg_refs, refs = refs[:slots], refs[slots:]
    kv_refs, valid_refs = refs[: len(refs) // 2], refs[len(refs) // 2 :]
    width = q_ref.shape[1]
    heads = width // HD
    window = pl.program_id(0)
    msg = jnp.concatenate([r[0].astype(f32) for r in msg_refs], axis=0)
    terms = msg[:, width:]
    stats = terms + pltpu.roll(terms, 96, 1) + pltpu.roll(terms, 64, 1)
    top = lanes_to_column(stats, heads, 0)
    inverse = lanes_to_column(stats, heads, heads)
    delta = lanes_to_column(stats, heads, 2 * heads)
    grad_wide = spread_heads(msg[:, :width].astype(bf16), heads)
    q_wide = spread_heads(q_ref[...], heads)

    @pl.when(window == 0)
    def _():
        acc_ref[...] = jnp.zeros_like(acc_ref)

    accum = acc_ref[...]
    for kv_ref, valid_ref in zip(kv_refs, valid_refs):
        key_rows = kv_ref[0, :, :width]
        scores = nt_dot(q_wide, key_rows) * scale_dot
        scores = jnp.where(valid_ref[0:1, :] > 0.0, scores, neg_big)
        prob = jnp.exp(scores - top) * inverse
        grad_prob = nt_dot(grad_wide, kv_ref[0, :, width:])
        dscore = (prob * (grad_prob - delta)).astype(bf16)
        accum = accum + nn_dot(dscore, key_rows)
    acc_ref[...] = accum

    @pl.when(window == pl.num_programs(0) - 1)
    def _():
        dq = collect_heads(acc_ref[...], heads) * scale_dot
        each = dq.shape[0] // slots
        for s in range(slots):
            place = pl.multiple_of(((y_ref[0] + (slots - s)) % slots) * each, each)
            dq_ref[pl.ds(place, each), :] = dq[s * each : (s + 1) * each]


def backward_attention(y, kvs, valids, q, msgs):
    windows = kvs[0].shape[0]
    lat, width = q.shape
    heads = width // HD
    whole = lambda a: pl.BlockSpec(a.shape, lambda p: (0,) * a.ndim, pipeline_mode=pl.Buffered(1))
    kvs = [pltpu.with_memory_space_constraint(kv, pltpu.HBM) for kv in kvs]
    each_window = lambda a: pl.BlockSpec((1,) + a.shape[1:], lambda p: (p, 0, 0))
    return pl.pallas_call(
        functools.partial(backward_kernel, slots=len(msgs)),
        grid=(windows,),
        in_specs=[pl.BlockSpec(memory_space=pltpu.SMEM), whole(q)]
        + [each_window(a) for a in (*msgs, *kvs)]
        + [whole(v) for v in valids],
        out_specs=pl.BlockSpec((lat, width), lambda p: (0, 0)),
        out_shape=jax.ShapeDtypeStruct((lat, width), f32),
        scratch_shapes=[pltpu.VMEM((lat * heads, width), f32)],
        compiler_params=pltpu.CompilerParams(vmem_limit_bytes=VMEM_BACK * MIB),
        name="backward_attention",
    )(y, q, *msgs, *kvs, *valids)


def shift(count, by):
    return [(i, (i + by) % count) for i in range(count)]


def local(
    signal, pos_idx, live_count, latents, pos_table, w_in, w_kv, w_query, w_out,
    conv_weight, conv_bias, cotangent,
):
    con_dev = signal.shape[0]
    pat_dev = signal.shape[1] // PATCH
    width = w_query.shape[0]
    lat_rows = latents.shape[0]
    y, z, tm = (lax.axis_index(a) for a in ("y", "z", "tm"))
    lat_dev = lat_rows // (NY * NZ)
    up1 = [(i, i + 1) for i in range(NTM - 1)]
    down1 = [(i + 1, i) for i in range(NTM - 1)]
    up2 = [(i, i + 2) for i in range(NTM - 2)]
    down2 = [(i + 2, i) for i in range(NTM - 2)]
    swap = [(i, i ^ 1) for i in range(NTM)]

    by_owner = latents.reshape(NY, NZ, lat_dev, width)
    mine = lax.dynamic_index_in_dim(by_owner, z, 1, False)
    slots = jnp.stack([lax.dynamic_index_in_dim(mine, (y + NY - s) % NY, 0, False) for s in range(NY)])
    queries = nn_dot(slots.reshape(NY * lat_dev, width), w_query).astype(bf16)

    lane = lax.broadcasted_iota(jnp.int32, (con_dev, 128), 1)
    index = pos_idx[:, None]
    meta = jnp.where(lane == 0, index // 64, jnp.where(lane == 1, index % 64, live_count[0]))
    own = jnp.concatenate([signal, meta.astype(bf16)], axis=1)

    def absorbed(messages, state, last=False):
        return absorb(messages, queries, w_in, w_kv, pos_table, state, last)

    cot = cotangent.reshape(pat_dev * lat_dev, width)
    cot_left = lax.ppermute(cot[lat_dev:], "tm", up1)
    cot_right = lax.ppermute(cot[: 3 * lat_dev], "tm", down1)

    below, above = own, own
    at_hand, state, kvs, valids = [own], None, [], []
    for step in range(1, NZ // 2 + 1):
        below = lax.ppermute(below, "z", shift(NZ, 1))
        if step < NZ // 2:
            above = lax.ppermute(above, "z", shift(NZ, -1))
        kv, valid, *state = absorbed(at_hand, state)
        kvs.append(kv)
        valids.append(valid)
        if step == 2:
            below, above, valids[-1], cot_left, cot_right = lax.optimization_barrier(
                (below, above, valids[-1], cot_left, cot_right)
            )
        elif step < NZ // 2:
            below, above, valids[-1] = lax.optimization_barrier((below, above, valids[-1]))
        at_hand = [below, above] if step < NZ // 2 else [below]
    kv, valid, *parts = absorbed(at_hand, state, last=True)
    kvs.append(kv)
    valids.append(valid)

    received = [lax.ppermute(parts[s], "y", shift(NY, -s)) for s in range(1, NY)]
    att, stats = combine([parts[0]] + received)

    partner = lax.ppermute(att, "tm", swap)
    chip = jnp.where(tm % 2 == 0, jnp.concatenate([att, partner]), jnp.concatenate([partner, att]))
    left = lax.ppermute(chip[2 * lat_dev :], "tm", up2)
    right = lax.ppermute(chip[: 6 * lat_dev], "tm", down2)
    features, msg = conv_stack(
        tm.reshape(1), (left, partner, right), att, stats,
        (cot_left, cot, cot_right), w_out, conv_weight, conv_bias,
    )

    msg = msg.reshape(pat_dev, lat_dev, width + 128)
    msgs = [msg] + [lax.ppermute(msg, "y", shift(NY, s)) for s in range(1, NY)]
    dq = backward_attention(y.reshape(1), kvs, valids, queries, msgs)

    pieces = lax.all_to_all(dq, ("y", "tm"), 0, 0, tiled=True)
    dq_row = jnp.sum(pieces, axis=0, keepdims=True).astype(bf16)
    copies = jnp.broadcast_to(dq_row.reshape(1, width // 128, 128), (lat_rows, width // 128, 128))
    dq_all = lax.all_to_all(copies, ("y", "z", "tm"), 0, 0, tiled=True)
    d_latents = nt_dot(dq_all.reshape(lat_rows, width), w_query)
    return features.reshape(pat_dev, lat_dev, width), d_latents


def solution(mesh):
    split = Mesh(mesh.devices.reshape(NY, NZ, NTM), ("y", "z", "tm"))
    contacts = ("y", "z")
    in_specs = (P(contacts, "tm"), P(contacts), P(contacts)) + (P(),) * 8 + (P("tm", contacts, None),)
    out_specs = (P("tm", contacts, None), P())
    return jax.shard_map(local, mesh=split, in_specs=in_specs, out_specs=out_specs, check_vma=False)
```

```python
import functools

import jax
import jax.numpy as jnp
from jax import lax
from jax.experimental import pallas as pl
from jax.experimental.pallas import tpu as pltpu
from jax.sharding import Mesh
from jax.sharding import PartitionSpec as P

HD = 64
PATCH = 32
KSIZE = 3
LAYERS = 2

neg_big = -1e30
scale_dot = 0.125

bf16 = jnp.bfloat16
f32 = jnp.float32

NY, NZ, NTM = 4, 8, 8
MIB = 1 << 20
PIECE, PARTS, HALVES, VMEM_ABSORB = 2048, 2, 2, 28
WUNROLL, VMEM_BACK = 4, 40


def nt_dot(a, b):
    return lax.dot_general(a, b, (((1,), (1,)), ((), ())), preferred_element_type=f32)


def nn_dot(a, b):
    return jnp.dot(a, b, preferred_element_type=f32)


def head_of_lane(shape):
    return lax.broadcasted_iota(jnp.int32, shape, len(shape) - 1) // HD


def spread_heads(rows, heads):
    head = head_of_lane(rows.shape)
    zero = jnp.zeros_like(rows)
    return jnp.concatenate([jnp.where(head == h, rows, zero) for h in range(heads)], axis=0)


def collect_heads(blocks, heads):
    r = blocks.shape[0] // heads
    head = head_of_lane((r, blocks.shape[1]))
    out = blocks[:r]
    for h in range(1, heads):
        out = jnp.where(head == h, blocks[h * r : (h + 1) * r], out)
    return out


def columns_to_lanes(column, heads, first, base):
    r = base.shape[0]
    lane = lax.broadcasted_iota(jnp.int32, base.shape, 1)
    for h in range(heads):
        base = jnp.where(lane == first + h, column[h * r : (h + 1) * r], base)
    return base


def lanes_to_column(stats, heads, first):
    return jnp.concatenate([stats[:, first + h : first + h + 1] for h in range(heads)], axis=0)


def lanes_to_columns_wide(stats, heads, first):
    r = stats.shape[0]
    head = head_of_lane((r, heads * HD))
    out = jnp.broadcast_to(stats[:, first : first + 1], (r, heads * HD))
    for h in range(1, heads):
        out = jnp.where(head == h, stats[:, first + h : first + h + 1], out)
    return out


def silu_slope(pre_act):
    sigmoid_v = jax.nn.sigmoid(pre_act)
    return sigmoid_v * (1.0 + pre_act * (1.0 - sigmoid_v))


def rounded(value):
    return value.astype(bf16).astype(f32)


def absorb_kernel(*refs, fresh, last, count):
    refs = list(refs)
    messages = [refs.pop(0) for _ in range(count)]
    q_ref, w_in_ref, w_kv_ref, table_ref = (refs.pop(0) for _ in range(4))
    if not fresh:
        acc_in, stat_in = refs.pop(0), refs.pop(0)
    kv_hbm, valid_ref = refs.pop(0), refs.pop(0)
    if last:
        part_refs = [refs.pop(0) for _ in range(NY)]
    else:
        acc_out, stat_out = refs.pop(0), refs.pop(0)
    pos_ref, tok_ref, kv_ref, sem = refs
    width = q_ref.shape[1]
    heads = width // HD
    con_dev, span = messages[0].shape[0], messages[0].shape[1] - 128
    windows = span // PATCH
    rows = count * con_dev
    message = jnp.concatenate([m[...] for m in messages], axis=0)
    sig = message[:, :span]
    meta = message[:, span:].astype(f32)
    idx = meta[:, 0:1] * 64.0 + meta[:, 1:2]
    lane = lax.broadcasted_iota(jnp.int32, (1, con_dev), 1).astype(f32)
    valid = jnp.concatenate(
        [jnp.where(lane < meta[c * con_dev : c * con_dev + 1, 2:3], 1.0, 0.0) for c in range(count)], axis=1
    )
    valid_ref[...] = jnp.broadcast_to(valid, valid_ref.shape)
    piece = PIECE
    ids = lax.broadcasted_iota(jnp.int32, (rows, piece), 1).astype(f32)
    pos_ref[...] = jnp.zeros_like(pos_ref)

    @pl.loop(0, table_ref.shape[0] // piece)
    def _(k):
        start = pl.multiple_of(k * piece, piece)
        hot = jnp.where(ids == idx - start.astype(f32), 1.0, 0.0).astype(bf16)
        pos_ref[...] = pos_ref[...] + nn_dot(hot, table_ref[pl.ds(start, piece), :])

    tall = jnp.concatenate([w_in_ref[...]] * windows, axis=0)
    band = lax.broadcasted_iota(jnp.int32, sig.shape, 1) // PATCH
    for w in range(windows):
        embedded = nn_dot(jnp.where(band == w, sig, jnp.zeros_like(sig)), tall)
        tok_ref[w * rows : (w + 1) * rows, :] = (embedded + pos_ref[...]).astype(bf16)
    copies = []
    ws = windows // PARTS
    for part in range(PARTS):
        tokens = tok_ref[part * ws * rows : (part + 1) * ws * rows, :]
        for half in range(HALVES):
            cols = slice(half * 2 * width // HALVES, (half + 1) * 2 * width // HALVES)
            keyval = nn_dot(tokens, w_kv_ref[:, cols]).astype(bf16)
            kv_ref[part * ws : (part + 1) * ws, :, cols] = keyval.reshape(ws, rows, 2 * width // HALVES)
        here = pl.ds(part * ws, ws)
        copies.append(pltpu.make_async_copy(kv_ref.at[here], kv_hbm.at[here], sem.at[part]))
        copies[-1].start()
    q_wide = spread_heads(q_ref[...], heads)

    def one_window(w):
        scores = nt_dot(q_wide, kv_ref[w, :, :width]) * scale_dot
        scores = jnp.where(valid > 0.0, scores, neg_big)
        top = jnp.max(scores, axis=1, keepdims=True)
        if not fresh:
            before, total_before = stat_in[w, :, 0:1], stat_in[w, :, 1:2]
            top = jnp.maximum(top, before)
        weights = jnp.exp(scores - top)
        totals = jnp.sum(weights, axis=1, keepdims=True)
        accum = nn_dot(weights.astype(bf16), kv_ref[w, :, width:])
        if not fresh:
            fade = jnp.exp(before - top)
            totals = totals + total_before * fade
            accum = accum + acc_in[w] * fade
        if not last:
            acc_out[w] = accum
            stat_out[w, :, 0:1] = top
            stat_out[w, :, 1:2] = totals
        else:
            mixed = collect_heads(accum, heads)
            stats = jnp.zeros((mixed.shape[0], 128), f32)
            stats = columns_to_lanes(top, heads, 0, stats)
            stats = columns_to_lanes(totals, heads, heads, stats)
            each = mixed.shape[0] // NY
            for s, part_ref in enumerate(part_refs):
                part_ref[w, :, :width] = mixed[s * each : (s + 1) * each]
                part_ref[w, :, width:] = stats[s * each : (s + 1) * each]

    together = WUNROLL // count

    @pl.loop(0, windows // together)
    def _(k):
        for part in range(together):
            one_window(k * together + part)

    for copy in copies:
        copy.wait()


def absorb(messages, q, w_in, w_kv, table, state, last):
    count = len(messages)
    lat, width = q.shape
    con_dev = messages[0].shape[0]
    windows = (messages[0].shape[1] - 128) // PATCH
    rows = lat * (width // HD)
    fresh = state is None
    vmem = pl.BlockSpec(memory_space=pltpu.VMEM)
    operands = list(messages) + [q, w_in, w_kv, table]
    in_specs = [vmem] * len(operands)
    aliases = {}
    if not fresh:
        n = len(operands)
        operands += list(state)
        in_specs += [vmem, vmem]
        aliases = {} if last else {n: 2, n + 1: 3}
    acc = jax.ShapeDtypeStruct((windows, rows, width), f32)
    stat = jax.ShapeDtypeStruct((windows, rows, 128), f32)
    part = jax.ShapeDtypeStruct((windows, lat // NY, width + 128), f32)
    tail = [part] * NY if last else [acc, stat]
    return pl.pallas_call(
        functools.partial(absorb_kernel, fresh=fresh, last=last, count=count),
        in_specs=in_specs,
        out_specs=[pl.BlockSpec(memory_space=pltpu.HBM)] + [vmem] * (1 + len(tail)),
        out_shape=[
            pltpu.HBM((windows, count * con_dev, 2 * width), bf16),
            jax.ShapeDtypeStruct((8, count * con_dev), f32),
        ]
        + tail,
        scratch_shapes=[
            pltpu.VMEM((count * con_dev, width), f32),
            pltpu.VMEM((windows * count * con_dev, width), bf16),
            pltpu.VMEM((windows, count * con_dev, 2 * width), bf16),
            pltpu.SemaphoreType.DMA((PARTS,)),
        ],
        input_output_aliases=aliases,
        compiler_params=pltpu.CompilerParams(vmem_limit_bytes=VMEM_ABSORB * MIB),
        name="absorb",
    )(*operands)


def combine_kernel(*refs):
    *part_refs, att_ref, stats_ref = refs
    rows, width = att_ref.shape
    heads = width // HD
    lane = lax.broadcasted_iota(jnp.int32, (rows, 128), 1)
    parts = [ref[...].reshape(rows, width + 128) for ref in part_refs]
    top = parts[0][:, width:]
    for part in parts[1:]:
        top = jnp.maximum(top, part[:, width:])
    totals = jnp.zeros((rows, 128), f32)
    accum = jnp.zeros((rows, width), f32)
    for part in parts:
        factor = jnp.exp(jnp.where(lane < heads, part[:, width:] - top, 0.0))
        totals = totals + factor * pltpu.roll(part[:, width:], 128 - heads, 1)
        accum = accum + part[:, :width] * lanes_to_columns_wide(factor, heads, 0)
    totals = jnp.where(lane < heads, totals, 1.0)
    att_ref[...] = (accum / lanes_to_columns_wide(totals, heads, 0)).astype(bf16)
    stats_ref[...] = jnp.where(lane < heads, top, pltpu.roll(1.0 / totals, heads, 1))


def combine(parts):
    windows, each, wide = parts[0].shape
    rows = windows * each
    return pl.pallas_call(
        combine_kernel,
        out_shape=[
            jax.ShapeDtypeStruct((rows, wide - 128), bf16),
            jax.ShapeDtypeStruct((rows, 128), f32),
        ],
        compiler_params=pltpu.CompilerParams(vmem_limit_bytes=8 * MIB),
        name="combine_parts",
    )(*parts)


def conv_kernel(
    tm_ref, own_ref, all_ref, stats_ref, cl_ref, cot_ref, cr_ref,
    w_out_ref, bias_ref, conv_hbm, *refs,
):
    n = (len(refs) - 6) // 2
    kv_hbms, (feat_ref, msg_ref), kv_refs = refs[:n], refs[n : n + 2], refs[n + 2 : 2 * n + 2]
    ext_ref, conv_ref, sem, kv_sem = refs[2 * n + 2 :]
    fetches = [pltpu.make_async_copy(kv_hbms[i].at[0], kv_refs[i], kv_sem.at[i]) for i in range(n)]
    weights = [pltpu.make_async_copy(conv_hbm.at[l], conv_ref.at[l], sem.at[l]) for l in range(LAYERS)]
    for copy in weights:
        copy.start()
    for copy in fetches:
        copy.start()
    rows, width = own_ref.shape
    heads = width // HD
    windows = 4
    each = rows // windows
    reach = 6
    first = tm_ref[0] * windows - reach
    total_windows = NTM * windows

    def inside(lo, count):
        w = lax.broadcasted_iota(jnp.int32, (count * each, width), 0) // each + (first + lo)
        return jnp.logical_and(w >= 0, w < total_windows)

    side = reach * each
    ext_ref[:side, :] = jnp.zeros((side, width), f32)
    ext_ref[side : side + NTM * rows, :] = all_ref[...].astype(f32)
    ext_ref[side + NTM * rows :, :] = jnp.zeros((side, width), f32)
    att = ext_ref[pl.ds(pl.multiple_of(tm_ref[0] * rows, rows), 2 * side + rows), :]
    w_out = w_out_ref[...]
    x0 = rounded(nn_dot(att.astype(bf16), w_out))
    n0 = 14 * each
    weights[0].wait()
    pre0 = bias_ref[0:1, :] + sum(nn_dot(x0[j * each : j * each + n0].astype(bf16), conv_ref[0, j]) for j in range(KSIZE))
    x1 = rounded(x0[each : each + n0] + jax.nn.silu(pre0))
    x1 = jnp.where(inside(1, 14), x1, 0.0)
    n1 = 10 * each
    weights[1].wait()
    pre1 = bias_ref[1:2, :] + sum(nn_dot(x1[2 * j * each : 2 * j * each + n1].astype(bf16), conv_ref[1, j]) for j in range(KSIZE))
    feat_ref[...] = (x1[5 * each : 9 * each] + jax.nn.silu(pre1[3 * each : 7 * each])).astype(bf16)
    g2 = jnp.concatenate([r[...].astype(f32) for r in (cl_ref, cot_ref, cr_ref)], axis=0)
    gpre1 = rounded(g2 * silu_slope(pre1))
    n2 = 6 * each
    g1 = g2[2 * each : 8 * each] + sum(
        nt_dot(gpre1[(4 - 2 * j) * each : (4 - 2 * j) * each + n2].astype(bf16), conv_ref[1, j]) for j in range(KSIZE)
    )
    gpre0 = rounded(g1 * silu_slope(pre0[4 * each : 10 * each]))
    gpre0 = jnp.where(inside(5, 6), gpre0, 0.0)
    g0 = g1[each : 5 * each] + sum(
        nt_dot(gpre0[(2 - j) * each : (2 - j) * each + rows].astype(bf16), conv_ref[0, j]) for j in range(KSIZE)
    )
    grad_att = rounded(nt_dot(g0.astype(bf16), w_out))
    msg_ref[:, :width] = grad_att.astype(bf16)
    product = grad_att * own_ref[...].astype(f32)
    head = head_of_lane((rows, width))
    lane = lax.broadcasted_iota(jnp.int32, (rows, 128), 1)
    stats = stats_ref[...]
    for h in range(heads):
        delta = jnp.sum(jnp.where(head == h, product, 0.0), axis=1, keepdims=True)
        stats = jnp.where(lane == 2 * heads + h, delta, stats)
    stats = jnp.where(lane < 3 * heads, stats, 0.0)
    high = rounded(stats)
    middle = rounded(stats - high)
    low = (stats - high) - middle
    for copy in fetches:
        copy.wait()
    msg_ref[:, width:] = (high + pltpu.roll(middle, 32, 1) + pltpu.roll(low, 64, 1)).astype(bf16)


def conv_stack(tm, own, everyone, stats, cots, w_out, conv_weight, conv_bias, kvs):
    rows, width = own.shape
    cl, cot, cr = cots
    vmem = pl.BlockSpec(memory_space=pltpu.VMEM)
    return pl.pallas_call(
        conv_kernel,
        in_specs=[pl.BlockSpec(memory_space=pltpu.SMEM)]
        + [vmem] * 8
        + [pl.BlockSpec(memory_space=pltpu.HBM)] * (1 + len(kvs)),
        out_specs=[vmem] * (2 + len(kvs)),
        out_shape=[
            jax.ShapeDtypeStruct((rows, width), bf16),
            jax.ShapeDtypeStruct((rows, width + 128), bf16),
        ]
        + [pltpu.VMEM(kv.shape[1:], kv.dtype) for kv in kvs],
        scratch_shapes=[
            pltpu.VMEM(((NTM + 3) * rows, width), f32),
            pltpu.VMEM(conv_weight.shape, conv_weight.dtype),
            pltpu.SemaphoreType.DMA((LAYERS,)),
            pltpu.SemaphoreType.DMA((len(kvs),)),
        ],
        compiler_params=pltpu.CompilerParams(vmem_limit_bytes=20 * MIB),
        name="conv_stack",
    )(tm, own, everyone, stats, cl, cot, cr, w_out, conv_bias, *(pltpu.with_memory_space_constraint(a, pltpu.HBM) for a in (conv_weight, *kvs)))


def backward_kernel(y_ref, q_ref, *refs, slots):
    msg_refs, refs = refs[:slots], refs[slots:]
    n = (len(refs) - 3) // 4
    first_refs, valid_refs, kv_hbms = refs[:n], refs[n : 2 * n], refs[2 * n : 3 * n]
    dq_ref, acc_ref, *kv_refs, sem = refs[3 * n :]
    width = q_ref.shape[1]
    heads = width // HD
    windows = msg_refs[0].shape[0]

    def fetch(window, i):
        return pltpu.make_async_copy(kv_hbms[i].at[window], kv_refs[i].at[window - 1], sem.at[window - 1, i])

    for window in range(1, windows):
        for i in range(n):
            fetch(window, i).start()

    def one_window(window, blocks):
        msg = jnp.concatenate([r[window].astype(f32) for r in msg_refs], axis=0)
        terms = msg[:, width:]
        stats = terms + pltpu.roll(terms, 96, 1) + pltpu.roll(terms, 64, 1)
        top = lanes_to_column(stats, heads, 0)
        inverse = lanes_to_column(stats, heads, heads)
        delta = lanes_to_column(stats, heads, 2 * heads)
        grad_wide = spread_heads(msg[:, :width].astype(bf16), heads)
        q_wide = spread_heads(q_ref[...], heads)
        accum = 0.0
        for block, valid_ref in zip(blocks, valid_refs):
            key_rows = block[:, :width]
            scores = nt_dot(q_wide, key_rows) * scale_dot
            scores = jnp.where(valid_ref[0:1, :] > 0.0, scores, neg_big)
            prob = jnp.exp(scores - top) * inverse
            grad_prob = nt_dot(grad_wide, block[:, width:])
            dscore = (prob * (grad_prob - delta)).astype(bf16)
            accum = accum + nn_dot(dscore, key_rows)
        return accum

    acc_ref[...] = one_window(0, first_refs)

    @pl.loop(1, windows)
    def _(window):
        for i in range(n):
            fetch(window, i).wait()
        acc_ref[...] = acc_ref[...] + one_window(window, [ref.at[window - 1] for ref in kv_refs])

    dq = collect_heads(acc_ref[...], heads) * scale_dot
    each = dq.shape[0] // slots
    for s in range(slots):
        place = pl.multiple_of(((y_ref[0] + (slots - s)) % slots) * each, each)
        dq_ref[pl.ds(place, each), :] = dq[s * each : (s + 1) * each]


def backward_attention(y, kvs, first, valids, q, msgs):
    lat, width = q.shape
    heads = width // HD
    vmem = pl.BlockSpec(memory_space=pltpu.VMEM)
    kvs = [pltpu.with_memory_space_constraint(kv, pltpu.HBM) for kv in kvs]
    return pl.pallas_call(
        functools.partial(backward_kernel, slots=len(msgs)),
        in_specs=[pl.BlockSpec(memory_space=pltpu.SMEM)]
        + [vmem] * (1 + len(msgs) + len(first) + len(valids))
        + [pl.BlockSpec(memory_space=pltpu.HBM)] * len(kvs),
        out_specs=vmem,
        out_shape=jax.ShapeDtypeStruct((lat, width), f32),
        scratch_shapes=[pltpu.VMEM((lat * heads, width), f32)]
        + [pltpu.VMEM((kv.shape[0] - 1,) + kv.shape[1:], kv.dtype) for kv in kvs]
        + [pltpu.SemaphoreType.DMA((kvs[0].shape[0] - 1, len(kvs)))],
        compiler_params=pltpu.CompilerParams(vmem_limit_bytes=VMEM_BACK * MIB),
        name="backward_attention",
    )(y, q, *msgs, *first, *valids, *kvs)


def shift(count, by):
    return [(i, (i + by) % count) for i in range(count)]


def local(
    signal, pos_idx, live_count, latents, pos_table, w_in, w_kv, w_query, w_out,
    conv_weight, conv_bias, cotangent,
):
    con_dev = signal.shape[0]
    pat_dev = signal.shape[1] // PATCH
    width = w_query.shape[0]
    lat_rows = latents.shape[0]
    y, z, tm = (lax.axis_index(a) for a in ("y", "z", "tm"))
    lat_dev = lat_rows // (NY * NZ)
    up1 = [(i, i + 1) for i in range(NTM - 1)]
    down1 = [(i + 1, i) for i in range(NTM - 1)]

    by_owner = latents.reshape(NY, NZ, lat_dev, width)
    mine = lax.dynamic_index_in_dim(by_owner, z, 1, False)
    slots = jnp.stack([lax.dynamic_index_in_dim(mine, (y + NY - s) % NY, 0, False) for s in range(NY)])
    queries = nn_dot(slots.reshape(NY * lat_dev, width), w_query).astype(bf16)

    lane = lax.broadcasted_iota(jnp.int32, (con_dev, 128), 1)
    index = pos_idx[:, None]
    meta = jnp.where(lane == 0, index // 64, jnp.where(lane == 1, index % 64, live_count[0]))
    own = jnp.concatenate([signal, meta.astype(bf16)], axis=1)

    def absorbed(messages, state, last=False):
        return absorb(messages, queries, w_in, w_kv, pos_table, state, last)

    cot = cotangent.reshape(pat_dev * lat_dev, width)
    cot_left = lax.ppermute(cot[lat_dev:], "tm", up1)
    cot_right = lax.ppermute(cot[: 3 * lat_dev], "tm", down1)

    below, above = own, own
    at_hand, state, kvs, valids = [own], None, [], []
    for step in range(1, NZ // 2 + 1):
        below = lax.ppermute(below, "z", shift(NZ, 1))
        if step < NZ // 2:
            above = lax.ppermute(above, "z", shift(NZ, -1))
        kv, valid, *state = absorbed(at_hand, state)
        kvs.append(kv)
        valids.append(valid)
        if step == 2:
            below, above, valids[-1], cot_left, cot_right = lax.optimization_barrier(
                (below, above, valids[-1], cot_left, cot_right)
            )
        elif step < NZ // 2:
            below, above, valids[-1] = lax.optimization_barrier((below, above, valids[-1]))
        at_hand = [below, above] if step < NZ // 2 else [below]
    kv, valid, *parts = absorbed(at_hand, state, last=True)
    kvs.append(kv)
    valids.append(valid)

    received = [lax.ppermute(parts[s], "y", shift(NY, -s)) for s in range(1, NY)]
    att, stats = combine([parts[0]] + received)

    everyone = lax.all_to_all(jnp.broadcast_to(att, (NTM,) + att.shape), "tm", 0, 0)
    features, msg, *first = conv_stack(
        tm.reshape(1), att, everyone.reshape(-1, width), stats,
        (cot_left, cot, cot_right), w_out, conv_weight, conv_bias, kvs,
    )

    msg = msg.reshape(pat_dev, lat_dev, width + 128)
    msgs = [msg] + [lax.ppermute(msg, "y", shift(NY, s)) for s in range(1, NY)]
    dq = backward_attention(y.reshape(1), kvs, first, valids, queries, msgs)

    pieces = lax.all_to_all(dq, ("y", "tm"), 0, 0, tiled=True)
    dq_row = jnp.sum(pieces, axis=0, keepdims=True).astype(bf16)
    copies = jnp.broadcast_to(dq_row.reshape(1, width // 128, 128), (lat_rows, width // 128, 128))
    dq_all = lax.all_to_all(copies, ("y", "z", "tm"), 0, 0, tiled=True)
    d_latents = nt_dot(dq_all.reshape(lat_rows, width), w_query)
    return features.reshape(pat_dev, lat_dev, width), d_latents


def solution(mesh):
    split = Mesh(mesh.devices.reshape(NY, NZ, NTM), ("y", "z", "tm"))
    contacts = ("y", "z")
    in_specs = (P(contacts, "tm"), P(contacts), P(contacts)) + (P(),) * 8 + (P("tm", contacts, None),)
    out_specs = (P("tm", contacts, None), P())
    return jax.shard_map(local, mesh=split, in_specs=in_specs, out_specs=out_specs, check_vma=False)
```

```python
import functools

import jax
import jax.numpy as jnp
from jax import lax
from jax.experimental import pallas as pl
from jax.experimental.pallas import tpu as pltpu
from jax.sharding import Mesh
from jax.sharding import PartitionSpec as P

HD = 64
PATCH = 32
KSIZE = 3
LAYERS = 2

neg_big = -1e30
scale_dot = 0.125

bf16 = jnp.bfloat16
f32 = jnp.float32

NY, NZ, NTM = 4, 8, 8
MIB = 1 << 20
PIECE, PARTS, HALVES, VMEM_ABSORB = 2048, 2, 2, 28
WUNROLL, VMEM_BACK = 4, 40


def nt_dot(a, b):
    return lax.dot_general(a, b, (((1,), (1,)), ((), ())), preferred_element_type=f32)


def nn_dot(a, b):
    return jnp.dot(a, b, preferred_element_type=f32)


def head_of_lane(shape):
    return lax.broadcasted_iota(jnp.int32, shape, len(shape) - 1) // HD


def spread_heads(rows, heads):
    head = head_of_lane(rows.shape)
    zero = jnp.zeros_like(rows)
    return jnp.concatenate([jnp.where(head == h, rows, zero) for h in range(heads)], axis=0)


def collect_heads(blocks, heads):
    r = blocks.shape[0] // heads
    head = head_of_lane((r, blocks.shape[1]))
    out = blocks[:r]
    for h in range(1, heads):
        out = jnp.where(head == h, blocks[h * r : (h + 1) * r], out)
    return out


def columns_to_lanes(column, heads, first, base):
    r = base.shape[0]
    lane = lax.broadcasted_iota(jnp.int32, base.shape, 1)
    for h in range(heads):
        base = jnp.where(lane == first + h, column[h * r : (h + 1) * r], base)
    return base


def lanes_to_column(stats, heads, first):
    return jnp.concatenate([stats[:, first + h : first + h + 1] for h in range(heads)], axis=0)


def lanes_to_columns_wide(stats, heads, first):
    r = stats.shape[0]
    head = head_of_lane((r, heads * HD))
    out = jnp.broadcast_to(stats[:, first : first + 1], (r, heads * HD))
    for h in range(1, heads):
        out = jnp.where(head == h, stats[:, first + h : first + h + 1], out)
    return out


def silu_slope(pre_act):
    sigmoid_v = jax.nn.sigmoid(pre_act)
    return sigmoid_v * (1.0 + pre_act * (1.0 - sigmoid_v))


def rounded(value):
    return value.astype(bf16).astype(f32)


def absorb_kernel(*refs, fresh, last, count):
    refs = list(refs)
    messages = [refs.pop(0) for _ in range(count)]
    q_ref, w_in_ref, w_kv_ref, table_ref = (refs.pop(0) for _ in range(4))
    if not fresh:
        acc_in, stat_in = refs.pop(0), refs.pop(0)
    kv_hbm, valid_ref = refs.pop(0), refs.pop(0)
    if last:
        part_refs = [refs.pop(0) for _ in range(NY)]
    else:
        acc_out, stat_out = refs.pop(0), refs.pop(0)
    pos_ref, tok_ref, kv_ref, sem = refs
    width = q_ref.shape[1]
    heads = width // HD
    con_dev, span = messages[0].shape[0], messages[0].shape[1] - 128
    windows = span // PATCH
    rows = count * con_dev
    message = jnp.concatenate([m[...] for m in messages], axis=0)
    sig = message[:, :span]
    meta = message[:, span:].astype(f32)
    idx = meta[:, 0:1] * 64.0 + meta[:, 1:2]
    lane = lax.broadcasted_iota(jnp.int32, (1, con_dev), 1).astype(f32)
    valid = jnp.concatenate(
        [jnp.where(lane < meta[c * con_dev : c * con_dev + 1, 2:3], 1.0, 0.0) for c in range(count)], axis=1
    )
    valid_ref[...] = jnp.broadcast_to(valid, valid_ref.shape)
    piece = PIECE
    ids = lax.broadcasted_iota(jnp.int32, (rows, piece), 1).astype(f32)
    pos_ref[...] = jnp.zeros_like(pos_ref)

    @pl.loop(0, table_ref.shape[0] // piece)
    def _(k):
        start = pl.multiple_of(k * piece, piece)
        hot = jnp.where(ids == idx - start.astype(f32), 1.0, 0.0).astype(bf16)
        pos_ref[...] = pos_ref[...] + nn_dot(hot, table_ref[pl.ds(start, piece), :])

    tall = jnp.concatenate([w_in_ref[...]] * windows, axis=0)
    band = lax.broadcasted_iota(jnp.int32, sig.shape, 1) // PATCH
    for w in range(windows):
        embedded = nn_dot(jnp.where(band == w, sig, jnp.zeros_like(sig)), tall)
        tok_ref[w * rows : (w + 1) * rows, :] = (embedded + pos_ref[...]).astype(bf16)
    ws = windows // PARTS

    def send(part):
        here = pl.ds(part * ws, ws)
        return pltpu.make_async_copy(kv_ref.at[here], kv_hbm.at[here], sem.at[part])

    def project(part):
        tokens = tok_ref[pl.ds(pl.multiple_of(part * ws * rows, ws * rows), ws * rows), :]
        for half in range(HALVES):
            cols = slice(half * 2 * width // HALVES, (half + 1) * 2 * width // HALVES)
            keyval = nn_dot(tokens, w_kv_ref[:, cols]).astype(bf16)
            kv_ref[pl.ds(part * ws, ws), :, cols] = keyval.reshape(ws, rows, 2 * width // HALVES)
        send(part).start()

    if count == 1:
        for part in range(PARTS):
            project(part)
    else:
        pl.loop(0, PARTS)(project)
    q_wide = spread_heads(q_ref[...], heads)

    def one_window(w):
        scores = nt_dot(q_wide, kv_ref[w, :, :width]) * scale_dot
        scores = jnp.where(valid > 0.0, scores, neg_big)
        top = jnp.max(scores, axis=1, keepdims=True)
        if not fresh:
            before, total_before = stat_in[w, :, 0:1], stat_in[w, :, 1:2]
            top = jnp.maximum(top, before)
        weights = jnp.exp(scores - top)
        totals = jnp.sum(weights, axis=1, keepdims=True)
        accum = nn_dot(weights.astype(bf16), kv_ref[w, :, width:])
        if not fresh:
            fade = jnp.exp(before - top)
            totals = totals + total_before * fade
            accum = accum + acc_in[w] * fade
        if not last:
            acc_out[w] = accum
            stat_out[w, :, 0:1] = top
            stat_out[w, :, 1:2] = totals
        else:
            mixed = collect_heads(accum, heads)
            stats = jnp.zeros((mixed.shape[0], 128), f32)
            stats = columns_to_lanes(top, heads, 0, stats)
            stats = columns_to_lanes(totals, heads, heads, stats)
            each = mixed.shape[0] // NY
            for s, part_ref in enumerate(part_refs):
                part_ref[w, :, :width] = mixed[s * each : (s + 1) * each]
                part_ref[w, :, width:] = stats[s * each : (s + 1) * each]

    together = WUNROLL // count

    @pl.loop(0, windows // together)
    def _(k):
        for part in range(together):
            one_window(k * together + part)

    for part in range(PARTS):
        send(part).wait()


def absorb(messages, q, w_in, w_kv, table, state, last):
    count = len(messages)
    lat, width = q.shape
    con_dev = messages[0].shape[0]
    windows = (messages[0].shape[1] - 128) // PATCH
    rows = lat * (width // HD)
    fresh = state is None
    vmem = pl.BlockSpec(memory_space=pltpu.VMEM)
    operands = list(messages) + [q, w_in, w_kv, table]
    in_specs = [vmem] * len(operands)
    aliases = {}
    if not fresh:
        n = len(operands)
        operands += list(state)
        in_specs += [vmem, vmem]
        aliases = {} if last else {n: 2, n + 1: 3}
    acc = jax.ShapeDtypeStruct((windows, rows, width), f32)
    stat = jax.ShapeDtypeStruct((windows, rows, 128), f32)
    part = jax.ShapeDtypeStruct((windows, lat // NY, width + 128), f32)
    tail = [part] * NY if last else [acc, stat]
    return pl.pallas_call(
        functools.partial(absorb_kernel, fresh=fresh, last=last, count=count),
        in_specs=in_specs,
        out_specs=[pl.BlockSpec(memory_space=pltpu.HBM)] + [vmem] * (1 + len(tail)),
        out_shape=[
            pltpu.HBM((windows, count * con_dev, 2 * width), bf16),
            jax.ShapeDtypeStruct((8, count * con_dev), f32),
        ]
        + tail,
        scratch_shapes=[
            pltpu.VMEM((count * con_dev, width), f32),
            pltpu.VMEM((windows * count * con_dev, width), bf16),
            pltpu.VMEM((windows, count * con_dev, 2 * width), bf16),
            pltpu.SemaphoreType.DMA((PARTS,)),
        ],
        input_output_aliases=aliases,
        compiler_params=pltpu.CompilerParams(vmem_limit_bytes=VMEM_ABSORB * MIB),
        name="absorb",
    )(*operands)


def combine_kernel(*refs):
    *part_refs, att_ref, copies_ref, stats_ref = refs
    rows, width = att_ref.shape
    heads = width // HD
    lane = lax.broadcasted_iota(jnp.int32, (rows, 128), 1)
    parts = [ref[...].reshape(rows, width + 128) for ref in part_refs]
    top = parts[0][:, width:]
    for part in parts[1:]:
        top = jnp.maximum(top, part[:, width:])
    totals = jnp.zeros((rows, 128), f32)
    accum = jnp.zeros((rows, width), f32)
    for part in parts:
        factor = jnp.exp(jnp.where(lane < heads, part[:, width:] - top, 0.0))
        totals = totals + factor * pltpu.roll(part[:, width:], 128 - heads, 1)
        accum = accum + part[:, :width] * lanes_to_columns_wide(factor, heads, 0)
    totals = jnp.where(lane < heads, totals, 1.0)
    att = (accum / lanes_to_columns_wide(totals, heads, 0)).astype(bf16)
    att_ref[...] = att
    for t in range(NTM):
        copies_ref[t] = att
    stats_ref[...] = jnp.where(lane < heads, top, pltpu.roll(1.0 / totals, heads, 1))


def combine(parts):
    windows, each, wide = parts[0].shape
    rows = windows * each
    return pl.pallas_call(
        combine_kernel,
        out_shape=[
            jax.ShapeDtypeStruct((rows, wide - 128), bf16),
            jax.ShapeDtypeStruct((NTM, rows, wide - 128), bf16),
            jax.ShapeDtypeStruct((rows, 128), f32),
        ],
        compiler_params=pltpu.CompilerParams(vmem_limit_bytes=8 * MIB),
        name="combine_parts",
    )(*parts)


def conv_kernel(
    tm_ref, own_ref, all_ref, stats_ref, cl_ref, cot_ref, cr_ref,
    w_out_ref, bias_ref, conv_hbm, *refs,
):
    n = (len(refs) - 6) // 2
    kv_hbms, (feat_ref, msg_ref), kv_refs = refs[:n], refs[n : n + 2], refs[n + 2 : 2 * n + 2]
    ext_ref, conv_ref, sem, kv_sem = refs[2 * n + 2 :]
    fetches = [pltpu.make_async_copy(kv_hbms[i].at[0], kv_refs[i], kv_sem.at[i]) for i in range(n)]
    weights = [pltpu.make_async_copy(conv_hbm.at[l], conv_ref.at[l], sem.at[l]) for l in range(LAYERS)]
    for copy in weights:
        copy.start()
    for copy in fetches:
        copy.start()
    rows, width = own_ref.shape
    heads = width // HD
    windows = 4
    each = rows // windows
    reach = 6
    first = tm_ref[0] * windows - reach
    total_windows = NTM * windows

    def inside(lo, count):
        w = lax.broadcasted_iota(jnp.int32, (count * each, width), 0) // each + (first + lo)
        return jnp.logical_and(w >= 0, w < total_windows)

    side = reach * each
    ext_ref[:side, :] = jnp.zeros((side, width), f32)
    ext_ref[side : side + NTM * rows, :] = all_ref[...].astype(f32)
    ext_ref[side + NTM * rows :, :] = jnp.zeros((side, width), f32)
    att = ext_ref[pl.ds(pl.multiple_of(tm_ref[0] * rows, rows), 2 * side + rows), :]
    w_out = w_out_ref[...]
    x0 = rounded(nn_dot(att.astype(bf16), w_out))
    n0 = 14 * each
    weights[0].wait()
    pre0 = bias_ref[0:1, :] + sum(nn_dot(x0[j * each : j * each + n0].astype(bf16), conv_ref[0, j]) for j in range(KSIZE))
    x1 = rounded(x0[each : each + n0] + jax.nn.silu(pre0))
    x1 = jnp.where(inside(1, 14), x1, 0.0)
    n1 = 10 * each
    weights[1].wait()
    pre1 = bias_ref[1:2, :] + sum(nn_dot(x1[2 * j * each : 2 * j * each + n1].astype(bf16), conv_ref[1, j]) for j in range(KSIZE))
    feat_ref[...] = (x1[5 * each : 9 * each] + jax.nn.silu(pre1[3 * each : 7 * each])).astype(bf16)
    g2 = jnp.concatenate([r[...].astype(f32) for r in (cl_ref, cot_ref, cr_ref)], axis=0)
    gpre1 = rounded(g2 * silu_slope(pre1))
    n2 = 6 * each
    g1 = g2[2 * each : 8 * each] + sum(
        nt_dot(gpre1[(4 - 2 * j) * each : (4 - 2 * j) * each + n2].astype(bf16), conv_ref[1, j]) for j in range(KSIZE)
    )
    gpre0 = rounded(g1 * silu_slope(pre0[4 * each : 10 * each]))
    gpre0 = jnp.where(inside(5, 6), gpre0, 0.0)
    g0 = g1[each : 5 * each] + sum(
        nt_dot(gpre0[(2 - j) * each : (2 - j) * each + rows].astype(bf16), conv_ref[0, j]) for j in range(KSIZE)
    )
    grad_att = rounded(nt_dot(g0.astype(bf16), w_out))
    msg_ref[:, :width] = grad_att.astype(bf16)
    product = grad_att * own_ref[...].astype(f32)
    head = head_of_lane((rows, width))
    lane = lax.broadcasted_iota(jnp.int32, (rows, 128), 1)
    stats = stats_ref[...]
    for h in range(heads):
        delta = jnp.sum(jnp.where(head == h, product, 0.0), axis=1, keepdims=True)
        stats = jnp.where(lane == 2 * heads + h, delta, stats)
    stats = jnp.where(lane < 3 * heads, stats, 0.0)
    high = rounded(stats)
    middle = rounded(stats - high)
    low = (stats - high) - middle
    for copy in fetches:
        copy.wait()
    msg_ref[:, width:] = (high + pltpu.roll(middle, 32, 1) + pltpu.roll(low, 64, 1)).astype(bf16)


def conv_stack(tm, own, everyone, stats, cots, w_out, conv_weight, conv_bias, kvs):
    rows, width = own.shape
    cl, cot, cr = cots
    vmem = pl.BlockSpec(memory_space=pltpu.VMEM)
    return pl.pallas_call(
        conv_kernel,
        in_specs=[pl.BlockSpec(memory_space=pltpu.SMEM)]
        + [vmem] * 8
        + [pl.BlockSpec(memory_space=pltpu.HBM)] * (1 + len(kvs)),
        out_specs=[vmem] * (2 + len(kvs)),
        out_shape=[
            jax.ShapeDtypeStruct((rows, width), bf16),
            jax.ShapeDtypeStruct((rows, width + 128), bf16),
        ]
        + [pltpu.VMEM(kv.shape[1:], kv.dtype) for kv in kvs],
        scratch_shapes=[
            pltpu.VMEM(((NTM + 3) * rows, width), f32),
            pltpu.VMEM(conv_weight.shape, conv_weight.dtype),
            pltpu.SemaphoreType.DMA((LAYERS,)),
            pltpu.SemaphoreType.DMA((len(kvs),)),
        ],
        compiler_params=pltpu.CompilerParams(vmem_limit_bytes=20 * MIB),
        name="conv_stack",
    )(tm, own, everyone, stats, cl, cot, cr, w_out, conv_bias, *(pltpu.with_memory_space_constraint(a, pltpu.HBM) for a in (conv_weight, *kvs)))


def backward_kernel(y_ref, q_ref, *refs, slots):
    msg_refs, refs = refs[:slots], refs[slots:]
    n = (len(refs) - 3) // 4
    first_refs, valid_refs, kv_hbms = refs[:n], refs[n : 2 * n], refs[2 * n : 3 * n]
    dq_ref, acc_ref, *kv_refs, sem = refs[3 * n :]
    width = q_ref.shape[1]
    heads = width // HD
    windows = msg_refs[0].shape[0]

    def fetch(window, i):
        return pltpu.make_async_copy(kv_hbms[i].at[window], kv_refs[i].at[window - 1], sem.at[window - 1, i])

    for window in range(1, windows):
        for i in range(n):
            fetch(window, i).start()

    def one_window(window, blocks):
        msg = jnp.concatenate([r[window].astype(f32) for r in msg_refs], axis=0)
        terms = msg[:, width:]
        stats = terms + pltpu.roll(terms, 96, 1) + pltpu.roll(terms, 64, 1)
        top = lanes_to_column(stats, heads, 0)
        inverse = lanes_to_column(stats, heads, heads)
        delta = lanes_to_column(stats, heads, 2 * heads)
        grad_wide = spread_heads(msg[:, :width].astype(bf16), heads)
        q_wide = spread_heads(q_ref[...], heads)
        accum = 0.0
        for block, valid_ref in zip(blocks, valid_refs):
            key_rows = block[:, :width]
            scores = nt_dot(q_wide, key_rows) * scale_dot
            scores = jnp.where(valid_ref[0:1, :] > 0.0, scores, neg_big)
            prob = jnp.exp(scores - top) * inverse
            grad_prob = nt_dot(grad_wide, block[:, width:])
            dscore = (prob * (grad_prob - delta)).astype(bf16)
            accum = accum + nn_dot(dscore, key_rows)
        return accum

    acc_ref[...] = one_window(0, first_refs)

    @pl.loop(1, windows)
    def _(window):
        for i in range(n):
            fetch(window, i).wait()
        acc_ref[...] = acc_ref[...] + one_window(window, [ref.at[window - 1] for ref in kv_refs])

    dq = collect_heads(acc_ref[...], heads) * scale_dot
    each = dq.shape[0] // slots
    for s in range(slots):
        place = pl.multiple_of(((y_ref[0] + (slots - s)) % slots) * each, each)
        dq_ref[pl.ds(place, each), :] = dq[s * each : (s + 1) * each]


def backward_attention(y, kvs, first, valids, q, msgs):
    lat, width = q.shape
    heads = width // HD
    vmem = pl.BlockSpec(memory_space=pltpu.VMEM)
    kvs = [pltpu.with_memory_space_constraint(kv, pltpu.HBM) for kv in kvs]
    return pl.pallas_call(
        functools.partial(backward_kernel, slots=len(msgs)),
        in_specs=[pl.BlockSpec(memory_space=pltpu.SMEM)]
        + [vmem] * (1 + len(msgs) + len(first) + len(valids))
        + [pl.BlockSpec(memory_space=pltpu.HBM)] * len(kvs),
        out_specs=vmem,
        out_shape=jax.ShapeDtypeStruct((lat, width), f32),
        scratch_shapes=[pltpu.VMEM((lat * heads, width), f32)]
        + [pltpu.VMEM((kv.shape[0] - 1,) + kv.shape[1:], kv.dtype) for kv in kvs]
        + [pltpu.SemaphoreType.DMA((kvs[0].shape[0] - 1, len(kvs)))],
        compiler_params=pltpu.CompilerParams(vmem_limit_bytes=VMEM_BACK * MIB),
        name="backward_attention",
    )(y, q, *msgs, *first, *valids, *kvs)


def shift(count, by):
    return [(i, (i + by) % count) for i in range(count)]


def local(
    signal, pos_idx, live_count, latents, pos_table, w_in, w_kv, w_query, w_out,
    conv_weight, conv_bias, cotangent,
):
    con_dev = signal.shape[0]
    pat_dev = signal.shape[1] // PATCH
    width = w_query.shape[0]
    lat_rows = latents.shape[0]
    y, z, tm = (lax.axis_index(a) for a in ("y", "z", "tm"))
    lat_dev = lat_rows // (NY * NZ)
    up1 = [(i, i + 1) for i in range(NTM - 1)]
    down1 = [(i + 1, i) for i in range(NTM - 1)]

    by_owner = latents.reshape(NY, NZ, lat_dev, width)
    mine = lax.dynamic_index_in_dim(by_owner, z, 1, False)
    slots = jnp.stack([lax.dynamic_index_in_dim(mine, (y + NY - s) % NY, 0, False) for s in range(NY)])
    queries = nn_dot(slots.reshape(NY * lat_dev, width), w_query).astype(bf16)

    lane = lax.broadcasted_iota(jnp.int32, (con_dev, 128), 1)
    index = pos_idx[:, None]
    meta = jnp.where(lane == 0, index // 64, jnp.where(lane == 1, index % 64, live_count[0]))
    own = jnp.concatenate([signal, meta.astype(bf16)], axis=1)

    def absorbed(messages, state, last=False):
        return absorb(messages, queries, w_in, w_kv, pos_table, state, last)

    below, above = own, own
    at_hand, state, kvs, valids = [own], None, [], []
    for step in range(1, NZ // 2 + 1):
        below = lax.ppermute(below, "z", shift(NZ, 1))
        if step < NZ // 2:
            above = lax.ppermute(above, "z", shift(NZ, -1))
        kv, valid, *state = absorbed(at_hand, state)
        kvs.append(kv)
        valids.append(valid)
        if step < NZ // 2:
            below, above, valids[-1] = lax.optimization_barrier((below, above, valids[-1]))
        at_hand = [below, above] if step < NZ // 2 else [below]
    kv, valid, *parts = absorbed(at_hand, state, last=True)
    kvs.append(kv)
    valids.append(valid)

    received = [lax.ppermute(parts[s], "y", shift(NY, -s)) for s in range(1, NY)]

    cot = cotangent.reshape(pat_dev * lat_dev, width)
    cot_late, cot_early, _ = lax.optimization_barrier((cot[lat_dev:], cot[: 3 * lat_dev], parts[0]))
    cot_left = lax.ppermute(cot_late, "tm", up1)
    cot_right = lax.ppermute(cot_early, "tm", down1)

    att, copies, stats = combine([parts[0]] + received)

    everyone = lax.all_to_all(copies, "tm", 0, 0)
    features, msg, *first = conv_stack(
        tm.reshape(1), att, everyone.reshape(-1, width), stats,
        (cot_left, cot, cot_right), w_out, conv_weight, conv_bias, kvs,
    )

    msg = msg.reshape(pat_dev, lat_dev, width + 128)
    msgs = [msg] + [lax.ppermute(msg, "y", shift(NY, s)) for s in range(1, NY)]
    dq = backward_attention(y.reshape(1), kvs, first, valids, queries, msgs)

    pieces = lax.all_to_all(dq, ("y", "tm"), 0, 0, tiled=True)
    dq_row = jnp.sum(pieces, axis=0, keepdims=True).astype(bf16)
    spread = jnp.broadcast_to(dq_row.reshape(1, width // 128, 128), (lat_rows, width // 128, 128))
    dq_all = lax.all_to_all(spread, ("y", "z", "tm"), 0, 0, tiled=True)
    d_latents = nt_dot(dq_all.reshape(lat_rows, width), w_query)
    return features.reshape(pat_dev, lat_dev, width), d_latents


def solution(mesh):
    split = Mesh(mesh.devices.reshape(NY, NZ, NTM), ("y", "z", "tm"))
    contacts = ("y", "z")
    in_specs = (P(contacts, "tm"), P(contacts), P(contacts)) + (P(),) * 8 + (P("tm", contacts, None),)
    out_specs = (P("tm", contacts, None), P())
    return jax.shard_map(local, mesh=split, in_specs=in_specs, out_specs=out_specs, check_vma=False)
```

```python
import functools

import jax
import jax.numpy as jnp
from jax import lax
from jax.experimental import pallas as pl
from jax.experimental.pallas import tpu as pltpu
from jax.sharding import Mesh
from jax.sharding import PartitionSpec as P

HD = 64
PATCH = 32
KSIZE = 3
LAYERS = 2

neg_big = -1e30
scale_dot = 0.125

bf16 = jnp.bfloat16
f32 = jnp.float32

NY, NZ, NTM = 4, 8, 8
MIB = 1 << 20
PIECE, PARTS, HALVES, VMEM_ABSORB = 2048, 2, 2, 28
WUNROLL, VMEM_BACK = 4, 40


def nt_dot(a, b):
    return lax.dot_general(a, b, (((1,), (1,)), ((), ())), preferred_element_type=f32)


def nn_dot(a, b):
    return jnp.dot(a, b, preferred_element_type=f32)


def head_of_lane(shape):
    return lax.broadcasted_iota(jnp.int32, shape, len(shape) - 1) // HD


def spread_heads(rows, heads):
    head = head_of_lane(rows.shape)
    zero = jnp.zeros_like(rows)
    return jnp.concatenate([jnp.where(head == h, rows, zero) for h in range(heads)], axis=0)


def collect_heads(blocks, heads):
    r = blocks.shape[0] // heads
    head = head_of_lane((r, blocks.shape[1]))
    out = blocks[:r]
    for h in range(1, heads):
        out = jnp.where(head == h, blocks[h * r : (h + 1) * r], out)
    return out


def columns_to_lanes(column, heads, first, base):
    r = base.shape[0]
    lane = lax.broadcasted_iota(jnp.int32, base.shape, 1)
    for h in range(heads):
        base = jnp.where(lane == first + h, column[h * r : (h + 1) * r], base)
    return base


def lanes_to_column(stats, heads, first):
    return jnp.concatenate([stats[:, first + h : first + h + 1] for h in range(heads)], axis=0)


def lanes_to_columns_wide(stats, heads, first):
    r = stats.shape[0]
    head = head_of_lane((r, heads * HD))
    out = jnp.broadcast_to(stats[:, first : first + 1], (r, heads * HD))
    for h in range(1, heads):
        out = jnp.where(head == h, stats[:, first + h : first + h + 1], out)
    return out


def silu_slope(pre_act):
    sigmoid_v = jax.nn.sigmoid(pre_act)
    return sigmoid_v * (1.0 + pre_act * (1.0 - sigmoid_v))


def rounded(value):
    return value.astype(bf16).astype(f32)


def message_kernel(live_ref, signal_hbm, index_hbm, message_ref, signal_ref, index_ref, sem):
    con_dev, span = signal_hbm.shape
    copies = [
        pltpu.make_async_copy(index_hbm, index_ref, sem.at[0]),
        pltpu.make_async_copy(signal_hbm, signal_ref, sem.at[1]),
    ]
    for copy in copies:
        copy.start()
    copies[0].wait()
    index = index_ref[...].astype(f32)
    for r in range(con_dev // 128):
        column = jnp.transpose(jnp.broadcast_to(index[r : r + 1], (128, 128)))
        high = jnp.floor(column * (1.0 / 64.0))
        lane = lax.broadcasted_iota(jnp.int32, column.shape, 1)
        meta = jnp.where(lane == 0, high, jnp.where(lane == 1, column - 64.0 * high, live_ref[0].astype(f32)))
        message_ref[r * 128 : (r + 1) * 128, span:] = meta.astype(bf16)
    copies[1].wait()
    message_ref[:, :span] = signal_ref[...]


def make_message(live_count, signal, pos_idx):
    con_dev, span = signal.shape
    index = pos_idx.reshape(con_dev // 128, 128)
    signal, index = (pltpu.with_memory_space_constraint(a, pltpu.HBM) for a in (signal, index))
    hbm = pl.BlockSpec(memory_space=pltpu.HBM)
    return pl.pallas_call(
        message_kernel,
        in_specs=[pl.BlockSpec(memory_space=pltpu.SMEM), hbm, hbm],
        out_specs=pl.BlockSpec(memory_space=pltpu.VMEM),
        out_shape=jax.ShapeDtypeStruct((con_dev, span + 128), bf16),
        scratch_shapes=[
            pltpu.VMEM(signal.shape, signal.dtype),
            pltpu.VMEM(index.shape, index.dtype),
            pltpu.SemaphoreType.DMA((2,)),
        ],
        compiler_params=pltpu.CompilerParams(vmem_limit_bytes=8 * MIB),
        name="make_message",
    )(live_count, signal, index)


def prepare_kernel(y_ref, z_ref, *refs):
    hbms, (q_ref, *here), sem = refs[:5], refs[5:11], refs[11]
    latents_ref, w_query_ref = here[3], here[4]
    copies = [pltpu.make_async_copy(a, b, sem.at[i]) for i, (a, b) in enumerate(zip(hbms, here))]
    for i in (3, 4, 0, 1, 2):
        copies[i].start()
    lat, each = latents_ref.shape[0], latents_ref.shape[0] // (NY * NZ)
    row = lax.broadcasted_iota(jnp.int32, (q_ref.shape[0], lat), 0)
    owner = (y_ref[0] + NY - row // each) % NY
    place = (owner * NZ + z_ref[0]) * each + row % each
    pick = jnp.where(lax.broadcasted_iota(jnp.int32, row.shape, 1) == place, 1.0, 0.0).astype(bf16)
    copies[3].wait()
    chosen = nn_dot(pick, latents_ref[...]).astype(bf16)
    copies[4].wait()
    q_ref[...] = nn_dot(chosen, w_query_ref[...]).astype(bf16)
    for copy in copies[:3]:
        copy.wait()


def prepare(y, z, table, w_kv, w_in, latents, w_query):
    smem, vmem = pl.BlockSpec(memory_space=pltpu.SMEM), pl.BlockSpec(memory_space=pltpu.VMEM)
    arrays = [pltpu.with_memory_space_constraint(a, pltpu.HBM) for a in (table, w_kv, w_in, latents, w_query)]
    return pl.pallas_call(
        prepare_kernel,
        in_specs=[smem] * 2 + [pl.BlockSpec(memory_space=pltpu.HBM)] * 5,
        out_specs=[vmem] * 4,
        out_shape=[jax.ShapeDtypeStruct((latents.shape[0] // NZ, w_query.shape[1]), bf16)]
        + [pltpu.VMEM(a.shape, a.dtype) for a in (table, w_kv, w_in)],
        scratch_shapes=[pltpu.VMEM(a.shape, a.dtype) for a in (latents, w_query)]
        + [pltpu.SemaphoreType.DMA((5,))],
        compiler_params=pltpu.CompilerParams(vmem_limit_bytes=8 * MIB),
        name="prepare",
    )(y, z, *arrays)


def absorb_kernel(*refs, fresh, last, count):
    refs = list(refs)
    messages = [refs.pop(0) for _ in range(count)]
    q_ref, w_in_ref, w_kv_ref, table_ref = (refs.pop(0) for _ in range(4))
    if not fresh:
        acc_in, stat_in = refs.pop(0), refs.pop(0)
    kv_hbm, valid_ref = refs.pop(0), refs.pop(0)
    if last:
        part_refs = [refs.pop(0) for _ in range(NY)]
    else:
        acc_out, stat_out = refs.pop(0), refs.pop(0)
    pos_ref, tok_ref, kv_ref, sem = refs
    width = q_ref.shape[1]
    heads = width // HD
    con_dev, span = messages[0].shape[0], messages[0].shape[1] - 128
    windows = span // PATCH
    rows = count * con_dev
    message = jnp.concatenate([m[...] for m in messages], axis=0)
    sig = message[:, :span]
    meta = message[:, span:].astype(f32)
    idx = meta[:, 0:1] * 64.0 + meta[:, 1:2]
    lane = lax.broadcasted_iota(jnp.int32, (1, con_dev), 1).astype(f32)
    valid = jnp.concatenate(
        [jnp.where(lane < meta[c * con_dev : c * con_dev + 1, 2:3], 1.0, 0.0) for c in range(count)], axis=1
    )
    valid_ref[...] = jnp.broadcast_to(valid, valid_ref.shape)
    piece = PIECE
    ids = lax.broadcasted_iota(jnp.int32, (rows, piece), 1).astype(f32)
    pos_ref[...] = jnp.zeros_like(pos_ref)

    @pl.loop(0, table_ref.shape[0] // piece)
    def _(k):
        start = pl.multiple_of(k * piece, piece)
        hot = jnp.where(ids == idx - start.astype(f32), 1.0, 0.0).astype(bf16)
        pos_ref[...] = pos_ref[...] + nn_dot(hot, table_ref[pl.ds(start, piece), :])

    tall = jnp.concatenate([w_in_ref[...]] * windows, axis=0)
    band = lax.broadcasted_iota(jnp.int32, sig.shape, 1) // PATCH
    for w in range(windows):
        embedded = nn_dot(jnp.where(band == w, sig, jnp.zeros_like(sig)), tall)
        tok_ref[w * rows : (w + 1) * rows, :] = (embedded + pos_ref[...]).astype(bf16)
    ws = windows // PARTS

    def send(part):
        here = pl.ds(part * ws, ws)
        return pltpu.make_async_copy(kv_ref.at[here], kv_hbm.at[here], sem.at[part])

    def project(part):
        tokens = tok_ref[pl.ds(pl.multiple_of(part * ws * rows, ws * rows), ws * rows), :]
        for half in range(HALVES):
            cols = slice(half * 2 * width // HALVES, (half + 1) * 2 * width // HALVES)
            keyval = nn_dot(tokens, w_kv_ref[:, cols]).astype(bf16)
            kv_ref[pl.ds(part * ws, ws), :, cols] = keyval.reshape(ws, rows, 2 * width // HALVES)
        send(part).start()

    if count == 1:
        for part in range(PARTS):
            project(part)
    else:
        pl.loop(0, PARTS)(project)
    q_wide = spread_heads(q_ref[...], heads)

    def one_window(w):
        scores = nt_dot(q_wide, kv_ref[w, :, :width]) * scale_dot
        scores = jnp.where(valid > 0.0, scores, neg_big)
        top = jnp.max(scores, axis=1, keepdims=True)
        if not fresh:
            before, total_before = stat_in[w, :, 0:1], stat_in[w, :, 1:2]
            top = jnp.maximum(top, before)
        weights = jnp.exp(scores - top)
        totals = jnp.sum(weights, axis=1, keepdims=True)
        accum = nn_dot(weights.astype(bf16), kv_ref[w, :, width:])
        if not fresh:
            fade = jnp.exp(before - top)
            totals = totals + total_before * fade
            accum = accum + acc_in[w] * fade
        if not last:
            acc_out[w] = accum
            stat_out[w, :, 0:1] = top
            stat_out[w, :, 1:2] = totals
        else:
            mixed = collect_heads(accum, heads)
            stats = jnp.zeros((mixed.shape[0], 128), f32)
            stats = columns_to_lanes(top, heads, 0, stats)
            stats = columns_to_lanes(totals, heads, heads, stats)
            each = mixed.shape[0] // NY
            for s, part_ref in enumerate(part_refs):
                part_ref[w, :, :width] = mixed[s * each : (s + 1) * each]
                part_ref[w, :, width:] = stats[s * each : (s + 1) * each]

    together = WUNROLL // count

    @pl.loop(0, windows // together)
    def _(k):
        for part in range(together):
            one_window(k * together + part)

    for part in range(PARTS):
        send(part).wait()


def absorb(messages, q, w_in, w_kv, table, state, last):
    count = len(messages)
    lat, width = q.shape
    con_dev = messages[0].shape[0]
    windows = (messages[0].shape[1] - 128) // PATCH
    rows = lat * (width // HD)
    fresh = state is None
    vmem = pl.BlockSpec(memory_space=pltpu.VMEM)
    operands = list(messages) + [q, w_in, w_kv, table]
    in_specs = [vmem] * len(operands)
    aliases = {}
    if not fresh:
        n = len(operands)
        operands += list(state)
        in_specs += [vmem, vmem]
        aliases = {} if last else {n: 2, n + 1: 3}
    acc = jax.ShapeDtypeStruct((windows, rows, width), f32)
    stat = jax.ShapeDtypeStruct((windows, rows, 128), f32)
    part = jax.ShapeDtypeStruct((windows, lat // NY, width + 128), f32)
    tail = [part] * NY if last else [acc, stat]
    return pl.pallas_call(
        functools.partial(absorb_kernel, fresh=fresh, last=last, count=count),
        in_specs=in_specs,
        out_specs=[pl.BlockSpec(memory_space=pltpu.HBM)] + [vmem] * (1 + len(tail)),
        out_shape=[
            pltpu.HBM((windows, count * con_dev, 2 * width), bf16),
            jax.ShapeDtypeStruct((8, count * con_dev), f32),
        ]
        + tail,
        scratch_shapes=[
            pltpu.VMEM((count * con_dev, width), f32),
            pltpu.VMEM((windows * count * con_dev, width), bf16),
            pltpu.VMEM((windows, count * con_dev, 2 * width), bf16),
            pltpu.SemaphoreType.DMA((PARTS,)),
        ],
        input_output_aliases=aliases,
        compiler_params=pltpu.CompilerParams(vmem_limit_bytes=VMEM_ABSORB * MIB),
        name="absorb",
    )(*operands)


def combine_kernel(*refs):
    *part_refs, att_ref, copies_ref, stats_ref = refs
    rows, width = att_ref.shape
    heads = width // HD
    lane = lax.broadcasted_iota(jnp.int32, (rows, 128), 1)
    parts = [ref[...].reshape(rows, width + 128) for ref in part_refs]
    top = parts[0][:, width:]
    for part in parts[1:]:
        top = jnp.maximum(top, part[:, width:])
    totals = jnp.zeros((rows, 128), f32)
    accum = jnp.zeros((rows, width), f32)
    for part in parts:
        factor = jnp.exp(jnp.where(lane < heads, part[:, width:] - top, 0.0))
        totals = totals + factor * pltpu.roll(part[:, width:], 128 - heads, 1)
        accum = accum + part[:, :width] * lanes_to_columns_wide(factor, heads, 0)
    totals = jnp.where(lane < heads, totals, 1.0)
    att = (accum / lanes_to_columns_wide(totals, heads, 0)).astype(bf16)
    att_ref[...] = att
    for t in range(NTM):
        copies_ref[t] = att
    stats_ref[...] = jnp.where(lane < heads, top, pltpu.roll(1.0 / totals, heads, 1))


def combine(parts):
    windows, each, wide = parts[0].shape
    rows = windows * each
    return pl.pallas_call(
        combine_kernel,
        out_shape=[
            jax.ShapeDtypeStruct((rows, wide - 128), bf16),
            jax.ShapeDtypeStruct((NTM, rows, wide - 128), bf16),
            jax.ShapeDtypeStruct((rows, 128), f32),
        ],
        compiler_params=pltpu.CompilerParams(vmem_limit_bytes=8 * MIB),
        name="combine_parts",
    )(*parts)


def conv_kernel(
    tm_ref, own_ref, all_ref, stats_ref, cl_ref, cot_ref, cr_ref,
    w_out_ref, bias_ref, conv_hbm, *refs,
):
    n = (len(refs) - 6) // 2
    kv_hbms, (feat_ref, msg_ref), kv_refs = refs[:n], refs[n : n + 2], refs[n + 2 : 2 * n + 2]
    ext_ref, conv_ref, sem, kv_sem = refs[2 * n + 2 :]
    fetches = [pltpu.make_async_copy(kv_hbms[i].at[0], kv_refs[i], kv_sem.at[i]) for i in range(n)]
    weights = [pltpu.make_async_copy(conv_hbm.at[l], conv_ref.at[l], sem.at[l]) for l in range(LAYERS)]
    for copy in weights:
        copy.start()
    rows, width = own_ref.shape
    heads = width // HD
    windows = 4
    each = rows // windows
    reach = 6
    first = tm_ref[0] * windows - reach
    total_windows = NTM * windows

    def inside(lo, count):
        w = lax.broadcasted_iota(jnp.int32, (count * each, width), 0) // each + (first + lo)
        return jnp.logical_and(w >= 0, w < total_windows)

    side = reach * each
    ext_ref[:side, :] = jnp.zeros((side, width), f32)
    ext_ref[side : side + NTM * rows, :] = all_ref[...].astype(f32)
    ext_ref[side + NTM * rows :, :] = jnp.zeros((side, width), f32)
    att = ext_ref[pl.ds(pl.multiple_of(tm_ref[0] * rows, rows), 2 * side + rows), :]
    w_out = w_out_ref[...]
    x0 = rounded(nn_dot(att.astype(bf16), w_out))
    n0 = 14 * each
    weights[0].wait()
    pre0 = bias_ref[0:1, :] + sum(nn_dot(x0[j * each : j * each + n0].astype(bf16), conv_ref[0, j]) for j in range(KSIZE))
    x1 = rounded(x0[each : each + n0] + jax.nn.silu(pre0))
    x1 = jnp.where(inside(1, 14), x1, 0.0)
    n1 = 10 * each
    weights[1].wait()
    for copy in fetches:
        copy.start()
    pre1 = bias_ref[1:2, :] + sum(nn_dot(x1[2 * j * each : 2 * j * each + n1].astype(bf16), conv_ref[1, j]) for j in range(KSIZE))
    feat_ref[...] = (x1[5 * each : 9 * each] + jax.nn.silu(pre1[3 * each : 7 * each])).astype(bf16)
    g2 = jnp.concatenate([r[...].astype(f32) for r in (cl_ref, cot_ref, cr_ref)], axis=0)
    gpre1 = rounded(g2 * silu_slope(pre1))
    n2 = 6 * each
    g1 = g2[2 * each : 8 * each] + sum(
        nt_dot(gpre1[(4 - 2 * j) * each : (4 - 2 * j) * each + n2].astype(bf16), conv_ref[1, j]) for j in range(KSIZE)
    )
    gpre0 = rounded(g1 * silu_slope(pre0[4 * each : 10 * each]))
    gpre0 = jnp.where(inside(5, 6), gpre0, 0.0)
    g0 = g1[each : 5 * each] + sum(
        nt_dot(gpre0[(2 - j) * each : (2 - j) * each + rows].astype(bf16), conv_ref[0, j]) for j in range(KSIZE)
    )
    grad_att = rounded(nt_dot(g0.astype(bf16), w_out))
    msg_ref[:, :width] = grad_att.astype(bf16)
    product = grad_att * own_ref[...].astype(f32)
    head = head_of_lane((rows, width))
    lane = lax.broadcasted_iota(jnp.int32, (rows, 128), 1)
    stats = stats_ref[...]
    for h in range(heads):
        delta = jnp.sum(jnp.where(head == h, product, 0.0), axis=1, keepdims=True)
        stats = jnp.where(lane == 2 * heads + h, delta, stats)
    stats = jnp.where(lane < 3 * heads, stats, 0.0)
    high = rounded(stats)
    middle = rounded(stats - high)
    low = (stats - high) - middle
    for copy in fetches:
        copy.wait()
    msg_ref[:, width:] = (high + pltpu.roll(middle, 32, 1) + pltpu.roll(low, 64, 1)).astype(bf16)


def conv_stack(tm, own, everyone, stats, cots, w_out, conv_weight, conv_bias, kvs):
    rows, width = own.shape
    cl, cot, cr = cots
    vmem = pl.BlockSpec(memory_space=pltpu.VMEM)
    return pl.pallas_call(
        conv_kernel,
        in_specs=[pl.BlockSpec(memory_space=pltpu.SMEM)]
        + [vmem] * 8
        + [pl.BlockSpec(memory_space=pltpu.HBM)] * (1 + len(kvs)),
        out_specs=[vmem] * (2 + len(kvs)),
        out_shape=[
            jax.ShapeDtypeStruct((rows, width), bf16),
            jax.ShapeDtypeStruct((rows, width + 128), bf16),
        ]
        + [pltpu.VMEM(kv.shape[1:], kv.dtype) for kv in kvs],
        scratch_shapes=[
            pltpu.VMEM(((NTM + 3) * rows, width), f32),
            pltpu.VMEM(conv_weight.shape, conv_weight.dtype),
            pltpu.SemaphoreType.DMA((LAYERS,)),
            pltpu.SemaphoreType.DMA((len(kvs),)),
        ],
        compiler_params=pltpu.CompilerParams(vmem_limit_bytes=20 * MIB),
        name="conv_stack",
    )(tm, own, everyone, stats, cl, cot, cr, w_out, conv_bias, *(pltpu.with_memory_space_constraint(a, pltpu.HBM) for a in (conv_weight, *kvs)))


def backward_kernel(y_ref, q_ref, *refs, slots):
    msg_refs, refs = refs[:slots], refs[slots:]
    n = (len(refs) - 3) // 4
    first_refs, valid_refs, kv_hbms = refs[:n], refs[n : 2 * n], refs[2 * n : 3 * n]
    dq_ref, acc_ref, *kv_refs, sem = refs[3 * n :]
    width = q_ref.shape[1]
    heads = width // HD
    windows = msg_refs[0].shape[0]

    def fetch(window, i):
        return pltpu.make_async_copy(kv_hbms[i].at[window], kv_refs[i].at[window - 1], sem.at[window - 1, i])

    for window in range(1, windows):
        for i in range(n):
            fetch(window, i).start()

    def one_window(window, blocks):
        msg = jnp.concatenate([r[window].astype(f32) for r in msg_refs], axis=0)
        terms = msg[:, width:]
        stats = terms + pltpu.roll(terms, 96, 1) + pltpu.roll(terms, 64, 1)
        top = lanes_to_column(stats, heads, 0)
        inverse = lanes_to_column(stats, heads, heads)
        delta = lanes_to_column(stats, heads, 2 * heads)
        grad_wide = spread_heads(msg[:, :width].astype(bf16), heads)
        q_wide = spread_heads(q_ref[...], heads)
        accum = 0.0
        for block, valid_ref in zip(blocks, valid_refs):
            key_rows = block[:, :width]
            scores = nt_dot(q_wide, key_rows) * scale_dot
            scores = jnp.where(valid_ref[0:1, :] > 0.0, scores, neg_big)
            prob = jnp.exp(scores - top) * inverse
            grad_prob = nt_dot(grad_wide, block[:, width:])
            dscore = (prob * (grad_prob - delta)).astype(bf16)
            accum = accum + nn_dot(dscore, key_rows)
        return accum

    acc_ref[...] = one_window(0, first_refs)

    @pl.loop(1, windows)
    def _(window):
        for i in range(n):
            fetch(window, i).wait()
        acc_ref[...] = acc_ref[...] + one_window(window, [ref.at[window - 1] for ref in kv_refs])

    dq = collect_heads(acc_ref[...], heads) * scale_dot
    each = dq.shape[0] // slots
    for s in range(slots):
        place = pl.multiple_of(((y_ref[0] + (slots - s)) % slots) * each, each)
        dq_ref[pl.ds(place, each), :] = dq[s * each : (s + 1) * each]


def backward_attention(y, kvs, first, valids, q, msgs):
    lat, width = q.shape
    heads = width // HD
    vmem = pl.BlockSpec(memory_space=pltpu.VMEM)
    kvs = [pltpu.with_memory_space_constraint(kv, pltpu.HBM) for kv in kvs]
    return pl.pallas_call(
        functools.partial(backward_kernel, slots=len(msgs)),
        in_specs=[pl.BlockSpec(memory_space=pltpu.SMEM)]
        + [vmem] * (1 + len(msgs) + len(first) + len(valids))
        + [pl.BlockSpec(memory_space=pltpu.HBM)] * len(kvs),
        out_specs=vmem,
        out_shape=jax.ShapeDtypeStruct((lat, width), f32),
        scratch_shapes=[pltpu.VMEM((lat * heads, width), f32)]
        + [pltpu.VMEM((kv.shape[0] - 1,) + kv.shape[1:], kv.dtype) for kv in kvs]
        + [pltpu.SemaphoreType.DMA((kvs[0].shape[0] - 1, len(kvs)))],
        compiler_params=pltpu.CompilerParams(vmem_limit_bytes=VMEM_BACK * MIB),
        name="backward_attention",
    )(y, q, *msgs, *first, *valids, *kvs)


def shift(count, by):
    return [(i, (i + by) % count) for i in range(count)]


def local(
    signal, pos_idx, live_count, latents, pos_table, w_in, w_kv, w_query, w_out,
    conv_weight, conv_bias, cotangent,
):
    con_dev = signal.shape[0]
    pat_dev = signal.shape[1] // PATCH
    width = w_query.shape[0]
    lat_rows = latents.shape[0]
    y, z, tm = (lax.axis_index(a) for a in ("y", "z", "tm"))
    lat_dev = lat_rows // (NY * NZ)
    up1 = [(i, i + 1) for i in range(NTM - 1)]
    down1 = [(i + 1, i) for i in range(NTM - 1)]

    own = make_message(live_count, signal, pos_idx)
    queries, table, kv_weights, in_weights = prepare(
        y.reshape(1), z.reshape(1), pos_table, w_kv, w_in, latents, w_query
    )

    def absorbed(messages, state, last=False):
        return absorb(messages, queries, in_weights, kv_weights, table, state, last)

    below, above = own, own
    at_hand, state, kvs, valids = [own], None, [], []
    for step in range(1, NZ // 2 + 1):
        below = lax.ppermute(below, "z", shift(NZ, 1))
        if step < NZ // 2:
            above = lax.ppermute(above, "z", shift(NZ, -1))
        kv, valid, *state = absorbed(at_hand, state)
        kvs.append(kv)
        valids.append(valid)
        if step < NZ // 2:
            below, above, valids[-1] = lax.optimization_barrier((below, above, valids[-1]))
        at_hand = [below, above] if step < NZ // 2 else [below]
    kv, valid, *parts = absorbed(at_hand, state, last=True)
    kvs.append(kv)
    valids.append(valid)

    received = [lax.ppermute(parts[s], "y", shift(NY, -s)) for s in range(1, NY)]

    cot = cotangent.reshape(pat_dev * lat_dev, width)
    cot_late, cot_early, _ = lax.optimization_barrier((cot[lat_dev:], cot[: 3 * lat_dev], parts[0]))
    cot_left = lax.ppermute(cot_late, "tm", up1)
    cot_right = lax.ppermute(cot_early, "tm", down1)

    att, copies, stats = combine([parts[0]] + received)

    everyone = lax.all_to_all(copies, "tm", 0, 0)
    features, msg, *first = conv_stack(
        tm.reshape(1), att, everyone.reshape(-1, width), stats,
        (cot_left, cot, cot_right), w_out, conv_weight, conv_bias, kvs,
    )

    msg = msg.reshape(pat_dev, lat_dev, width + 128)
    msgs = [msg] + [lax.ppermute(msg, "y", shift(NY, s)) for s in range(1, NY)]
    dq = backward_attention(y.reshape(1), kvs, first, valids, queries, msgs)

    pieces = lax.all_to_all(dq, ("y", "tm"), 0, 0, tiled=True)
    dq_row = jnp.sum(pieces, axis=0, keepdims=True).astype(bf16)
    spread = jnp.broadcast_to(dq_row.reshape(1, width // 128, 128), (lat_rows, width // 128, 128))
    dq_all = lax.all_to_all(spread, ("y", "z", "tm"), 0, 0, tiled=True)
    d_latents = nt_dot(dq_all.reshape(lat_rows, width), w_query)
    return features.reshape(pat_dev, lat_dev, width), d_latents


def solution(mesh):
    split = Mesh(mesh.devices.reshape(NY, NZ, NTM), ("y", "z", "tm"))
    contacts = ("y", "z")
    in_specs = (P(contacts, "tm"), P(contacts), P(contacts)) + (P(),) * 8 + (P("tm", contacts, None),)
    out_specs = (P("tm", contacts, None), P())
    return jax.shard_map(local, mesh=split, in_specs=in_specs, out_specs=out_specs, check_vma=False)
```

```python
import functools

import jax
import jax.numpy as jnp
from jax import lax
from jax.experimental import pallas as pl
from jax.experimental.pallas import tpu as pltpu
from jax.sharding import Mesh
from jax.sharding import PartitionSpec as P

HD = 64
PATCH = 32
KSIZE = 3
LAYERS = 2

neg_big = -1e30
scale_dot = 0.125

bf16 = jnp.bfloat16
f32 = jnp.float32

NY, NZ, NTM = 4, 8, 8
MIB = 1 << 20
PIECE, PARTS, HALVES, VMEM_ABSORB = 2048, 2, 2, 28
WUNROLL, VMEM_BACK = 4, 40


def nt_dot(a, b):
    return lax.dot_general(a, b, (((1,), (1,)), ((), ())), preferred_element_type=f32)


def nn_dot(a, b):
    return jnp.dot(a, b, preferred_element_type=f32)


def head_of_lane(shape):
    return lax.broadcasted_iota(jnp.int32, shape, len(shape) - 1) // HD


def spread_heads(rows, heads):
    head = head_of_lane(rows.shape)
    zero = jnp.zeros_like(rows)
    return jnp.concatenate([jnp.where(head == h, rows, zero) for h in range(heads)], axis=0)


def collect_heads(blocks, heads):
    r = blocks.shape[0] // heads
    head = head_of_lane((r, blocks.shape[1]))
    out = blocks[:r]
    for h in range(1, heads):
        out = jnp.where(head == h, blocks[h * r : (h + 1) * r], out)
    return out


def columns_to_lanes(column, heads, first, base):
    r = base.shape[0]
    lane = lax.broadcasted_iota(jnp.int32, base.shape, 1)
    for h in range(heads):
        base = jnp.where(lane == first + h, column[h * r : (h + 1) * r], base)
    return base


def lanes_to_column(stats, heads, first):
    return jnp.concatenate([stats[:, first + h : first + h + 1] for h in range(heads)], axis=0)


def lanes_to_columns_wide(stats, heads, first):
    r = stats.shape[0]
    head = head_of_lane((r, heads * HD))
    out = jnp.broadcast_to(stats[:, first : first + 1], (r, heads * HD))
    for h in range(1, heads):
        out = jnp.where(head == h, stats[:, first + h : first + h + 1], out)
    return out


def silu_slope(pre_act):
    sigmoid_v = jax.nn.sigmoid(pre_act)
    return sigmoid_v * (1.0 + pre_act * (1.0 - sigmoid_v))


def rounded(value):
    return value.astype(bf16).astype(f32)


def message_kernel(live_ref, signal_hbm, index_hbm, message_ref, signal_ref, index_ref, sem):
    con_dev, span = signal_hbm.shape
    copies = [
        pltpu.make_async_copy(index_hbm, index_ref, sem.at[0]),
        pltpu.make_async_copy(signal_hbm, signal_ref, sem.at[1]),
    ]
    for copy in copies:
        copy.start()
    copies[0].wait()
    index = index_ref[...].astype(f32)
    for r in range(con_dev // 128):
        column = jnp.transpose(jnp.broadcast_to(index[r : r + 1], (128, 128)))
        high = jnp.floor(column * (1.0 / 64.0))
        lane = lax.broadcasted_iota(jnp.int32, column.shape, 1)
        meta = jnp.where(lane == 0, high, jnp.where(lane == 1, column - 64.0 * high, live_ref[0].astype(f32)))
        message_ref[r * 128 : (r + 1) * 128, span:] = meta.astype(bf16)
    copies[1].wait()
    message_ref[:, :span] = signal_ref[...]


def make_message(live_count, signal, pos_idx):
    con_dev, span = signal.shape
    index = pos_idx.reshape(con_dev // 128, 128)
    signal, index = (pltpu.with_memory_space_constraint(a, pltpu.HBM) for a in (signal, index))
    hbm = pl.BlockSpec(memory_space=pltpu.HBM)
    return pl.pallas_call(
        message_kernel,
        in_specs=[pl.BlockSpec(memory_space=pltpu.SMEM), hbm, hbm],
        out_specs=pl.BlockSpec(memory_space=pltpu.VMEM),
        out_shape=jax.ShapeDtypeStruct((con_dev, span + 128), bf16),
        scratch_shapes=[
            pltpu.VMEM(signal.shape, signal.dtype),
            pltpu.VMEM(index.shape, index.dtype),
            pltpu.SemaphoreType.DMA((2,)),
        ],
        compiler_params=pltpu.CompilerParams(vmem_limit_bytes=8 * MIB),
        name="make_message",
    )(live_count, signal, index)


def prepare_kernel(y_ref, z_ref, *refs):
    hbms, (q_ref, *here), sem = refs[:5], refs[5:11], refs[11]
    latents_ref, w_query_ref = here[3], here[4]
    copies = [pltpu.make_async_copy(a, b, sem.at[i]) for i, (a, b) in enumerate(zip(hbms, here))]
    for i in (3, 4, 0, 1, 2):
        copies[i].start()
    lat, each = latents_ref.shape[0], latents_ref.shape[0] // (NY * NZ)
    row = lax.broadcasted_iota(jnp.int32, (q_ref.shape[0], lat), 0)
    owner = (y_ref[0] + NY - row // each) % NY
    place = (owner * NZ + z_ref[0]) * each + row % each
    pick = jnp.where(lax.broadcasted_iota(jnp.int32, row.shape, 1) == place, 1.0, 0.0).astype(bf16)
    copies[3].wait()
    chosen = nn_dot(pick, latents_ref[...]).astype(bf16)
    copies[4].wait()
    q_ref[...] = nn_dot(chosen, w_query_ref[...]).astype(bf16)
    for copy in copies[:3]:
        copy.wait()


def prepare(y, z, table, w_kv, w_in, latents, w_query):
    smem, vmem = pl.BlockSpec(memory_space=pltpu.SMEM), pl.BlockSpec(memory_space=pltpu.VMEM)
    arrays = [pltpu.with_memory_space_constraint(a, pltpu.HBM) for a in (table, w_kv, w_in, latents, w_query)]
    return pl.pallas_call(
        prepare_kernel,
        in_specs=[smem] * 2 + [pl.BlockSpec(memory_space=pltpu.HBM)] * 5,
        out_specs=[vmem] * 4,
        out_shape=[jax.ShapeDtypeStruct((latents.shape[0] // NZ, w_query.shape[1]), bf16)]
        + [pltpu.VMEM(a.shape, a.dtype) for a in (table, w_kv, w_in)],
        scratch_shapes=[pltpu.VMEM(a.shape, a.dtype) for a in (latents, w_query)]
        + [pltpu.SemaphoreType.DMA((5,))],
        compiler_params=pltpu.CompilerParams(vmem_limit_bytes=8 * MIB),
        name="prepare",
    )(y, z, *arrays)


def absorb_kernel(*refs, fresh, last, count):
    refs = list(refs)
    messages = [refs.pop(0) for _ in range(count)]
    q_ref, w_in_ref, w_kv_ref, table_ref = (refs.pop(0) for _ in range(4))
    if not fresh:
        acc_in, stat_in = refs.pop(0), refs.pop(0)
    kv_hbm, valid_ref = refs.pop(0), refs.pop(0)
    if last:
        part_refs = [refs.pop(0) for _ in range(NY)]
    else:
        acc_out, stat_out = refs.pop(0), refs.pop(0)
    pos_ref, tok_ref, kv_ref, sem = refs
    width = q_ref.shape[1]
    heads = width // HD
    con_dev, span = messages[0].shape[0], messages[0].shape[1] - 128
    windows = span // PATCH
    rows = count * con_dev
    message = jnp.concatenate([m[...] for m in messages], axis=0)
    sig = message[:, :span]
    meta = message[:, span:].astype(f32)
    idx = meta[:, 0:1] * 64.0 + meta[:, 1:2]
    lane = lax.broadcasted_iota(jnp.int32, (1, con_dev), 1).astype(f32)
    valid = jnp.concatenate(
        [jnp.where(lane < meta[c * con_dev : c * con_dev + 1, 2:3], 1.0, 0.0) for c in range(count)], axis=1
    )
    valid_ref[...] = jnp.broadcast_to(valid, valid_ref.shape)
    piece = PIECE
    ids = lax.broadcasted_iota(jnp.int32, (rows, piece), 1).astype(f32)
    pos_ref[...] = jnp.zeros_like(pos_ref)

    @pl.loop(0, table_ref.shape[0] // piece)
    def _(k):
        start = pl.multiple_of(k * piece, piece)
        hot = jnp.where(ids == idx - start.astype(f32), 1.0, 0.0).astype(bf16)
        pos_ref[...] = pos_ref[...] + nn_dot(hot, table_ref[pl.ds(start, piece), :])

    tall = jnp.concatenate([w_in_ref[...]] * windows, axis=0)
    band = lax.broadcasted_iota(jnp.int32, sig.shape, 1) // PATCH
    for w in range(windows):
        embedded = nn_dot(jnp.where(band == w, sig, jnp.zeros_like(sig)), tall)
        tok_ref[w * rows : (w + 1) * rows, :] = (embedded + pos_ref[...]).astype(bf16)
    ws = windows // PARTS

    def send(part):
        here = pl.ds(part * ws, ws)
        return pltpu.make_async_copy(kv_ref.at[here], kv_hbm.at[here], sem.at[part])

    def project(part):
        tokens = tok_ref[pl.ds(pl.multiple_of(part * ws * rows, ws * rows), ws * rows), :]
        for half in range(HALVES):
            cols = slice(half * 2 * width // HALVES, (half + 1) * 2 * width // HALVES)
            keyval = nn_dot(tokens, w_kv_ref[:, cols]).astype(bf16)
            kv_ref[pl.ds(part * ws, ws), :, cols] = keyval.reshape(ws, rows, 2 * width // HALVES)
        send(part).start()

    if count == 1:
        for part in range(PARTS):
            project(part)
    else:
        pl.loop(0, PARTS)(project)
    q_wide = spread_heads(q_ref[...], heads)

    def one_window(w):
        scores = nt_dot(q_wide, kv_ref[w, :, :width]) * scale_dot
        scores = jnp.where(valid > 0.0, scores, neg_big)
        top = jnp.max(scores, axis=1, keepdims=True)
        if not fresh:
            before, total_before = stat_in[w, :, 0:1], stat_in[w, :, 1:2]
            top = jnp.maximum(top, before)
        weights = jnp.exp(scores - top)
        totals = jnp.sum(weights, axis=1, keepdims=True)
        accum = nn_dot(weights.astype(bf16), kv_ref[w, :, width:])
        if not fresh:
            fade = jnp.exp(before - top)
            totals = totals + total_before * fade
            accum = accum + acc_in[w] * fade
        if not last:
            acc_out[w] = accum
            stat_out[w, :, 0:1] = top
            stat_out[w, :, 1:2] = totals
        else:
            mixed = collect_heads(accum, heads)
            stats = jnp.zeros((mixed.shape[0], 128), f32)
            stats = columns_to_lanes(top, heads, 0, stats)
            stats = columns_to_lanes(totals, heads, heads, stats)
            each = mixed.shape[0] // NY
            for s, part_ref in enumerate(part_refs):
                part_ref[w, :, :width] = mixed[s * each : (s + 1) * each]
                part_ref[w, :, width:] = stats[s * each : (s + 1) * each]

    together = WUNROLL // count

    @pl.loop(0, windows // together)
    def _(k):
        for part in range(together):
            one_window(k * together + part)

    for part in range(PARTS):
        send(part).wait()


def absorb(messages, q, w_in, w_kv, table, state, last):
    count = len(messages)
    lat, width = q.shape
    con_dev = messages[0].shape[0]
    windows = (messages[0].shape[1] - 128) // PATCH
    rows = lat * (width // HD)
    fresh = state is None
    vmem = pl.BlockSpec(memory_space=pltpu.VMEM)
    operands = list(messages) + [q, w_in, w_kv, table]
    in_specs = [vmem] * len(operands)
    aliases = {}
    if not fresh:
        n = len(operands)
        operands += list(state)
        in_specs += [vmem, vmem]
        aliases = {} if last else {n: 2, n + 1: 3}
    acc = jax.ShapeDtypeStruct((windows, rows, width), f32)
    stat = jax.ShapeDtypeStruct((windows, rows, 128), f32)
    part = jax.ShapeDtypeStruct((windows, lat // NY, width + 128), f32)
    tail = [part] * NY if last else [acc, stat]
    return pl.pallas_call(
        functools.partial(absorb_kernel, fresh=fresh, last=last, count=count),
        in_specs=in_specs,
        out_specs=[pl.BlockSpec(memory_space=pltpu.HBM)] + [vmem] * (1 + len(tail)),
        out_shape=[
            pltpu.HBM((windows, count * con_dev, 2 * width), bf16),
            jax.ShapeDtypeStruct((8, count * con_dev), f32),
        ]
        + tail,
        scratch_shapes=[
            pltpu.VMEM((count * con_dev, width), f32),
            pltpu.VMEM((windows * count * con_dev, width), bf16),
            pltpu.VMEM((windows, count * con_dev, 2 * width), bf16),
            pltpu.SemaphoreType.DMA((PARTS,)),
        ],
        input_output_aliases=aliases,
        compiler_params=pltpu.CompilerParams(vmem_limit_bytes=VMEM_ABSORB * MIB),
        name="absorb",
    )(*operands)


def combine_kernel(*refs):
    *part_refs, att_ref, copies_ref, stats_ref = refs
    rows, width = att_ref.shape
    heads = width // HD
    lane = lax.broadcasted_iota(jnp.int32, (rows, 128), 1)
    parts = [ref[...].reshape(rows, width + 128) for ref in part_refs]
    top = parts[0][:, width:]
    for part in parts[1:]:
        top = jnp.maximum(top, part[:, width:])
    totals = jnp.zeros((rows, 128), f32)
    accum = jnp.zeros((rows, width), f32)
    for part in parts:
        factor = jnp.exp(jnp.where(lane < heads, part[:, width:] - top, 0.0))
        totals = totals + factor * pltpu.roll(part[:, width:], 128 - heads, 1)
        accum = accum + part[:, :width] * lanes_to_columns_wide(factor, heads, 0)
    totals = jnp.where(lane < heads, totals, 1.0)
    att = (accum / lanes_to_columns_wide(totals, heads, 0)).astype(bf16)
    att_ref[...] = att
    for t in range(NTM):
        copies_ref[t] = att
    stats_ref[...] = jnp.where(lane < heads, top, pltpu.roll(1.0 / totals, heads, 1))


def combine(parts):
    windows, each, wide = parts[0].shape
    rows = windows * each
    return pl.pallas_call(
        combine_kernel,
        out_shape=[
            jax.ShapeDtypeStruct((rows, wide - 128), bf16),
            jax.ShapeDtypeStruct((NTM, rows, wide - 128), bf16),
            jax.ShapeDtypeStruct((rows, 128), f32),
        ],
        compiler_params=pltpu.CompilerParams(vmem_limit_bytes=8 * MIB),
        name="combine_parts",
    )(*parts)


def conv_kernel(
    tm_ref, own_ref, all_ref, stats_ref, cl_ref, cot_ref, cr_ref,
    w_out_ref, bias_ref, conv_hbm, *refs,
):
    n = (len(refs) - 6) // 2
    kv_hbms, (feat_ref, msg_ref), kv_refs = refs[:n], refs[n : n + 2], refs[n + 2 : 2 * n + 2]
    ext_ref, conv_ref, sem, kv_sem = refs[2 * n + 2 :]
    fetches = [pltpu.make_async_copy(kv_hbms[i].at[0], kv_refs[i], kv_sem.at[i]) for i in range(n)]
    weights = [pltpu.make_async_copy(conv_hbm.at[l], conv_ref.at[l], sem.at[l]) for l in range(LAYERS)]
    for copy in weights:
        copy.start()
    rows, width = own_ref.shape
    heads = width // HD
    windows = 4
    each = rows // windows
    reach = 6
    first = tm_ref[0] * windows - reach
    total_windows = NTM * windows

    def inside(lo, count):
        w = lax.broadcasted_iota(jnp.int32, (count * each, width), 0) // each + (first + lo)
        return jnp.logical_and(w >= 0, w < total_windows)

    side = reach * each
    ext_ref[:side, :] = jnp.zeros((side, width), f32)
    ext_ref[side : side + NTM * rows, :] = all_ref[...].astype(f32)
    ext_ref[side + NTM * rows :, :] = jnp.zeros((side, width), f32)
    att = ext_ref[pl.ds(pl.multiple_of(tm_ref[0] * rows, rows), 2 * side + rows), :]
    w_out = w_out_ref[...]
    x0 = rounded(nn_dot(att.astype(bf16), w_out))
    n0 = 14 * each
    weights[0].wait()
    pre0 = bias_ref[0:1, :] + sum(nn_dot(x0[j * each : j * each + n0].astype(bf16), conv_ref[0, j]) for j in range(KSIZE))
    x1 = rounded(x0[each : each + n0] + jax.nn.silu(pre0))
    x1 = jnp.where(inside(1, 14), x1, 0.0)
    n1 = 10 * each
    weights[1].wait()
    for copy in fetches:
        copy.start()
    pre1 = bias_ref[1:2, :] + sum(nn_dot(x1[2 * j * each : 2 * j * each + n1].astype(bf16), conv_ref[1, j]) for j in range(KSIZE))
    feat_ref[...] = (x1[5 * each : 9 * each] + jax.nn.silu(pre1[3 * each : 7 * each])).astype(bf16)
    g2 = jnp.concatenate([r[...].astype(f32) for r in (cl_ref, cot_ref, cr_ref)], axis=0)
    gpre1 = rounded(g2 * silu_slope(pre1))
    n2 = 6 * each
    g1 = g2[2 * each : 8 * each] + sum(
        nt_dot(gpre1[(4 - 2 * j) * each : (4 - 2 * j) * each + n2].astype(bf16), conv_ref[1, j]) for j in range(KSIZE)
    )
    gpre0 = rounded(g1 * silu_slope(pre0[4 * each : 10 * each]))
    gpre0 = jnp.where(inside(5, 6), gpre0, 0.0)
    g0 = g1[each : 5 * each] + sum(
        nt_dot(gpre0[(2 - j) * each : (2 - j) * each + rows].astype(bf16), conv_ref[0, j]) for j in range(KSIZE)
    )
    grad_att = rounded(nt_dot(g0.astype(bf16), w_out))
    msg_ref[:, :width] = grad_att.astype(bf16)
    product = grad_att * own_ref[...].astype(f32)
    head = head_of_lane((rows, width))
    lane = lax.broadcasted_iota(jnp.int32, (rows, 128), 1)
    stats = stats_ref[...]
    for h in range(heads):
        delta = jnp.sum(jnp.where(head == h, product, 0.0), axis=1, keepdims=True)
        stats = jnp.where(lane == 2 * heads + h, delta, stats)
    stats = jnp.where(lane < 3 * heads, stats, 0.0)
    high = rounded(stats)
    middle = rounded(stats - high)
    low = (stats - high) - middle
    for copy in fetches:
        copy.wait()
    msg_ref[:, width:] = (high + pltpu.roll(middle, 32, 1) + pltpu.roll(low, 64, 1)).astype(bf16)


def conv_stack(tm, own, everyone, stats, cots, w_out, conv_weight, conv_bias, kvs):
    rows, width = own.shape
    cl, cot, cr = cots
    vmem = pl.BlockSpec(memory_space=pltpu.VMEM)
    return pl.pallas_call(
        conv_kernel,
        in_specs=[pl.BlockSpec(memory_space=pltpu.SMEM)]
        + [vmem] * 8
        + [pl.BlockSpec(memory_space=pltpu.HBM)] * (1 + len(kvs)),
        out_specs=[vmem] * (2 + len(kvs)),
        out_shape=[
            jax.ShapeDtypeStruct((rows, width), bf16),
            jax.ShapeDtypeStruct((rows, width + 128), bf16),
        ]
        + [pltpu.VMEM(kv.shape[1:], kv.dtype) for kv in kvs],
        scratch_shapes=[
            pltpu.VMEM(((NTM + 3) * rows, width), f32),
            pltpu.VMEM(conv_weight.shape, conv_weight.dtype),
            pltpu.SemaphoreType.DMA((LAYERS,)),
            pltpu.SemaphoreType.DMA((len(kvs),)),
        ],
        compiler_params=pltpu.CompilerParams(vmem_limit_bytes=20 * MIB),
        name="conv_stack",
    )(tm, own, everyone, stats, cl, cot, cr, w_out, conv_bias, *(pltpu.with_memory_space_constraint(a, pltpu.HBM) for a in (conv_weight, *kvs)))


def backward_kernel(y_ref, q_ref, *refs, slots):
    msg_refs, refs = refs[:slots], refs[slots:]
    n = (len(refs) - 3) // 4
    first_refs, valid_refs, kv_hbms = refs[:n], refs[n : 2 * n], refs[2 * n : 3 * n]
    dq_ref, acc_ref, *kv_refs, sem = refs[3 * n :]
    width = q_ref.shape[1]
    heads = width // HD
    windows = msg_refs[0].shape[0]

    def fetch(window, i):
        return pltpu.make_async_copy(kv_hbms[i].at[window], kv_refs[i].at[window - 1], sem.at[window - 1, i])

    for window in range(1, windows):
        for i in range(n):
            fetch(window, i).start()

    def one_window(window, blocks):
        msg = jnp.concatenate([r[window].astype(f32) for r in msg_refs], axis=0)
        terms = msg[:, width:]
        stats = terms + pltpu.roll(terms, 96, 1) + pltpu.roll(terms, 64, 1)
        top = lanes_to_column(stats, heads, 0)
        inverse = lanes_to_column(stats, heads, heads)
        delta = lanes_to_column(stats, heads, 2 * heads)
        grad_wide = spread_heads(msg[:, :width].astype(bf16), heads)
        q_wide = spread_heads(q_ref[...], heads)
        accum = 0.0
        for block, valid_ref in zip(blocks, valid_refs):
            key_rows = block[:, :width]
            scores = nt_dot(q_wide, key_rows) * scale_dot
            scores = jnp.where(valid_ref[0:1, :] > 0.0, scores, neg_big)
            prob = jnp.exp(scores - top) * inverse
            grad_prob = nt_dot(grad_wide, block[:, width:])
            dscore = (prob * (grad_prob - delta)).astype(bf16)
            accum = accum + nn_dot(dscore, key_rows)
        return accum

    acc_ref[...] = one_window(0, first_refs)

    @pl.loop(1, windows)
    def _(window):
        for i in range(n):
            fetch(window, i).wait()
        acc_ref[...] = acc_ref[...] + one_window(window, [ref.at[window - 1] for ref in kv_refs])

    dq = collect_heads(acc_ref[...], heads) * scale_dot
    each = dq.shape[0] // slots
    for s in range(slots):
        place = pl.multiple_of(((y_ref[0] + (slots - s)) % slots) * each, each)
        dq_ref[pl.ds(place, each), :] = dq[s * each : (s + 1) * each]


def backward_attention(y, kvs, first, valids, q, msgs):
    lat, width = q.shape
    heads = width // HD
    vmem = pl.BlockSpec(memory_space=pltpu.VMEM)
    kvs = [pltpu.with_memory_space_constraint(kv, pltpu.HBM) for kv in kvs]
    return pl.pallas_call(
        functools.partial(backward_kernel, slots=len(msgs)),
        in_specs=[pl.BlockSpec(memory_space=pltpu.SMEM)]
        + [vmem] * (1 + len(msgs) + len(first) + len(valids))
        + [pl.BlockSpec(memory_space=pltpu.HBM)] * len(kvs),
        out_specs=vmem,
        out_shape=jax.ShapeDtypeStruct((lat, width), f32),
        scratch_shapes=[pltpu.VMEM((lat * heads, width), f32)]
        + [pltpu.VMEM((kv.shape[0] - 1,) + kv.shape[1:], kv.dtype) for kv in kvs]
        + [pltpu.SemaphoreType.DMA((kvs[0].shape[0] - 1, len(kvs)))],
        compiler_params=pltpu.CompilerParams(vmem_limit_bytes=VMEM_BACK * MIB),
        name="backward_attention",
    )(y, q, *msgs, *first, *valids, *kvs)


def shift(count, by):
    return [(i, (i + by) % count) for i in range(count)]


def local(
    signal, pos_idx, live_count, latents, pos_table, w_in, w_kv, w_query, w_out,
    conv_weight, conv_bias, cotangent,
):
    pat_dev = signal.shape[1] // PATCH
    width = w_query.shape[0]
    lat_rows = latents.shape[0]
    y, z, tm = (lax.axis_index(a) for a in ("y", "z", "tm"))
    lat_dev = lat_rows // (NY * NZ)
    up1 = [(i, i + 1) for i in range(NTM - 1)]
    down1 = [(i + 1, i) for i in range(NTM - 1)]

    own = make_message(live_count, signal, pos_idx)
    own, y_one = lax.optimization_barrier((own, y.reshape(1)))
    below = lax.ppermute(own, "z", shift(NZ, 1))
    queries, table, kv_weights, in_weights = prepare(y_one, z.reshape(1), pos_table, w_kv, w_in, latents, w_query)
    own_again, queries = lax.optimization_barrier((own, queries))

    def absorbed(messages, state, last=False):
        return absorb(messages, queries, in_weights, kv_weights, table, state, last)

    above = own_again
    at_hand, state, kvs, valids = [own], None, [], []
    for step in range(1, NZ // 2 + 1):
        if step > 1:
            below = lax.ppermute(below, "z", shift(NZ, 1))
        if step < NZ // 2:
            above = lax.ppermute(above, "z", shift(NZ, -1))
        kv, valid, *state = absorbed(at_hand, state)
        kvs.append(kv)
        valids.append(valid)
        if step < NZ // 2:
            below, above, valids[-1] = lax.optimization_barrier((below, above, valids[-1]))
        at_hand = [below, above] if step < NZ // 2 else [below]
    kv, valid, *parts = absorbed(at_hand, state, last=True)
    kvs.append(kv)
    valids.append(valid)

    received = [lax.ppermute(parts[s], "y", shift(NY, -s)) for s in range(1, NY)]

    cot = cotangent.reshape(pat_dev * lat_dev, width)
    cot_late, cot_early, _ = lax.optimization_barrier((cot[lat_dev:], cot[: 3 * lat_dev], parts[0]))
    cot_left = lax.ppermute(cot_late, "tm", up1)
    cot_right = lax.ppermute(cot_early, "tm", down1)

    att, copies, stats = combine([parts[0]] + received)

    everyone = lax.all_to_all(copies, "tm", 0, 0)
    features, msg, *first = conv_stack(
        tm.reshape(1), att, everyone.reshape(-1, width), stats,
        (cot_left, cot, cot_right), w_out, conv_weight, conv_bias, kvs,
    )

    msg = msg.reshape(pat_dev, lat_dev, width + 128)
    msgs = [msg] + [lax.ppermute(msg, "y", shift(NY, s)) for s in range(1, NY)]
    dq = backward_attention(y.reshape(1), kvs, first, valids, queries, msgs)

    pieces = lax.all_to_all(dq, ("y", "tm"), 0, 0, tiled=True)
    dq_row = jnp.sum(pieces, axis=0, keepdims=True).astype(bf16)
    spread = jnp.broadcast_to(dq_row.reshape(1, width // 128, 128), (lat_rows, width // 128, 128))
    dq_all = lax.all_to_all(spread, ("y", "z", "tm"), 0, 0, tiled=True)
    d_latents = nt_dot(dq_all.reshape(lat_rows, width), w_query)
    return features.reshape(pat_dev, lat_dev, width), d_latents


def solution(mesh):
    split = Mesh(mesh.devices.reshape(NY, NZ, NTM), ("y", "z", "tm"))
    contacts = ("y", "z")
    in_specs = (P(contacts, "tm"), P(contacts), P(contacts)) + (P(),) * 8 + (P("tm", contacts, None),)
    out_specs = (P("tm", contacts, None), P())
    return jax.shard_map(local, mesh=split, in_specs=in_specs, out_specs=out_specs, check_vma=False)
```

```python
import functools

import jax
import jax.numpy as jnp
from jax import lax
from jax.experimental import pallas as pl
from jax.experimental.pallas import tpu as pltpu
from jax.sharding import Mesh
from jax.sharding import PartitionSpec as P

HD = 64
PATCH = 32
KSIZE = 3
LAYERS = 2

neg_big = -1e30
scale_dot = 0.125

bf16 = jnp.bfloat16
f32 = jnp.float32

NY, NZ, NTM = 4, 8, 8
MIB = 1 << 20
PIECE, PARTS, HALVES, VMEM_ABSORB = 4096, 2, 2, 28
WUNROLL, VMEM_BACK = 4, 40


def nt_dot(a, b):
    return lax.dot_general(a, b, (((1,), (1,)), ((), ())), preferred_element_type=f32)


def nn_dot(a, b):
    return jnp.dot(a, b, preferred_element_type=f32)


def head_of_lane(shape):
    return lax.broadcasted_iota(jnp.int32, shape, len(shape) - 1) // HD


def spread_heads(rows, heads):
    head = head_of_lane(rows.shape)
    zero = jnp.zeros_like(rows)
    return jnp.concatenate([jnp.where(head == h, rows, zero) for h in range(heads)], axis=0)


def collect_heads(blocks, heads):
    r = blocks.shape[0] // heads
    head = head_of_lane((r, blocks.shape[1]))
    out = blocks[:r]
    for h in range(1, heads):
        out = jnp.where(head == h, blocks[h * r : (h + 1) * r], out)
    return out


def columns_to_lanes(column, heads, first, base):
    r = base.shape[0]
    lane = lax.broadcasted_iota(jnp.int32, base.shape, 1)
    for h in range(heads):
        base = jnp.where(lane == first + h, column[h * r : (h + 1) * r], base)
    return base


def lanes_to_column(stats, heads, first):
    return jnp.concatenate([stats[:, first + h : first + h + 1] for h in range(heads)], axis=0)


def lanes_to_columns_wide(stats, heads, first):
    r = stats.shape[0]
    head = head_of_lane((r, heads * HD))
    out = jnp.broadcast_to(stats[:, first : first + 1], (r, heads * HD))
    for h in range(1, heads):
        out = jnp.where(head == h, stats[:, first + h : first + h + 1], out)
    return out


def silu_slope(pre_act):
    sigmoid_v = jax.nn.sigmoid(pre_act)
    return sigmoid_v * (1.0 + pre_act * (1.0 - sigmoid_v))


def rounded(value):
    return value.astype(bf16).astype(f32)


def message_kernel(live_ref, signal_hbm, index_hbm, message_ref, signal_ref, index_ref, sem):
    con_dev, span = signal_hbm.shape
    copies = [
        pltpu.make_async_copy(index_hbm, index_ref, sem.at[0]),
        pltpu.make_async_copy(signal_hbm, signal_ref, sem.at[1]),
    ]
    for copy in copies:
        copy.start()
    copies[0].wait()
    index = index_ref[...].astype(f32)
    for r in range(con_dev // 128):
        column = jnp.transpose(jnp.broadcast_to(index[r : r + 1], (128, 128)))
        high = jnp.floor(column * (1.0 / 64.0))
        lane = lax.broadcasted_iota(jnp.int32, column.shape, 1)
        meta = jnp.where(lane == 0, high, jnp.where(lane == 1, column - 64.0 * high, live_ref[0].astype(f32)))
        message_ref[r * 128 : (r + 1) * 128, span:] = meta.astype(bf16)
    copies[1].wait()
    message_ref[:, :span] = signal_ref[...]


def make_message(live_count, signal, pos_idx):
    con_dev, span = signal.shape
    index = pos_idx.reshape(con_dev // 128, 128)
    signal, index = (pltpu.with_memory_space_constraint(a, pltpu.HBM) for a in (signal, index))
    hbm = pl.BlockSpec(memory_space=pltpu.HBM)
    return pl.pallas_call(
        message_kernel,
        in_specs=[pl.BlockSpec(memory_space=pltpu.SMEM), hbm, hbm],
        out_specs=pl.BlockSpec(memory_space=pltpu.VMEM),
        out_shape=jax.ShapeDtypeStruct((con_dev, span + 128), bf16),
        scratch_shapes=[
            pltpu.VMEM(signal.shape, signal.dtype),
            pltpu.VMEM(index.shape, index.dtype),
            pltpu.SemaphoreType.DMA((2,)),
        ],
        compiler_params=pltpu.CompilerParams(vmem_limit_bytes=8 * MIB),
        name="make_message",
    )(live_count, signal, index)


def prepare_kernel(y_ref, z_ref, *refs):
    hbms, (q_ref, *here), sem = refs[:5], refs[5:11], refs[11]
    latents_ref, w_query_ref = here[3], here[4]
    copies = [pltpu.make_async_copy(a, b, sem.at[i]) for i, (a, b) in enumerate(zip(hbms, here))]
    for i in (3, 4, 0, 1, 2):
        copies[i].start()
    lat, each = latents_ref.shape[0], latents_ref.shape[0] // (NY * NZ)
    row = lax.broadcasted_iota(jnp.int32, (q_ref.shape[0], lat), 0)
    owner = (y_ref[0] + NY - row // each) % NY
    place = (owner * NZ + z_ref[0]) * each + row % each
    pick = jnp.where(lax.broadcasted_iota(jnp.int32, row.shape, 1) == place, 1.0, 0.0).astype(bf16)
    copies[3].wait()
    chosen = nn_dot(pick, latents_ref[...]).astype(bf16)
    copies[4].wait()
    q_ref[...] = nn_dot(chosen, w_query_ref[...]).astype(bf16)
    for copy in copies[:3]:
        copy.wait()


def prepare(y, z, table, w_kv, w_in, latents, w_query):
    smem, vmem = pl.BlockSpec(memory_space=pltpu.SMEM), pl.BlockSpec(memory_space=pltpu.VMEM)
    arrays = [pltpu.with_memory_space_constraint(a, pltpu.HBM) for a in (table, w_kv, w_in, latents, w_query)]
    return pl.pallas_call(
        prepare_kernel,
        in_specs=[smem] * 2 + [pl.BlockSpec(memory_space=pltpu.HBM)] * 5,
        out_specs=[vmem] * 4,
        out_shape=[jax.ShapeDtypeStruct((latents.shape[0] // NZ, w_query.shape[1]), bf16)]
        + [pltpu.VMEM(a.shape, a.dtype) for a in (table, w_kv, w_in)],
        scratch_shapes=[pltpu.VMEM(a.shape, a.dtype) for a in (latents, w_query)]
        + [pltpu.SemaphoreType.DMA((5,))],
        compiler_params=pltpu.CompilerParams(vmem_limit_bytes=8 * MIB),
        name="prepare",
    )(y, z, *arrays)


def absorb_kernel(*refs, fresh, last, count):
    refs = list(refs)
    messages = [refs.pop(0) for _ in range(count)]
    q_ref, w_in_ref, w_kv_ref, table_ref = (refs.pop(0) for _ in range(4))
    if not fresh:
        acc_in, stat_in = refs.pop(0), refs.pop(0)
    kv_hbm, valid_ref = refs.pop(0), refs.pop(0)
    if last:
        part_refs = [refs.pop(0) for _ in range(NY)]
    else:
        acc_out, stat_out = refs.pop(0), refs.pop(0)
    pos_ref, tok_ref, kv_ref, sem = refs
    width = q_ref.shape[1]
    heads = width // HD
    con_dev, span = messages[0].shape[0], messages[0].shape[1] - 128
    windows = span // PATCH
    rows = count * con_dev
    message = jnp.concatenate([m[...] for m in messages], axis=0)
    sig = message[:, :span]
    meta = message[:, span:].astype(f32)
    idx = meta[:, 0:1] * 64.0 + meta[:, 1:2]
    lane = lax.broadcasted_iota(jnp.int32, (1, con_dev), 1).astype(f32)
    valid = jnp.concatenate(
        [jnp.where(lane < meta[c * con_dev : c * con_dev + 1, 2:3], 1.0, 0.0) for c in range(count)], axis=1
    )
    valid_ref[...] = jnp.broadcast_to(valid, valid_ref.shape)
    piece = PIECE
    ids = lax.broadcasted_iota(jnp.int32, (rows, piece), 1).astype(f32)
    hot = jnp.where(ids == idx, 1.0, 0.0).astype(bf16)
    pos_ref[...] = nn_dot(hot, table_ref[...])
    tall = jnp.concatenate([w_in_ref[...]] * windows, axis=0)
    band = lax.broadcasted_iota(jnp.int32, sig.shape, 1) // PATCH
    for w in range(windows):
        embedded = nn_dot(jnp.where(band == w, sig, jnp.zeros_like(sig)), tall)
        tok_ref[w * rows : (w + 1) * rows, :] = (embedded + pos_ref[...]).astype(bf16)
    ws = windows // PARTS

    def send(part):
        here = pl.ds(part * ws, ws)
        return pltpu.make_async_copy(kv_ref.at[here], kv_hbm.at[here], sem.at[part])

    def project(part):
        tokens = tok_ref[pl.ds(pl.multiple_of(part * ws * rows, ws * rows), ws * rows), :]
        for half in range(HALVES):
            cols = slice(half * 2 * width // HALVES, (half + 1) * 2 * width // HALVES)
            keyval = nn_dot(tokens, w_kv_ref[:, cols]).astype(bf16)
            kv_ref[pl.ds(part * ws, ws), :, cols] = keyval.reshape(ws, rows, 2 * width // HALVES)
        send(part).start()

    if count == 1:
        for part in range(PARTS):
            project(part)
    else:
        pl.loop(0, PARTS)(project)
    q_wide = spread_heads(q_ref[...], heads)

    def one_window(w):
        scores = nt_dot(q_wide, kv_ref[w, :, :width]) * scale_dot
        scores = jnp.where(valid > 0.0, scores, neg_big)
        top = jnp.max(scores, axis=1, keepdims=True)
        if not fresh:
            before, total_before = stat_in[w, :, 0:1], stat_in[w, :, 1:2]
            top = jnp.maximum(top, before)
        weights = jnp.exp(scores - top)
        totals = jnp.sum(weights, axis=1, keepdims=True)
        accum = nn_dot(weights.astype(bf16), kv_ref[w, :, width:])
        if not fresh:
            fade = jnp.exp(before - top)
            totals = totals + total_before * fade
            accum = accum + acc_in[w] * fade
        if not last:
            acc_out[w] = accum
            stat_out[w, :, 0:1] = top
            stat_out[w, :, 1:2] = totals
        else:
            mixed = collect_heads(accum, heads)
            stats = jnp.zeros((mixed.shape[0], 128), f32)
            stats = columns_to_lanes(top, heads, 0, stats)
            stats = columns_to_lanes(totals, heads, heads, stats)
            each = mixed.shape[0] // NY
            for s, part_ref in enumerate(part_refs):
                part_ref[w, :, :width] = mixed[s * each : (s + 1) * each]
                part_ref[w, :, width:] = stats[s * each : (s + 1) * each]

    together = WUNROLL // count

    @pl.loop(0, windows // together)
    def _(k):
        for part in range(together):
            one_window(k * together + part)

    for part in range(PARTS):
        send(part).wait()


def absorb(messages, q, w_in, w_kv, table, state, last):
    count = len(messages)
    lat, width = q.shape
    con_dev = messages[0].shape[0]
    windows = (messages[0].shape[1] - 128) // PATCH
    rows = lat * (width // HD)
    fresh = state is None
    vmem = pl.BlockSpec(memory_space=pltpu.VMEM)
    operands = list(messages) + [q, w_in, w_kv, table]
    in_specs = [vmem] * len(operands)
    aliases = {}
    if not fresh:
        n = len(operands)
        operands += list(state)
        in_specs += [vmem, vmem]
        aliases = {} if last else {n: 2, n + 1: 3}
    acc = jax.ShapeDtypeStruct((windows, rows, width), f32)
    stat = jax.ShapeDtypeStruct((windows, rows, 128), f32)
    part = jax.ShapeDtypeStruct((windows, lat // NY, width + 128), f32)
    tail = [part] * NY if last else [acc, stat]
    return pl.pallas_call(
        functools.partial(absorb_kernel, fresh=fresh, last=last, count=count),
        in_specs=in_specs,
        out_specs=[pl.BlockSpec(memory_space=pltpu.HBM)] + [vmem] * (1 + len(tail)),
        out_shape=[
            pltpu.HBM((windows, count * con_dev, 2 * width), bf16),
            jax.ShapeDtypeStruct((8, count * con_dev), f32),
        ]
        + tail,
        scratch_shapes=[
            pltpu.VMEM((count * con_dev, width), f32),
            pltpu.VMEM((windows * count * con_dev, width), bf16),
            pltpu.VMEM((windows, count * con_dev, 2 * width), bf16),
            pltpu.SemaphoreType.DMA((PARTS,)),
        ],
        input_output_aliases=aliases,
        compiler_params=pltpu.CompilerParams(vmem_limit_bytes=VMEM_ABSORB * MIB),
        name="absorb",
    )(*operands)


def combine_kernel(*refs):
    *part_refs, att_ref, copies_ref, stats_ref = refs
    rows, width = att_ref.shape
    heads = width // HD
    lane = lax.broadcasted_iota(jnp.int32, (rows, 128), 1)
    parts = [ref[...].reshape(rows, width + 128) for ref in part_refs]
    top = parts[0][:, width:]
    for part in parts[1:]:
        top = jnp.maximum(top, part[:, width:])
    totals = jnp.zeros((rows, 128), f32)
    accum = jnp.zeros((rows, width), f32)
    for part in parts:
        factor = jnp.exp(jnp.where(lane < heads, part[:, width:] - top, 0.0))
        totals = totals + factor * pltpu.roll(part[:, width:], 128 - heads, 1)
        accum = accum + part[:, :width] * lanes_to_columns_wide(factor, heads, 0)
    totals = jnp.where(lane < heads, totals, 1.0)
    att = (accum / lanes_to_columns_wide(totals, heads, 0)).astype(bf16)
    att_ref[...] = att
    for t in range(NTM):
        copies_ref[t] = att
    stats_ref[...] = jnp.where(lane < heads, top, pltpu.roll(1.0 / totals, heads, 1))


def combine(parts):
    windows, each, wide = parts[0].shape
    rows = windows * each
    return pl.pallas_call(
        combine_kernel,
        out_shape=[
            jax.ShapeDtypeStruct((rows, wide - 128), bf16),
            jax.ShapeDtypeStruct((NTM, rows, wide - 128), bf16),
            jax.ShapeDtypeStruct((rows, 128), f32),
        ],
        compiler_params=pltpu.CompilerParams(vmem_limit_bytes=8 * MIB),
        name="combine_parts",
    )(*parts)


def conv_kernel(
    tm_ref, own_ref, all_ref, stats_ref, cl_ref, cot_ref, cr_ref,
    w_out_ref, bias_ref, conv_hbm, *refs,
):
    n = (len(refs) - 6) // 2
    kv_hbms, (feat_ref, msg_ref), kv_refs = refs[:n], refs[n : n + 2], refs[n + 2 : 2 * n + 2]
    ext_ref, conv_ref, sem, kv_sem = refs[2 * n + 2 :]
    fetches = [pltpu.make_async_copy(kv_hbms[i].at[0], kv_refs[i], kv_sem.at[i]) for i in range(n)]
    weights = [pltpu.make_async_copy(conv_hbm.at[l], conv_ref.at[l], sem.at[l]) for l in range(LAYERS)]
    for copy in weights:
        copy.start()
    rows, width = own_ref.shape
    heads = width // HD
    windows = 4
    each = rows // windows
    reach = 6
    first = tm_ref[0] * windows - reach
    total_windows = NTM * windows

    def inside(lo, count):
        w = lax.broadcasted_iota(jnp.int32, (count * each, width), 0) // each + (first + lo)
        return jnp.logical_and(w >= 0, w < total_windows)

    side = reach * each
    ext_ref[:side, :] = jnp.zeros((side, width), f32)
    ext_ref[side : side + NTM * rows, :] = all_ref[...].astype(f32)
    ext_ref[side + NTM * rows :, :] = jnp.zeros((side, width), f32)
    att = ext_ref[pl.ds(pl.multiple_of(tm_ref[0] * rows, rows), 2 * side + rows), :]
    w_out = w_out_ref[...]
    x0 = rounded(nn_dot(att.astype(bf16), w_out))
    n0 = 14 * each
    weights[0].wait()
    pre0 = bias_ref[0:1, :] + sum(nn_dot(x0[j * each : j * each + n0].astype(bf16), conv_ref[0, j]) for j in range(KSIZE))
    x1 = rounded(x0[each : each + n0] + jax.nn.silu(pre0))
    x1 = jnp.where(inside(1, 14), x1, 0.0)
    n1 = 10 * each
    weights[1].wait()
    for copy in fetches:
        copy.start()
    pre1 = bias_ref[1:2, :] + sum(nn_dot(x1[2 * j * each : 2 * j * each + n1].astype(bf16), conv_ref[1, j]) for j in range(KSIZE))
    feat_ref[...] = (x1[5 * each : 9 * each] + jax.nn.silu(pre1[3 * each : 7 * each])).astype(bf16)
    g2 = jnp.concatenate([r[...].astype(f32) for r in (cl_ref, cot_ref, cr_ref)], axis=0)
    gpre1 = rounded(g2 * silu_slope(pre1))
    n2 = 6 * each
    g1 = g2[2 * each : 8 * each] + sum(
        nt_dot(gpre1[(4 - 2 * j) * each : (4 - 2 * j) * each + n2].astype(bf16), conv_ref[1, j]) for j in range(KSIZE)
    )
    gpre0 = rounded(g1 * silu_slope(pre0[4 * each : 10 * each]))
    gpre0 = jnp.where(inside(5, 6), gpre0, 0.0)
    g0 = g1[each : 5 * each] + sum(
        nt_dot(gpre0[(2 - j) * each : (2 - j) * each + rows].astype(bf16), conv_ref[0, j]) for j in range(KSIZE)
    )
    grad_att = rounded(nt_dot(g0.astype(bf16), w_out))
    msg_ref[:, :width] = grad_att.astype(bf16)
    product = grad_att * own_ref[...].astype(f32)
    head = head_of_lane((rows, width))
    lane = lax.broadcasted_iota(jnp.int32, (rows, 128), 1)
    stats = stats_ref[...]
    for h in range(heads):
        delta = jnp.sum(jnp.where(head == h, product, 0.0), axis=1, keepdims=True)
        stats = jnp.where(lane == 2 * heads + h, delta, stats)
    stats = jnp.where(lane < 3 * heads, stats, 0.0)
    high = rounded(stats)
    middle = rounded(stats - high)
    low = (stats - high) - middle
    for copy in fetches:
        copy.wait()
    msg_ref[:, width:] = (high + pltpu.roll(middle, 32, 1) + pltpu.roll(low, 64, 1)).astype(bf16)


def conv_stack(tm, own, everyone, stats, cots, w_out, conv_weight, conv_bias, kvs):
    rows, width = own.shape
    cl, cot, cr = cots
    vmem = pl.BlockSpec(memory_space=pltpu.VMEM)
    return pl.pallas_call(
        conv_kernel,
        in_specs=[pl.BlockSpec(memory_space=pltpu.SMEM)]
        + [vmem] * 8
        + [pl.BlockSpec(memory_space=pltpu.HBM)] * (1 + len(kvs)),
        out_specs=[vmem] * (2 + len(kvs)),
        out_shape=[
            jax.ShapeDtypeStruct((rows, width), bf16),
            jax.ShapeDtypeStruct((rows, width + 128), bf16),
        ]
        + [pltpu.VMEM(kv.shape[1:], kv.dtype) for kv in kvs],
        scratch_shapes=[
            pltpu.VMEM(((NTM + 3) * rows, width), f32),
            pltpu.VMEM(conv_weight.shape, conv_weight.dtype),
            pltpu.SemaphoreType.DMA((LAYERS,)),
            pltpu.SemaphoreType.DMA((len(kvs),)),
        ],
        compiler_params=pltpu.CompilerParams(vmem_limit_bytes=20 * MIB),
        name="conv_stack",
    )(tm, own, everyone, stats, cl, cot, cr, w_out, conv_bias, *(pltpu.with_memory_space_constraint(a, pltpu.HBM) for a in (conv_weight, *kvs)))


def backward_kernel(y_ref, q_ref, *refs, slots):
    msg_refs, refs = refs[:slots], refs[slots:]
    n = (len(refs) - 3) // 4
    first_refs, valid_refs, kv_hbms = refs[:n], refs[n : 2 * n], refs[2 * n : 3 * n]
    dq_ref, acc_ref, *kv_refs, sem = refs[3 * n :]
    width = q_ref.shape[1]
    heads = width // HD
    windows = msg_refs[0].shape[0]

    def fetch(window, i):
        return pltpu.make_async_copy(kv_hbms[i].at[window], kv_refs[i].at[window - 1], sem.at[window - 1, i])

    for window in range(1, windows):
        for i in range(n):
            fetch(window, i).start()

    def one_window(window, blocks):
        msg = jnp.concatenate([r[window].astype(f32) for r in msg_refs], axis=0)
        terms = msg[:, width:]
        stats = terms + pltpu.roll(terms, 96, 1) + pltpu.roll(terms, 64, 1)
        top = lanes_to_column(stats, heads, 0)
        inverse = lanes_to_column(stats, heads, heads)
        delta = lanes_to_column(stats, heads, 2 * heads)
        grad_wide = spread_heads(msg[:, :width].astype(bf16), heads)
        q_wide = spread_heads(q_ref[...], heads)
        accum = 0.0
        for block, valid_ref in zip(blocks, valid_refs):
            key_rows = block[:, :width]
            scores = nt_dot(q_wide, key_rows) * scale_dot
            scores = jnp.where(valid_ref[0:1, :] > 0.0, scores, neg_big)
            prob = jnp.exp(scores - top) * inverse
            grad_prob = nt_dot(grad_wide, block[:, width:])
            dscore = (prob * (grad_prob - delta)).astype(bf16)
            accum = accum + nn_dot(dscore, key_rows)
        return accum

    acc_ref[...] = one_window(0, first_refs)

    @pl.loop(1, windows)
    def _(window):
        for i in range(n):
            fetch(window, i).wait()
        acc_ref[...] = acc_ref[...] + one_window(window, [ref.at[window - 1] for ref in kv_refs])

    dq = collect_heads(acc_ref[...], heads) * scale_dot
    each = dq.shape[0] // slots
    for s in range(slots):
        place = pl.multiple_of(((y_ref[0] + (slots - s)) % slots) * each, each)
        dq_ref[pl.ds(place, each), :] = dq[s * each : (s + 1) * each]


def backward_attention(y, kvs, first, valids, q, msgs):
    lat, width = q.shape
    heads = width // HD
    vmem = pl.BlockSpec(memory_space=pltpu.VMEM)
    kvs = [pltpu.with_memory_space_constraint(kv, pltpu.HBM) for kv in kvs]
    return pl.pallas_call(
        functools.partial(backward_kernel, slots=len(msgs)),
        in_specs=[pl.BlockSpec(memory_space=pltpu.SMEM)]
        + [vmem] * (1 + len(msgs) + len(first) + len(valids))
        + [pl.BlockSpec(memory_space=pltpu.HBM)] * len(kvs),
        out_specs=vmem,
        out_shape=jax.ShapeDtypeStruct((lat, width), f32),
        scratch_shapes=[pltpu.VMEM((lat * heads, width), f32)]
        + [pltpu.VMEM((kv.shape[0] - 1,) + kv.shape[1:], kv.dtype) for kv in kvs]
        + [pltpu.SemaphoreType.DMA((kvs[0].shape[0] - 1, len(kvs)))],
        compiler_params=pltpu.CompilerParams(vmem_limit_bytes=VMEM_BACK * MIB),
        name="backward_attention",
    )(y, q, *msgs, *first, *valids, *kvs)


def shift(count, by):
    return [(i, (i + by) % count) for i in range(count)]


def local(
    signal, pos_idx, live_count, latents, pos_table, w_in, w_kv, w_query, w_out,
    conv_weight, conv_bias, cotangent,
):
    con_dev = signal.shape[0]
    pat_dev = signal.shape[1] // PATCH
    width = w_query.shape[0]
    lat_rows = latents.shape[0]
    y, z, tm = (lax.axis_index(a) for a in ("y", "z", "tm"))
    lat_dev = lat_rows // (NY * NZ)
    up1 = [(i, i + 1) for i in range(NTM - 1)]
    down1 = [(i + 1, i) for i in range(NTM - 1)]

    own = make_message(live_count, signal, pos_idx)
    queries, table, kv_weights, in_weights = prepare(
        y.reshape(1), z.reshape(1), pos_table, w_kv, w_in, latents, w_query
    )

    def absorbed(messages, state, last=False):
        return absorb(messages, queries, in_weights, kv_weights, table, state, last)

    below, above = own, own
    at_hand, state, kvs, valids = [own], None, [], []
    for step in range(1, NZ // 2 + 1):
        below = lax.ppermute(below, "z", shift(NZ, 1))
        if step < NZ // 2:
            above = lax.ppermute(above, "z", shift(NZ, -1))
        kv, valid, *state = absorbed(at_hand, state)
        kvs.append(kv)
        valids.append(valid)
        if step < NZ // 2:
            below, above, valids[-1] = lax.optimization_barrier((below, above, valids[-1]))
        at_hand = [below, above] if step < NZ // 2 else [below]
    kv, valid, *parts = absorbed(at_hand, state, last=True)
    kvs.append(kv)
    valids.append(valid)

    received = [lax.ppermute(parts[s], "y", shift(NY, -s)) for s in range(1, NY)]

    cot = cotangent.reshape(pat_dev * lat_dev, width)
    cot_late, cot_early, _ = lax.optimization_barrier((cot[lat_dev:], cot[: 3 * lat_dev], parts[0]))
    cot_left = lax.ppermute(cot_late, "tm", up1)
    cot_right = lax.ppermute(cot_early, "tm", down1)

    att, copies, stats = combine([parts[0]] + received)

    everyone = lax.all_to_all(copies, "tm", 0, 0)
    features, msg, *first = conv_stack(
        tm.reshape(1), att, everyone.reshape(-1, width), stats,
        (cot_left, cot, cot_right), w_out, conv_weight, conv_bias, kvs,
    )

    msg = msg.reshape(pat_dev, lat_dev, width + 128)
    msgs = [msg] + [lax.ppermute(msg, "y", shift(NY, s)) for s in range(1, NY)]
    dq = backward_attention(y.reshape(1), kvs, first, valids, queries, msgs)

    pieces = lax.all_to_all(dq, ("y", "tm"), 0, 0, tiled=True)
    dq_row = jnp.sum(pieces, axis=0, keepdims=True).astype(bf16)
    spread = jnp.broadcast_to(dq_row.reshape(1, width // 128, 128), (lat_rows, width // 128, 128))
    dq_all = lax.all_to_all(spread, ("y", "z", "tm"), 0, 0, tiled=True)
    d_latents = nt_dot(dq_all.reshape(lat_rows, width), w_query)
    return features.reshape(pat_dev, lat_dev, width), d_latents


def solution(mesh):
    split = Mesh(mesh.devices.reshape(NY, NZ, NTM), ("y", "z", "tm"))
    contacts = ("y", "z")
    in_specs = (P(contacts, "tm"), P(contacts), P(contacts)) + (P(),) * 8 + (P("tm", contacts, None),)
    out_specs = (P("tm", contacts, None), P())
    return jax.shard_map(local, mesh=split, in_specs=in_specs, out_specs=out_specs, check_vma=False)
```
